256 devices in a mesh: req: 8 (over z), row: 8 (over y, core), col: 4 (over x).
Axes of the slice: x: 4, y: 4, z: 8, core: 2. Of those that a mesh axis runs over, the one named last changes fastest.
Arguments:
- tokens: bfloat16 [16384, 2, 1792], P(('req', 'row'), None, 'col'), may hold values from -6 to 6
- w_query: bfloat16 [1792, 256], P('col', 'row'), may hold values from -0.125 to 0.125
- w_key: bfloat16 [1792, 256], P('col', 'row'), may hold values from -0.125 to 0.125
- w_value: bfloat16 [16, 200704], P('row', 'col'), may hold values from -0.125 to 0.125
- w_out: bfloat16 [1792, 1792], P('row', 'col'), may hold values from -0.125 to 0.125
- cached_state: bfloat16 [32, 273, 57344], P(('req', 'col'), None, 'row'), may hold values from -24 to 24
- cached_norm: bfloat16 [1024, 273, 16], P(('req', 'col'), None, 'row'), as said below
- slot_prompt: int32 [1024], P(('req', 'col')), may hold values from 0 to 1023, as said below
- prompt_of: int32 [16384], P(('req', 'col')), may hold values from 0 to 1023, as said below
- tail_keys: bfloat16 [16384, 2048], P(('req', 'col'), 'row'), may hold values from -6 to 6
- tail_values: bfloat16 [16384, 14336], P(('req', 'col'), 'row'), may hold values from -6 to 6
- tail_length: int32 [16384], P(('req', 'col')), may hold values from 0 to 8, as said below
Outputs:
- layer_out: bfloat16 [16384, 2, 1792], P(('req', 'row'), None, 'col')
The draws below stay inside these ranges and needn't reach their ends.
Inputs may be any that keep to these rules, and one draw needn't show every extreme that they name: `slot_prompt`: each prompt sits in exactly one slot. The h-th block of 32 slots (holder h) keeps exactly 16 of its own prompts h * 32 to (h + 1) * 32 - 1; its other slots hold prompts of other holders, at most 1 of any one holder. The bound 1 is reached: some holder keeps 1 of one other holder's prompts. `prompt_of`: the h-th aligned block of 512 continuations holds exactly 16 continuations of each prompt h * 32 to (h + 1) * 32 - 1. `tail_length`: each aligned block of 512 continuations holds at least one continuation with a tail of 8 tokens. `cached_norm`: each prompt's column for a head is a sum of phi of some key vectors with positive weights.
All inputs are finite; a program needn't handle non-finite values.
Results may differ from the reference program's by a relative error of at most 0.019.
Values may be sent and summed in bfloat16 or wider, within the bound.
No kernel may reach another device: no remote copies, remote signals or barrier semaphores. Data moves between devices by JAX's collectives and lax.ppermute only.
A program may use at most 128 MiB of HBM per device.

```python
import jax
import jax.numpy as jnp
from jax import lax

D = 1792
HEADS = 16
FEAT = 16
HEAD_DIM = 112
QK = 256
TAYLOR = 273
CONTS_PER = 16
P_DEV = 32
TAIL = 8
HOLDERS = 32
PROMPTS = 1024
CONT = 16384
N_ROW = 8
N_COL = 4


def holder_table(key):
    half_count = P_DEV // 2
    group_keys = jax.random.split(jax.random.fold_in(key, 11), HOLDERS)
    orders = jax.vmap(lambda subkey: jax.random.permutation(subkey, P_DEV))(group_keys)
    steps_along = jnp.arange(half_count)
    offsets = 1 + (HOLDERS - 2 + steps_along * (HOLDERS // 2)) % (HOLDERS - 1)
    holders = jnp.arange(HOLDERS)
    sources = (holders[:, None] - offsets[None, :]) % HOLDERS
    incoming = sources * P_DEV + orders[sources, half_count + jnp.arange(half_count)[None, :]]
    staying = holders[:, None] * P_DEV + orders[:, :half_count]
    contents = jnp.concatenate([staying, incoming], axis=1)
    shuffle_keys = jax.random.split(jax.random.fold_in(key, 13), HOLDERS)
    shuffles = jax.vmap(lambda subkey: jax.random.permutation(subkey, P_DEV))(shuffle_keys)
    return jnp.take_along_axis(contents, shuffles, axis=1).reshape(-1).astype(jnp.int32)


def draw_slot_prompt(key, part):
    return holder_table(key)


def draw_prompt_of(key, part):
    block_rows = CONTS_PER * P_DEV
    block_keys = jax.random.split(jax.random.fold_in(key, 21), HOLDERS)
    orders = jax.vmap(lambda subkey: jax.random.permutation(subkey, block_rows))(block_keys)
    return (jnp.arange(HOLDERS)[:, None] * P_DEV + orders // CONTS_PER).reshape(-1).astype(jnp.int32)


def draw_tail_length(key, part):
    block_rows = CONTS_PER * P_DEV
    drawn = jax.random.randint(jax.random.fold_in(key, 31), (HOLDERS, block_rows), 0, TAIL + 1)
    longest_at = jax.random.randint(jax.random.fold_in(key, 32), (HOLDERS, 1), 0, block_rows)
    drawn = jnp.where(jnp.arange(block_rows)[None, :] == longest_at, TAIL, drawn)
    return drawn.reshape(-1).astype(jnp.int32)


def draw_cached_norm(key, part):
    pseudo_count = 8
    pseudo_keys = jax.random.normal(jax.random.fold_in(key, 41), (PROMPTS, HEADS, pseudo_count, FEAT), jnp.float32)
    weights = jax.random.uniform(jax.random.fold_in(key, 42), (PROMPTS, HEADS, pseudo_count), jnp.float32, 0.5, 1.5)
    linear = pseudo_keys * FEAT ** (-0.25)
    square = (pseudo_keys[..., :, None] * pseudo_keys[..., None, :]).reshape(PROMPTS, HEADS, pseudo_count, FEAT * FEAT)
    square = square * (0.5 ** 0.5 / FEAT ** 0.5)
    unit_column = jnp.ones((PROMPTS, HEADS, pseudo_count, 1), jnp.float32)
    taylor_terms = jnp.concatenate([unit_column, linear, square], axis=-1)
    weighted = jnp.sum(weights[..., None] * taylor_terms, axis=2)
    return jnp.transpose(weighted, (0, 2, 1)).astype(jnp.bfloat16)


def steps_of(own_key, shape, shards, least, top_value):
    def one(axis_at, parts):
        steps = jax.random.uniform(jax.random.fold_in(jax.random.fold_in(own_key, 6), axis_at), (parts,), jnp.float32, least / len(shards), top_value / len(shards))
        return jnp.repeat(jnp.exp(steps), shape[axis_at] // parts).reshape((-1,) + (1,) * (len(shape) - axis_at - 1))

    level = one(*shards[0])
    for cut in shards[1:]:
        level = level * one(*cut)
    return level


def normal_values(key, shape, deviation, bound, pieces=(), kind=jnp.bfloat16):
    level = steps_of(key, shape, pieces, -0.22, 0.18) if pieces else 1.0
    values = jax.random.normal(key, shape, jnp.float32) * deviation * level
    return jnp.minimum(jnp.maximum(values, -bound), bound).astype(kind)


def setup_inputs(seed: int = 0) -> dict:
    key_list = jax.random.split(jax.random.key(seed), 13)
    return {
        "tokens": normal_values(key_list[0], (CONT, 2, D), 1.0, 6.0, ((0, 64), (2, 4))),
        "w_query": normal_values(key_list[1], (D, QK), D ** -0.5, 0.125, ((0, 4), (1, 8))),
        "w_key": normal_values(key_list[2], (D, QK), D ** -0.5, 0.125, ((0, 4), (1, 8))),
        "w_value": normal_values(key_list[3], (HEADS, D * HEAD_DIM), D ** -0.5, 0.125, ((0, 8), (1, 4))),
        "w_out": normal_values(key_list[4], (D, D), D ** -0.5, 0.125, ((0, 8), (1, 4))),
        "cached_state": normal_values(key_list[5], (HOLDERS, TAYLOR, D * P_DEV), 4.0, 24.0, ((0, 32), (2, 8))),
        "cached_norm": draw_cached_norm(jax.random.fold_in(key_list[12], 71), 0),
        "slot_prompt": draw_slot_prompt(jax.random.fold_in(key_list[12], 71), 0),
        "prompt_of": draw_prompt_of(jax.random.fold_in(key_list[12], 71), 0),
        "tail_keys": normal_values(key_list[9], (CONT, HEADS * TAIL * FEAT), 1.0, 6.0, ((0, 32), (1, 8))),
        "tail_values": normal_values(key_list[10], (CONT, D * TAIL), 1.0, 6.0, ((0, 32), (1, 8))),
        "tail_length": draw_tail_length(jax.random.fold_in(key_list[12], 71), 0),
    }


def features(values):
    feature_width = values.shape[-1]
    linear = values * feature_width ** -0.25
    square = (values[..., :, None] * values[..., None, :]).reshape(values.shape[:-1] + (feature_width * feature_width,))
    square = square * (0.5 ** 0.5 / feature_width ** 0.5)
    unit_column = jnp.ones(values.shape[:-1] + (1,), values.dtype)
    return jnp.concatenate([unit_column, linear, square], axis=-1)


def kernel_weight(scores):
    return 1.0 + scores + 0.5 * scores * scores


def rounded(values):
    return lax.optimization_barrier(values.astype(jnp.bfloat16)).astype(jnp.float32)


def reference(tokens, w_query, w_key, w_value, w_out, cached_state, cached_norm, slot_prompt, prompt_of, tail_keys, tail_values, tail_length):
    highest = lax.Precision.HIGHEST
    value_weight = jnp.transpose(w_value.reshape(HEADS, D, HEAD_DIM), (1, 0, 2)).reshape(D, D)
    stacked = jnp.concatenate([w_query, w_key, value_weight], axis=1).astype(jnp.float32)
    token_values = tokens.astype(jnp.float32)
    col_width = D // N_COL
    summed = jnp.zeros((CONT, 2, stacked.shape[1]), jnp.float32)
    for block_index in range(N_COL):
        lower = block_index * col_width
        product = jnp.einsum("ctd,de->cte", token_values[:, :, lower:lower + col_width], stacked[lower:lower + col_width], precision=highest)
        summed = summed + rounded(product)
    projected = rounded(summed)
    queries = projected[:, :, :QK].reshape(CONT, 2, HEADS, FEAT)
    key_new = projected[:, :, QK:2 * QK].reshape(CONT, 2, HEADS, FEAT)
    value_new = projected[:, :, 2 * QK:].reshape(CONT, 2, HEADS, HEAD_DIM)
    inverse = jnp.argsort(slot_prompt, stable=True).astype(jnp.int32)
    block_rows = CONTS_PER * P_DEV
    scale = FEAT ** -0.5
    causal = (jnp.arange(2)[:, None] >= jnp.arange(2)[None, :]).astype(jnp.float32)
    state_blocks = cached_state.reshape(HOLDERS, TAYLOR, D, P_DEV)

    def one_block(block_index):
        start = (block_index * block_rows).astype(jnp.int32)
        queries_here = lax.dynamic_slice_in_dim(queries, start, block_rows, 0)
        keys_here = lax.dynamic_slice_in_dim(key_new, start, block_rows, 0)
        values_here = lax.dynamic_slice_in_dim(value_new, start, block_rows, 0)
        tail_k = lax.dynamic_slice_in_dim(tail_keys, start, block_rows, 0).astype(jnp.float32).reshape(block_rows, HEADS, TAIL, FEAT)
        tail_v = lax.dynamic_slice_in_dim(tail_values, start, block_rows, 0).astype(jnp.float32).reshape(block_rows, HEADS, TAIL, HEAD_DIM)
        lengths = lax.dynamic_slice_in_dim(tail_length, start, block_rows, 0)
        owner_ids = lax.dynamic_slice_in_dim(prompt_of, start, block_rows, 0)
        slot_index = lax.dynamic_slice_in_dim(inverse, (block_index * P_DEV).astype(jnp.int32), P_DEV, 0)
        holder_of = (slot_index // P_DEV).astype(jnp.int32)
        within = (slot_index % P_DEV).astype(jnp.int32)
        states = state_blocks[holder_of, :, :, within].astype(jnp.float32).reshape(P_DEV, TAYLOR, HEADS, HEAD_DIM)
        norms = cached_norm[slot_index].astype(jnp.float32)
        ordering = jnp.argsort(owner_ids, stable=True)
        restore = jnp.argsort(ordering, stable=True)
        grouped = features(queries_here[ordering]).reshape(P_DEV, CONTS_PER, 2, HEADS, TAYLOR)
        numerator = jnp.einsum("pcthf,pfhv->pcthv", rounded(grouped), states, precision=highest)
        denominator = jnp.einsum("pcthf,pfh->pcth", grouped, norms, precision=highest)
        numerator = numerator.reshape(block_rows, 2, HEADS, HEAD_DIM)[restore]
        denominator = denominator.reshape(block_rows, 2, HEADS)[restore]
        tail_scores = jnp.einsum("cthf,chuf->cthu", queries_here, tail_k, precision=highest) * scale
        live_mask = (jnp.arange(TAIL)[None, :] < lengths[:, None]).astype(jnp.float32)
        tail_kernel = kernel_weight(tail_scores) * live_mask[:, None, None, :]
        new_scores = jnp.einsum("cthf,cjhf->cthj", queries_here, keys_here, precision=highest) * scale
        new_kernel = kernel_weight(new_scores) * causal[None, :, None, :]
        numerator = numerator + jnp.einsum("cthu,chuv->cthv", rounded(tail_kernel), tail_v, precision=highest)
        numerator = numerator + jnp.einsum("cthj,cjhv->cthv", rounded(new_kernel), values_here, precision=highest)
        denominator = denominator + jnp.sum(tail_kernel, axis=-1) + jnp.sum(new_kernel, axis=-1)
        return (numerator / denominator[..., None]).astype(jnp.bfloat16).reshape(block_rows, 2, D)

    heads_out = lax.map(one_block, jnp.arange(HOLDERS, dtype=jnp.int32)).reshape(CONT, 2, D).astype(jnp.float32)
    row_width = D // N_ROW
    result = token_values
    out_weights = w_out.astype(jnp.float32)
    for block_index in range(N_ROW):
        lower = block_index * row_width
        product = jnp.einsum("cte,ed->ctd", heads_out[:, :, lower:lower + row_width], out_weights[lower:lower + row_width], precision=highest)
        result = result + rounded(product)
    return result.astype(jnp.bfloat16)
```

```python
import functools

import jax
import jax.numpy as jnp
from jax import lax
from jax.experimental import pallas as pl
from jax.experimental.pallas import tpu as pltpu
from jax.sharding import Mesh, PartitionSpec as P

BF = jnp.bfloat16
F32 = jnp.float32
VMEM_LIMIT = 48 * 1024 * 1024
VM = pl.BlockSpec(memory_space=pltpu.VMEM)
SM = pl.BlockSpec(memory_space=pltpu.SMEM)


def dot(a, b):
    return jnp.dot(a, b, preferred_element_type=F32)


def iota(shape, dim):
    return lax.broadcasted_iota(jnp.int32, shape, dim)


def onehot(cond):
    return jnp.where(cond, 1.0, 0.0).astype(BF)


def split(x):
    high = x.astype(BF)
    return high, (x - high.astype(F32)).astype(BF)


def call(kernel, out_shapes, n_smem, n_vmem, **kw):
    return pl.pallas_call(
        kernel,
        out_shape=out_shapes,
        in_specs=[SM] * n_smem + [VM] * n_vmem,
        out_specs=jax.tree.map(lambda _: VM, out_shapes),
        compiler_params=pltpu.CompilerParams(vmem_limit_bytes=VMEM_LIMIT),
        **kw,
    )


def project_kernel(pos_ref, t0, t1, t2, t3, w_ref, out_ref):
    w = w_ref[...]
    for shift, block in enumerate((t0, t1, t2, t3)):
        slot = lax.rem(pos_ref[0] + 4 - shift, 4)
        out_ref[slot] = dot(block[...], w).astype(BF)


def sum_kernel(pos_ref, p_ref, own_ref, oth_ref):
    core = pos_ref[1]

    def total(lo, hi):
        acc = p_ref[0, :, lo:hi].astype(F32)
        for i in range(1, 4):
            acc = acc + p_ref[i, :, lo:hi].astype(F32)
        return acc.astype(BF)

    first, second, keys = total(0, 256), total(256, 512), total(512, 640)
    own_ref[:, 0:256] = jnp.where(core == 0, first, second)
    oth_ref[:, 0:256] = jnp.where(core == 0, second, first)
    own_ref[:, 256:384] = keys
    oth_ref[:, 256:384] = keys


def group_kernel(pos_ref, g_ref, s_ref, own_ref, rec_ref, place_ref, send_ref, keep_ref, grouped):
    core = pos_ref[1]
    me = pos_ref[2]
    rows, cols = iota((256, 128), 0), iota((256, 128), 1)
    acc = None
    for e, ref in enumerate((own_ref, rec_ref)):
        half = core if e == 0 else 1 - core
        queries = None
        for t in range(2):
            pick = onehot((rows >= 224) & (cols == rows - 224 + 32 * t))
            part = dot(ref[t * 256 : (t + 1) * 256, 0:256], pick)
            queries = part if queries is None else queries + part
        hot = onehot(iota((512, 256), 0) == place_ref[half])
        part = dot(hot, queries.astype(BF))
        acc = part if acc is None else acc + part
    grouped[...] = acc.astype(BF)
    send_ref[...] = jnp.zeros_like(send_ref)
    keep_ref[...] = jnp.zeros_like(keep_ref)
    for p in range(32):
        holder, slot = g_ref[p], s_ref[p]

        @pl.when(holder != me)
        def _():
            send_ref[holder] = grouped[p * 16 : (p + 1) * 16, :]

        @pl.when(holder == me)
        def _():
            keep_ref[slot] = grouped[p * 16 : (p + 1) * 16, :]


def slot_kernel(pos_ref, owner_ref, rec_ref, keep_ref, state_ref, send_ref, own_ref, buf):
    me = pos_ref[2]
    step = pl.program_id(0)

    @pl.when(step == 0)
    def _():
        send_ref[...] = jnp.zeros_like(send_ref)
        own_ref[...] = jnp.zeros_like(own_ref)

    for i in range(8):
        slot = step * 8 + i
        owner = owner_ref[slot]

        @pl.when(owner != me)
        def _():
            buf[i * 16 : (i + 1) * 16, :] = rec_ref[owner]

        @pl.when(owner == me)
        def _():
            buf[i * 16 : (i + 1) * 16, :] = keep_ref[slot]

    q = buf[...]
    row, f = iota((128, 384), 0), iota((128, 384), 1)
    lane = iota((1, 384), 1)
    square, line = lane >= 17, (lane >= 1) & (lane < 17)
    unit_a = jnp.where(lane == 0, 1.0, 0.0)
    unit_b = jnp.where(lane < 17, 1.0, 0.0)
    scale = jnp.where(square, 0.5**0.5 / 4.0, jnp.where(line, 0.5, 1.0))
    scale = jnp.where(lane < 273, scale, 0.0)
    a_at = jnp.where(f >= 17, lax.shift_right_logical(f - 17, 4), f - 1)
    b_at = (f - 17) & 15
    live_a = (f >= 1) & (f < 273)
    live_b = (f >= 17) & (f < 273)
    high, low = [], []
    for t in range(2):
        for h in range(2):
            base = t * 32 + h * 16
            left = dot(q, onehot(live_a & (row == a_at + base))) + unit_a
            right = dot(q, onehot(live_b & (row == b_at + base))) + unit_b
            one, two = split(left * right * scale)
            high.append(one)
            low.append(two)
    out_lane = iota((16, 256), 1)
    first_head = (out_lane < 112) | (out_lane == 224) | (out_lane == 226)
    for i in range(8):
        phi = jnp.concatenate([x[i * 16 : (i + 1) * 16, 0:273] for x in high + low], axis=0)
        both = dot(phi, state_ref[i])
        terms = both[0:64] + both[64:128]
        results = []
        for t in range(2):
            r = jnp.where(first_head, terms[t * 32 : t * 32 + 16], terms[t * 32 + 16 : t * 32 + 32])
            rough = r.astype(BF).astype(F32)
            results.append(jnp.where(out_lane >= 226, r - rough, r).astype(BF))
        slot = step * 8 + i
        owner = owner_ref[slot]

        @pl.when(owner != me)
        def _():
            send_ref[owner, :, 0:256] = results[0]
            send_ref[owner, :, 256:512] = results[1]

        @pl.when(owner == me)
        def _():
            own_ref[slot, :, 0:256] = results[0]
            own_ref[slot, :, 256:512] = results[1]


def kappa(s):
    return 1.0 + s + 0.5 * s * s


def tail_kernel(pos_ref, own_ref, rec_ref, tk_ref, tv_ref, len_ref, num_ref, den_ref):
    core = pos_ref[1]
    r, c = iota((256, 256), 0), iota((256, 256), 1)
    expand_q = onehot((r >= 224) & (r - 224 == lax.shift_right_logical(c, 7) * 16 + (c & 15)))
    r, c = iota((256, 128), 0), iota((256, 128), 1)
    sum_a = onehot(lax.shift_right_logical(r, 4) == c)
    pick_q = onehot((r >= 224) & (r - 224 == c))
    r, c = iota((128, 128), 0), iota((128, 128), 1)
    pick_k = onehot((c < 32) & (r == c + 32 * core))
    sum_new = onehot((r < 32) & (lax.shift_right_logical(r, 4) == c))
    r, c = iota((128, 1792), 0), iota((128, 1792), 1)
    expand_w = onehot((r < 16) & (c >= r * 112) & (c < (r + 1) * 112))
    r, c = iota((1792, 256), 0), iota((1792, 256), 1)
    sum_v = onehot(
        functools.reduce(
            jnp.logical_or,
            [(r - c == 112 * (7 * (k // 8) + k % 8)) & (c >= 112 * (k // 8)) & (c < 112 * (k // 8 + 1)) for k in range(16)],
        )
    )
    r, c = iota((128, 256), 0), iota((128, 256), 1)
    spread = onehot((r < 16) & (c < 224) & ((c >= 112) == (r >= 8)))
    spread_new = onehot((r < 2) & (c < 224) & ((c >= 112) == (r >= 1)))
    head_lane = iota((256, 128), 1)
    for e, ref in enumerate((own_ref, rec_ref)):
        half = core if e == 0 else 1 - core
        at = pl.multiple_of(half * 256, 256)
        keys = tk_ref[pl.ds(at, 256), :].astype(F32)
        live = (head_lane & 7) < len_ref[pl.ds(at, 256), :]
        live = live & (head_lane < 16)
        values = tv_ref[pl.ds(at, 256), :]
        new_keys = [dot(ref[t * 256 : (t + 1) * 256, 256:384], pick_k) for t in range(2)]
        for t in range(2):
            vq = ref[t * 256 : (t + 1) * 256, 0:256]
            one, two = split(dot(vq, expand_q) * keys)
            weight = kappa((dot(one, sum_a) + dot(two, sum_a)) * 0.25)
            weight = jnp.where(live, weight, 0.0)
            one, two = split(weight)
            den = dot(one, spread) + dot(two, spread)
            terms = dot(one, expand_w).astype(BF) * values
            num = dot(terms, sum_v)
            query = dot(vq, pick_q)
            for i in range(t + 1):
                one, two = split(query * new_keys[i])
                weight = kappa((dot(one, sum_new) + dot(two, sum_new)) * 0.25)
                one, two = split(weight)
                high = dot(one, spread_new)
                den = den + high + dot(two, spread_new)
                num = num + high * ref[i * 256 : (i + 1) * 256, 0:256].astype(F32)
            num_ref[e, t * 256 : (t + 1) * 256, :] = num
            den_ref[e, t * 256 : (t + 1) * 256, :] = den


def combine_kernel(pos_ref, g_ref, s_ref, num_ref, den_ref, rec_ref, own_ref, place_ref, same_ref, other_ref, buf):
    core = pos_ref[1]
    me = pos_ref[2]
    for p in range(32):
        holder, slot = g_ref[p], s_ref[p]

        @pl.when(holder != me)
        def _():
            buf[p * 16 : (p + 1) * 16, :] = rec_ref[holder]

        @pl.when(holder == me)
        def _():
            buf[p * 16 : (p + 1) * 16, :] = own_ref[slot]

    r, c = iota((256, 256), 0), iota((256, 256), 1)
    spread = onehot((c < 224) & (((c < 112) & ((r == 224) | (r == 226))) | ((c >= 112) & ((r == 225) | (r == 227)))))
    lane = iota((256, 256), 1)
    for e, out_ref in enumerate((same_ref, other_ref)):
        half = core if e == 0 else 1 - core
        at = pl.multiple_of(half * 256, 256)
        hot = onehot(iota((256, 512), 1) == place_ref[pl.ds(at, 256), :])
        prompt = dot(hot, buf[...])
        for t in range(2):
            part = prompt[:, t * 256 : (t + 1) * 256]
            den = den_ref[e, t * 256 : (t + 1) * 256, :] + dot(part.astype(BF), spread)
            num = num_ref[e, t * 256 : (t + 1) * 256, :] + part
            out = jnp.where(lane < 224, num / jnp.where(lane < 224, den, 1.0), 0.0)
            out_ref[t * 256 : (t + 1) * 256, :] = out.astype(BF)


def out_kernel(pos_ref, *refs):
    chunks, w_ref, tok_ref, out_ref = refs[:8], refs[8], refs[9], refs[10]
    core, col = pos_ref[1], pos_ref[3]
    acc = tok_ref[...].astype(F32)
    for s in range(4):
        for d in range(2):
            j = lax.rem(col + 4 - s, 4)
            k = core if d == 0 else 1 - core
            acc = acc + dot(chunks[s * 2 + d][:, 0:224], w_ref[j * 2 + k])
    out_ref[...] = acc.astype(BF)


def body(tokens, w_query, w_key, w_value, w_out, cached_state, cached_norm, slot_prompt, prompt_of, tail_keys, tail_values, tail_length):
    y, core, col = lax.axis_index("y"), lax.axis_index("core"), lax.axis_index("col")
    me = lax.axis_index(("req", "col"))
    pos = jnp.stack([y, core, me, col]).astype(jnp.int32)
    tok = jnp.transpose(tokens, (1, 0, 2)).reshape(512, 448)
    blocks = [tok] + [lax.ppermute(tok, "y", [(i, (i + s) % 4) for i in range(4)]) for s in range(1, 4)]
    value_w = jnp.moveaxis(w_value.reshape(2, 448, 112), 0, 1).reshape(448, 224)
    mine = jnp.concatenate([value_w, w_query, w_key], axis=1)
    theirs = lax.ppermute(mine, "core", [(0, 1), (1, 0)])
    w0, w1 = jnp.where(core == 0, mine, theirs), jnp.where(core == 0, theirs, mine)
    weights = jnp.concatenate(
        [w0[:, :256], w1[:, :256], w0[:, 256:], w1[:, 256:], jnp.zeros((448, 64), BF)], axis=1
    )
    w_all = lax.all_gather(w_out, ("y", "core"), axis=0, tiled=False)
    owner = slot_prompt // 32
    slots = jnp.arange(32, dtype=jnp.int32)
    away = owner != me
    code = jnp.max(
        jnp.where((owner[None, :] == slots[:, None]) & away[None, :], (slots * 32 + slot_prompt % 32 + 1)[None, :], 0), axis=1
    )
    told = lax.all_to_all(code[:, None], ("req", "col"), split_axis=0, concat_axis=0, tiled=True)[:, 0]
    here = (slot_prompt[None, :] == (me * 32 + slots)[:, None])
    there = (told[None, :] > 0) & ((told[None, :] - 1) % 32 == slots[:, None])
    at_slot = jnp.max(jnp.where(here, slots[None, :], 0), axis=1)
    at_holder = jnp.where(jnp.any(here, axis=1), me, jnp.max(jnp.where(there, slots[None, :], 0), axis=1)).astype(jnp.int32)
    index = jnp.arange(512)
    rank = jnp.sum(((prompt_of[None, :] == prompt_of[:, None]) & (index[None, :] < index[:, None])).astype(jnp.int32), axis=1)
    place = (prompt_of - me * 32) * 16 + rank
    norms = jnp.concatenate([cached_norm, cached_norm, jnp.zeros((32, 273, 28), BF)], axis=2)
    states = jnp.transpose(cached_state[0].reshape(273, 224, 32), (2, 0, 1))
    states = jnp.concatenate([states, norms], axis=2)

    partial = call(project_kernel, jax.ShapeDtypeStruct((4, 512, 640), BF), 1, 5)(pos, *blocks, weights)
    partial = lax.all_to_all(partial, "col", split_axis=0, concat_axis=0, tiled=True)
    shape = jax.ShapeDtypeStruct((512, 384), BF)
    own, oth = call(sum_kernel, (shape, shape), 1, 1)(pos, partial)
    rec = lax.ppermute(oth, "core", [(0, 1), (1, 0)])

    shape = jax.ShapeDtypeStruct((32, 16, 128), BF)
    q_send, q_keep = call(group_kernel, (shape, shape), 3, 3, scratch_shapes=[pltpu.VMEM((512, 128), BF)])(
        pos, at_holder, at_slot, own, rec, place.reshape(2, 1, 256)
    )
    q_rec = lax.all_to_all(q_send, ("req", "col"), split_axis=0, concat_axis=0, tiled=True)
    shape = jax.ShapeDtypeStruct((2, 512, 256), F32)
    num, den = call(tail_kernel, (shape, shape), 1, 5)(pos, own, rec, tail_keys, tail_values, tail_length[:, None])
    shape = jax.ShapeDtypeStruct((32, 16, 512), BF)
    whole = pl.BlockSpec((32, 16, 128), lambda i: (0, 0, 0))
    whole_out = pl.BlockSpec((32, 16, 512), lambda i: (0, 0, 0))
    r_send, r_keep = pl.pallas_call(
        slot_kernel,
        grid=(4,),
        out_shape=(shape, shape),
        in_specs=[SM, SM, whole, whole, pl.BlockSpec((8, 273, 256), lambda i: (i, 0, 0))],
        out_specs=(whole_out, whole_out),
        scratch_shapes=[pltpu.VMEM((128, 128), BF)],
        compiler_params=pltpu.CompilerParams(vmem_limit_bytes=VMEM_LIMIT),
    )(pos, owner, q_rec, q_keep, states)
    r_rec = lax.all_to_all(r_send, ("req", "col"), split_axis=0, concat_axis=0, tiled=True)
    shape = jax.ShapeDtypeStruct((512, 256), BF)
    same, other = call(combine_kernel, (shape, shape), 3, 5, scratch_shapes=[pltpu.VMEM((512, 512), BF)])(
        pos, at_holder, at_slot, num, den, r_rec, r_keep, place[:, None]
    )

    def at(y, core, col):
        return (y * 2 + core) * 4 + col

    chunks = []
    for s in range(4):
        for d, part in ((0, same), (1, other)):
            perm = [
                (at(j, k, b), at(b, k ^ d, (j + s) % 4)) for b in range(4) for j in range(4) for k in range(2)
            ]
            chunks.append(lax.ppermute(part, ("y", "core", "col"), perm))
    out = call(out_kernel, jax.ShapeDtypeStruct((512, 448), BF), 1, 10)(pos, *chunks, w_all, tok)
    return jnp.transpose(out.reshape(2, 256, 448), (1, 0, 2))


def solution(mesh):
    inner = Mesh(mesh.devices.reshape(8, 4, 2, 4), ("req", "y", "core", "col"))
    rows = ("y", "core")
    hold = ("req", "col")
    return jax.shard_map(
        body,
        mesh=inner,
        in_specs=(
            P(("req", "y", "core"), None, "col"),
            P("col", rows),
            P("col", rows),
            P(rows, "col"),
            P(rows, "col"),
            P(hold, None, rows),
            P(hold, None, rows),
            P(hold),
            P(hold),
            P(hold, rows),
            P(hold, rows),
            P(hold),
        ),
        out_specs=P(("req", "y", "core"), None, "col"),
        check_vma=False,
    )
```

```python
import functools

import jax
import jax.numpy as jnp
from jax import lax
from jax.experimental import pallas as pl
from jax.experimental.pallas import tpu as pltpu
from jax.sharding import Mesh, PartitionSpec as P

BF = jnp.bfloat16
F32 = jnp.float32
VMEM_LIMIT = 48 * 1024 * 1024
VM = pl.BlockSpec(memory_space=pltpu.VMEM)
SM = pl.BlockSpec(memory_space=pltpu.SMEM)


def dot(a, b):
    return jnp.dot(a, b, preferred_element_type=F32)


def iota(shape, dim):
    return lax.broadcasted_iota(jnp.int32, shape, dim)


def onehot(cond):
    return jnp.where(cond, 1.0, 0.0).astype(BF)


def split(x):
    high = x.astype(BF)
    return high, (x - high.astype(F32)).astype(BF)


def call(kernel, out_shapes, n_smem, n_vmem, **kw):
    return pl.pallas_call(
        kernel,
        out_shape=out_shapes,
        in_specs=[SM] * n_smem + [VM] * n_vmem,
        out_specs=jax.tree.map(lambda _: VM, out_shapes),
        compiler_params=pltpu.CompilerParams(vmem_limit_bytes=VMEM_LIMIT),
        **kw,
    )


def order_kernel(pos_ref, t0, t1, t2, t3, out_ref):
    for shift, block in enumerate((t0, t1, t2, t3)):
        out_ref[lax.rem(pos_ref[0] + 4 - shift, 4)] = block[...]


def project_kernel(pos_ref, t_ref, *refs):
    weights, own_ref, oth_ref, padded = refs[:8], refs[8], refs[9], refs[10]
    padded[0:64, :] = jnp.zeros((64, 288), BF)
    for which, out_ref in enumerate((own_ref, oth_ref)):
        first = second = None
        for shift in range(4):
            block = lax.rem(pos_ref[3] + 4 - shift, 4)
            w = weights[which * 4 + shift][...]
            padded[64:512, :] = w
            one = dot(t_ref[block, :, 0:448], w)
            two = dot(t_ref[block, :, 384:896], padded[...])
            first = one if first is None else first + one
            second = two if second is None else second + two
        out_ref[0:256, :] = first.astype(BF)
        out_ref[256:512, :] = second.astype(BF)


def group_kernel(pos_ref, g_ref, s_ref, own_ref, rec_ref, place_ref, send_ref, keep_ref, grouped):
    core = pos_ref[1]
    me = pos_ref[2]
    rows, cols = iota((256, 128), 0), iota((256, 128), 1)
    acc = None
    for e, ref in enumerate((own_ref, rec_ref)):
        half = core if e == 0 else 1 - core
        queries = None
        for t in range(2):
            pick = onehot((rows >= 224) & (cols == rows - 224 + 32 * t))
            part = dot(ref[t * 256 : (t + 1) * 256, 0:256], pick)
            queries = part if queries is None else queries + part
        hot = onehot(iota((512, 256), 0) == place_ref[half])
        part = dot(hot, queries.astype(BF))
        acc = part if acc is None else acc + part
    grouped[...] = acc.astype(BF)
    send_ref[...] = jnp.zeros_like(send_ref)
    keep_ref[...] = jnp.zeros_like(keep_ref)
    for p in range(32):
        holder, slot = g_ref[p], s_ref[p]

        @pl.when(holder != me)
        def _():
            send_ref[holder] = grouped[p * 16 : (p + 1) * 16, :]

        @pl.when(holder == me)
        def _():
            keep_ref[slot] = grouped[p * 16 : (p + 1) * 16, :]


def slot_kernel(pos_ref, owner_ref, rec_ref, keep_ref, state_ref, send_ref, own_ref, buf):
    me = pos_ref[2]
    step = pl.program_id(0)

    @pl.when(step == 0)
    def _():
        send_ref[...] = jnp.zeros_like(send_ref)
        own_ref[...] = jnp.zeros_like(own_ref)

    for i in range(8):
        slot = step * 8 + i
        owner = owner_ref[slot]

        @pl.when(owner != me)
        def _():
            buf[i * 16 : (i + 1) * 16, :] = rec_ref[owner]

        @pl.when(owner == me)
        def _():
            buf[i * 16 : (i + 1) * 16, :] = keep_ref[slot]

    q = buf[...]
    row, f = iota((128, 384), 0), iota((128, 384), 1)
    lane = iota((1, 384), 1)
    square, line = lane >= 17, (lane >= 1) & (lane < 17)
    unit_a = jnp.where(lane == 0, 1.0, 0.0)
    unit_b = jnp.where(lane < 17, 1.0, 0.0)
    scale = jnp.where(square, 0.5**0.5 / 4.0, jnp.where(line, 0.5, 1.0))
    scale = jnp.where(lane < 273, scale, 0.0)
    a_at = jnp.where(f >= 17, lax.shift_right_logical(f - 17, 4), f - 1)
    b_at = (f - 17) & 15
    live_a = (f >= 1) & (f < 273)
    live_b = (f >= 17) & (f < 273)
    high, low = [], []
    for t in range(2):
        for h in range(2):
            base = t * 32 + h * 16
            left = dot(q, onehot(live_a & (row == a_at + base))) + unit_a
            right = dot(q, onehot(live_b & (row == b_at + base))) + unit_b
            one, two = split(left * right * scale)
            high.append(one)
            low.append(two)
    out_lane = iota((16, 256), 1)
    first_head = (out_lane < 112) | (out_lane == 224) | (out_lane == 226)
    for i in range(8):
        phi = jnp.concatenate([x[i * 16 : (i + 1) * 16, 0:273] for x in high + low], axis=0)
        both = dot(phi, state_ref[i])
        terms = both[0:64] + both[64:128]
        results = []
        for t in range(2):
            r = jnp.where(first_head, terms[t * 32 : t * 32 + 16], terms[t * 32 + 16 : t * 32 + 32])
            rough = r.astype(BF).astype(F32)
            results.append(jnp.where(out_lane >= 226, r - rough, r).astype(BF))
        slot = step * 8 + i
        owner = owner_ref[slot]

        @pl.when(owner != me)
        def _():
            send_ref[owner, :, 0:256] = results[0]
            send_ref[owner, :, 256:512] = results[1]

        @pl.when(owner == me)
        def _():
            own_ref[slot, :, 0:256] = results[0]
            own_ref[slot, :, 256:512] = results[1]


def kappa(s):
    return 1.0 + s + 0.5 * s * s


def tail_kernel(pos_ref, own_ref, rec_ref, tk_ref, tv_ref, len_ref, num_ref, den_ref):
    core = pos_ref[1]
    r, c = iota((256, 256), 0), iota((256, 256), 1)
    expand_q = onehot((r >= 224) & (r - 224 == lax.shift_right_logical(c, 7) * 16 + (c & 15)))
    r, c = iota((256, 128), 0), iota((256, 128), 1)
    sum_a = onehot(lax.shift_right_logical(r, 4) == c)
    pick_q = onehot((r >= 224) & (r - 224 == c))
    r, c = iota((128, 128), 0), iota((128, 128), 1)
    pick_k = onehot(iota((32, 128), 0) == iota((32, 128), 1))
    sum_new = onehot((r < 32) & (lax.shift_right_logical(r, 4) == c))
    r, c = iota((128, 1792), 0), iota((128, 1792), 1)
    expand_w = onehot((r < 16) & (c >= r * 112) & (c < (r + 1) * 112))
    r, c = iota((1792, 256), 0), iota((1792, 256), 1)
    sum_v = onehot(
        functools.reduce(
            jnp.logical_or,
            [(r - c == 112 * (7 * (k // 8) + k % 8)) & (c >= 112 * (k // 8)) & (c < 112 * (k // 8 + 1)) for k in range(16)],
        )
    )
    r, c = iota((128, 256), 0), iota((128, 256), 1)
    spread = onehot((r < 16) & (c < 224) & ((c >= 112) == (r >= 8)))
    spread_new = onehot((r < 2) & (c < 224) & ((c >= 112) == (r >= 1)))
    head_lane = iota((256, 128), 1)
    for e, ref in enumerate((own_ref, rec_ref)):
        half = core if e == 0 else 1 - core
        at = pl.multiple_of(half * 256, 256)
        keys = tk_ref[pl.ds(at, 256), :].astype(F32)
        live = (head_lane & 7) < len_ref[pl.ds(at, 256), :]
        live = live & (head_lane < 16)
        values = tv_ref[pl.ds(at, 256), :]
        new_keys = [dot(ref[t * 256 : (t + 1) * 256, 256:288], pick_k) for t in range(2)]
        for t in range(2):
            vq = ref[t * 256 : (t + 1) * 256, 0:256]
            one, two = split(dot(vq, expand_q) * keys)
            weight = kappa((dot(one, sum_a) + dot(two, sum_a)) * 0.25)
            weight = jnp.where(live, weight, 0.0)
            one, two = split(weight)
            den = dot(one, spread) + dot(two, spread)
            terms = dot(one, expand_w).astype(BF) * values
            num = dot(terms, sum_v)
            query = dot(vq, pick_q)
            for i in range(t + 1):
                one, two = split(query * new_keys[i])
                weight = kappa((dot(one, sum_new) + dot(two, sum_new)) * 0.25)
                one, two = split(weight)
                high = dot(one, spread_new)
                den = den + high + dot(two, spread_new)
                num = num + high * ref[i * 256 : (i + 1) * 256, 0:256].astype(F32)
            num_ref[e, t * 256 : (t + 1) * 256, :] = num
            den_ref[e, t * 256 : (t + 1) * 256, :] = den


def combine_kernel(pos_ref, g_ref, s_ref, num_ref, den_ref, rec_ref, own_ref, place_ref, out_ref, buf):
    core = pos_ref[1]
    me = pos_ref[2]
    for p in range(32):
        holder, slot = g_ref[p], s_ref[p]

        @pl.when(holder != me)
        def _():
            buf[p * 16 : (p + 1) * 16, :] = rec_ref[holder]

        @pl.when(holder == me)
        def _():
            buf[p * 16 : (p + 1) * 16, :] = own_ref[slot]

    r, c = iota((256, 256), 0), iota((256, 256), 1)
    spread = onehot((c < 224) & (((c < 112) & ((r == 224) | (r == 226))) | ((c >= 112) & ((r == 225) | (r == 227)))))
    lane = iota((256, 256), 1)
    for e in range(2):
        half = core if e == 0 else 1 - core
        at = pl.multiple_of(half * 256, 256)
        hot = onehot(iota((256, 512), 1) == place_ref[pl.ds(at, 256), :])
        prompt = dot(hot, buf[...])
        for t in range(2):
            part = prompt[:, t * 256 : (t + 1) * 256]
            den = den_ref[e, t * 256 : (t + 1) * 256, :] + dot(part.astype(BF), spread)
            num = num_ref[e, t * 256 : (t + 1) * 256, :] + part
            out = jnp.where(lane < 224, num / jnp.where(lane < 224, den, 1.0), 0.0)
            out = out.astype(BF)
            for part in range(2):
                out_ref[half * 2 + part, t * 128 : (t + 1) * 128, :] = out[part * 128 : (part + 1) * 128]


def out_kernel(pos_ref, own_ref, oth_ref, w0, w1, w2, w3, first_ref, second_ref):
    y, core, col = pos_ref[0], pos_ref[1], pos_ref[3]
    acc = [None, None]
    for shift, w_ref in enumerate((w0, w1, w2, w3)):
        j = lax.rem(y + 4 - shift, 4)
        for which, ref in enumerate((own_ref, oth_ref)):
            k = core if which == 0 else 1 - core
            heads = ref[j, :, 0:224]
            for e in range(2):
                part = dot(heads, w_ref[jnp.bitwise_xor(2 * e + k, col)])
                acc[e] = part if acc[e] is None else acc[e] + part
    even = lax.rem(y, 2) == 0
    first_ref[...] = jnp.where(even, acc[0], acc[1]).astype(BF)
    second_ref[...] = jnp.where(even, acc[1], acc[0]).astype(BF)


def body(tokens, w_query, w_key, w_value, w_out, cached_state, cached_norm, slot_prompt, prompt_of, tail_keys, tail_values, tail_length):
    y, core, col = lax.axis_index("y"), lax.axis_index("core"), lax.axis_index("col")
    me = lax.axis_index(("req", "col"))
    pos = jnp.stack([y, core, me, col]).astype(jnp.int32)
    tok = tokens.reshape(256, 896)
    blocks = [tok] + [lax.ppermute(tok, "y", [(i, (i + s) % 4) for i in range(4)]) for s in range(1, 4)]
    value_w = jnp.moveaxis(w_value.reshape(2, 448, 112), 0, 1).reshape(448, 224)
    mine = jnp.concatenate([value_w, w_query, w_key], axis=1)
    mine = [mine] + [lax.ppermute(mine, "col", [(i, (i + s) % 4) for i in range(4)]) for s in range(1, 4)]
    theirs = [lax.ppermute(w, "core", [(0, 1), (1, 0)]) for w in mine]
    owner = slot_prompt // 32
    slots = jnp.arange(32, dtype=jnp.int32)
    away = owner != me
    code = jnp.max(
        jnp.where((owner[None, :] == slots[:, None]) & away[None, :], (slots * 32 + slot_prompt % 32 + 1)[None, :], 0), axis=1
    )
    told = lax.all_to_all(code[:, None], ("req", "col"), split_axis=0, concat_axis=0, tiled=True)[:, 0]
    here = (slot_prompt[None, :] == (me * 32 + slots)[:, None])
    there = (told[None, :] > 0) & ((told[None, :] - 1) % 32 == slots[:, None])
    at_slot = jnp.max(jnp.where(here, slots[None, :], 0), axis=1)
    at_holder = jnp.where(jnp.any(here, axis=1), me, jnp.max(jnp.where(there, slots[None, :], 0), axis=1)).astype(jnp.int32)
    index = jnp.arange(512)
    rank = jnp.sum(((prompt_of[None, :] == prompt_of[:, None]) & (index[None, :] < index[:, None])).astype(jnp.int32), axis=1)
    place = (prompt_of - me * 32) * 16 + rank
    norms = jnp.concatenate([cached_norm, cached_norm, jnp.zeros((32, 273, 28), BF)], axis=2)
    states = jnp.transpose(cached_state[0].reshape(273, 224, 32), (2, 0, 1))
    states = jnp.concatenate([states, norms], axis=2)

    held = call(order_kernel, jax.ShapeDtypeStruct((4, 256, 896), BF), 1, 4)(pos, *blocks)
    held = lax.all_to_all(held, "col", split_axis=0, concat_axis=0, tiled=True)
    shape = jax.ShapeDtypeStruct((512, 288), BF)
    own, oth = call(project_kernel, (shape, shape), 1, 9, scratch_shapes=[pltpu.VMEM((512, 288), BF)])(
        pos, held, *mine, *theirs
    )
    rec = lax.ppermute(oth, "core", [(0, 1), (1, 0)])
    w_out, own = lax.optimization_barrier((w_out, own))
    pieces = []
    for s in range(4):
        perm = [(k * 4 + c, (c >> 1) * 4 + (s ^ (2 * (c & 1) + k))) for k in range(2) for c in range(4)]
        pieces.append(lax.ppermute(w_out, ("core", "col"), perm))
    pieces = jnp.stack(pieces)
    out_w = [pieces] + [lax.ppermute(pieces, "y", [(i, (i + s) % 4) for i in range(4)]) for s in range(1, 4)]

    shape = jax.ShapeDtypeStruct((32, 16, 128), BF)
    q_send, q_keep = call(group_kernel, (shape, shape), 3, 3, scratch_shapes=[pltpu.VMEM((512, 128), BF)])(
        pos, at_holder, at_slot, own, rec, place.reshape(2, 1, 256)
    )
    q_rec = lax.all_to_all(q_send, ("req", "col"), split_axis=0, concat_axis=0, tiled=True)
    shape = jax.ShapeDtypeStruct((2, 512, 256), F32)
    num, den = call(tail_kernel, (shape, shape), 1, 5)(pos, own, rec, tail_keys, tail_values, tail_length[:, None])
    shape = jax.ShapeDtypeStruct((32, 16, 512), BF)
    whole = pl.BlockSpec((32, 16, 128), lambda i: (0, 0, 0))
    whole_out = pl.BlockSpec((32, 16, 512), lambda i: (0, 0, 0))
    r_send, r_keep = pl.pallas_call(
        slot_kernel,
        grid=(4,),
        out_shape=(shape, shape),
        in_specs=[SM, SM, whole, whole, pl.BlockSpec((8, 273, 256), lambda i: (i, 0, 0))],
        out_specs=(whole_out, whole_out),
        scratch_shapes=[pltpu.VMEM((128, 128), BF)],
        compiler_params=pltpu.CompilerParams(vmem_limit_bytes=VMEM_LIMIT),
    )(pos, owner, q_rec, q_keep, states)
    r_rec = lax.all_to_all(r_send, ("req", "col"), split_axis=0, concat_axis=0, tiled=True)
    shape = jax.ShapeDtypeStruct((4, 256, 256), BF)
    heads = call(combine_kernel, shape, 3, 5, scratch_shapes=[pltpu.VMEM((512, 512), BF)])(
        pos, at_holder, at_slot, num, den, r_rec, r_keep, place[:, None]
    )
    heads = lax.all_to_all(heads, "y", split_axis=0, concat_axis=0, tiled=True)
    heads_oth = lax.ppermute(heads, "core", [(0, 1), (1, 0)])
    shape = jax.ShapeDtypeStruct((256, 448), BF)
    mixed = call(out_kernel, (shape, shape), 1, 6)(pos, heads, heads_oth, *out_w)

    def at(y, core, col):
        return (y * 2 + core) * 4 + col

    got = []
    for s, part in enumerate(mixed):
        perm = [
            (at(j, k, b), at(b, j >> 1, 2 * k + (s ^ (j & 1)))) for b in range(4) for j in range(4) for k in range(2)
        ]
        got.append(lax.ppermute(part, ("y", "core", "col"), perm).reshape(2, 128, 448))
    odd = col % 2 == 1
    mixed = jnp.concatenate([jnp.where(odd, got[1], got[0]), jnp.where(odd, got[0], got[1])], axis=1)
    mixed = jnp.transpose(mixed, (1, 0, 2)).astype(F32)
    return (mixed + tokens.astype(F32)).astype(BF)


def solution(mesh):
    inner = Mesh(mesh.devices.reshape(8, 4, 2, 4), ("req", "y", "core", "col"))
    rows = ("y", "core")
    hold = ("req", "col")
    return jax.shard_map(
        body,
        mesh=inner,
        in_specs=(
            P(("req", "y", "core"), None, "col"),
            P("col", rows),
            P("col", rows),
            P(rows, "col"),
            P(rows, "col"),
            P(hold, None, rows),
            P(hold, None, rows),
            P(hold),
            P(hold),
            P(hold, rows),
            P(hold, rows),
            P(hold),
        ),
        out_specs=P(("req", "y", "core"), None, "col"),
        check_vma=False,
    )
```

```python
import functools

import jax
import jax.numpy as jnp
from jax import lax
from jax.experimental import pallas as pl
from jax.experimental.pallas import tpu as pltpu
from jax.sharding import Mesh, PartitionSpec as P

BF = jnp.bfloat16
F32 = jnp.float32
VMEM_LIMIT = 48 * 1024 * 1024
SM = pl.BlockSpec(memory_space=pltpu.SMEM)


def dot(a, b):
    return jnp.dot(a, b, preferred_element_type=F32)


def iota(shape, dim):
    return lax.broadcasted_iota(jnp.int32, shape, dim)


def onehot(cond):
    return jnp.where(cond, 1.0, 0.0).astype(BF)


def split(x):
    high = x.astype(BF)
    return high, (x - high.astype(F32)).astype(BF)


def call(kernel, out_shapes, n_smem, *args, scratch=()):
    def full(shape):
        zeros = (0,) * len(shape)
        return pl.BlockSpec(shape, lambda i: zeros)

    return pl.pallas_call(
        kernel,
        grid=(1,),
        out_shape=out_shapes,
        in_specs=[SM] * n_smem + [full(x.shape) for x in args[n_smem:]],
        out_specs=jax.tree.map(lambda x: full(x.shape), out_shapes),
        scratch_shapes=scratch,
        compiler_params=pltpu.CompilerParams(vmem_limit_bytes=VMEM_LIMIT),
    )(*args)


def order_kernel(pos_ref, t0, t1, t2, t3, out_ref):
    for shift, block in enumerate((t0, t1, t2, t3)):
        out_ref[lax.rem(pos_ref[0] + 4 - shift, 4)] = block[...]


def project_kernel(pos_ref, t_ref, *refs):
    weights, own_ref, oth_ref, padded = refs[:8], refs[8], refs[9], refs[10]
    padded[0:64, :] = jnp.zeros((64, 288), BF)
    for which, out_ref in enumerate((own_ref, oth_ref)):
        first = second = None
        for shift in range(4):
            block = lax.rem(pos_ref[3] + 4 - shift, 4)
            w = weights[which * 4 + shift][...]
            padded[64:512, :] = w
            one = dot(t_ref[block, :, 0:448], w)
            two = dot(t_ref[block, :, 384:896], padded[...])
            first = one if first is None else first + one
            second = two if second is None else second + two
        out_ref[0:256, :] = first.astype(BF)
        out_ref[256:512, :] = second.astype(BF)


def group_kernel(pos_ref, g_ref, s_ref, own_ref, rec_ref, place_ref, send_ref, keep_ref, grouped):
    core = pos_ref[1]
    me = pos_ref[2]
    rows, cols = iota((256, 128), 0), iota((256, 128), 1)
    acc = None
    for e, ref in enumerate((own_ref, rec_ref)):
        half = core if e == 0 else 1 - core
        queries = None
        for t in range(2):
            pick = onehot((rows >= 224) & (cols == rows - 224 + 32 * t))
            part = dot(ref[t * 256 : (t + 1) * 256, 0:256], pick)
            queries = part if queries is None else queries + part
        hot = onehot(iota((512, 256), 0) == place_ref[half])
        part = dot(hot, queries.astype(BF))
        acc = part if acc is None else acc + part
    grouped[...] = acc.astype(BF)
    send_ref[...] = jnp.zeros_like(send_ref)
    keep_ref[...] = jnp.zeros_like(keep_ref)
    for p in range(32):
        holder, slot = g_ref[p], s_ref[p]

        @pl.when(holder != me)
        def _():
            send_ref[holder] = grouped[p * 16 : (p + 1) * 16, :]

        @pl.when(holder == me)
        def _():
            keep_ref[slot] = grouped[p * 16 : (p + 1) * 16, :]


def slot_kernel(pos_ref, owner_ref, rec_ref, keep_ref, state_ref, send_ref, own_ref, buf):
    me = pos_ref[2]
    step = pl.program_id(0)

    @pl.when(step == 0)
    def _():
        send_ref[...] = jnp.zeros_like(send_ref)
        own_ref[...] = jnp.zeros_like(own_ref)

    for i in range(8):
        slot = step * 8 + i
        owner = owner_ref[slot]

        @pl.when(owner != me)
        def _():
            buf[i * 16 : (i + 1) * 16, :] = rec_ref[owner]

        @pl.when(owner == me)
        def _():
            buf[i * 16 : (i + 1) * 16, :] = keep_ref[slot]

    q = buf[...]
    row, f = iota((128, 384), 0), iota((128, 384), 1)
    lane = iota((1, 384), 1)
    square, line = lane >= 17, (lane >= 1) & (lane < 17)
    unit_a = jnp.where(lane == 0, 1.0, 0.0)
    unit_b = jnp.where(lane < 17, 1.0, 0.0)
    scale = jnp.where(square, 0.5**0.5 / 4.0, jnp.where(line, 0.5, 1.0))
    scale = jnp.where(lane < 273, scale, 0.0)
    a_at = jnp.where(f >= 17, lax.shift_right_logical(f - 17, 4), f - 1)
    b_at = (f - 17) & 15
    live_a = (f >= 1) & (f < 273)
    live_b = (f >= 17) & (f < 273)
    high, low = [], []
    for t in range(2):
        for h in range(2):
            base = t * 32 + h * 16
            left = dot(q, onehot(live_a & (row == a_at + base))) + unit_a
            right = dot(q, onehot(live_b & (row == b_at + base))) + unit_b
            one, two = split(left * right * scale)
            high.append(one)
            low.append(two)
    out_lane = iota((16, 256), 1)
    first_head = (out_lane < 112) | (out_lane == 224) | (out_lane == 226)
    for i in range(8):
        phi = jnp.concatenate([x[i * 16 : (i + 1) * 16, 0:273] for x in high + low], axis=0)
        both = dot(phi, state_ref[i])
        terms = both[0:64] + both[64:128]
        results = []
        for t in range(2):
            r = jnp.where(first_head, terms[t * 32 : t * 32 + 16], terms[t * 32 + 16 : t * 32 + 32])
            rough = r.astype(BF).astype(F32)
            results.append(jnp.where(out_lane >= 226, r - rough, r).astype(BF))
        slot = step * 8 + i
        owner = owner_ref[slot]

        @pl.when(owner != me)
        def _():
            send_ref[owner, :, 0:256] = results[0]
            send_ref[owner, :, 256:512] = results[1]

        @pl.when(owner == me)
        def _():
            own_ref[slot, :, 0:256] = results[0]
            own_ref[slot, :, 256:512] = results[1]


def kappa(s):
    return 1.0 + s + 0.5 * s * s


def tail_kernel(pos_ref, own_ref, rec_ref, tk_ref, tv_ref, len_ref, num_ref, den_ref):
    core = pos_ref[1]
    r, c = iota((256, 256), 0), iota((256, 256), 1)
    expand_q = onehot((r >= 224) & (r - 224 == lax.shift_right_logical(c, 7) * 16 + (c & 15)))
    r, c = iota((256, 128), 0), iota((256, 128), 1)
    sum_a = onehot(lax.shift_right_logical(r, 4) == c)
    pick_q = onehot((r >= 224) & (r - 224 == c))
    r, c = iota((128, 128), 0), iota((128, 128), 1)
    pick_k = onehot(iota((32, 128), 0) == iota((32, 128), 1))
    sum_new = onehot((r < 32) & (lax.shift_right_logical(r, 4) == c))
    r, c = iota((128, 1792), 0), iota((128, 1792), 1)
    expand_w = onehot((r < 16) & (c >= r * 112) & (c < (r + 1) * 112))
    r, c = iota((1792, 256), 0), iota((1792, 256), 1)
    sum_v = onehot(
        functools.reduce(
            jnp.logical_or,
            [(r - c == 112 * (7 * (k // 8) + k % 8)) & (c >= 112 * (k // 8)) & (c < 112 * (k // 8 + 1)) for k in range(16)],
        )
    )
    r, c = iota((128, 256), 0), iota((128, 256), 1)
    spread = onehot((r < 16) & (c < 224) & ((c >= 112) == (r >= 8)))
    spread_new = onehot((r < 2) & (c < 224) & ((c >= 112) == (r >= 1)))
    head_lane = iota((256, 128), 1)
    for e, ref in enumerate((own_ref, rec_ref)):
        half = core if e == 0 else 1 - core
        at = pl.multiple_of(half * 256, 256)
        keys = tk_ref[pl.ds(at, 256), :].astype(F32)
        live = (head_lane & 7) < len_ref[pl.ds(at, 256), :]
        live = live & (head_lane < 16)
        values = tv_ref[pl.ds(at, 256), :]
        new_keys = [dot(ref[t * 256 : (t + 1) * 256, 256:288], pick_k) for t in range(2)]
        for t in range(2):
            vq = ref[t * 256 : (t + 1) * 256, 0:256]
            one, two = split(dot(vq, expand_q) * keys)
            weight = kappa((dot(one, sum_a) + dot(two, sum_a)) * 0.25)
            weight = jnp.where(live, weight, 0.0)
            one, two = split(weight)
            den = dot(one, spread) + dot(two, spread)
            terms = dot(one, expand_w).astype(BF) * values
            num = dot(terms, sum_v)
            query = dot(vq, pick_q)
            for i in range(t + 1):
                one, two = split(query * new_keys[i])
                weight = kappa((dot(one, sum_new) + dot(two, sum_new)) * 0.25)
                one, two = split(weight)
                high = dot(one, spread_new)
                den = den + high + dot(two, spread_new)
                num = num + high * ref[i * 256 : (i + 1) * 256, 0:256].astype(F32)
            num_ref[e, t * 256 : (t + 1) * 256, :] = num
            den_ref[e, t * 256 : (t + 1) * 256, :] = den


def combine_kernel(pos_ref, g_ref, s_ref, num_ref, den_ref, rec_ref, own_ref, place_ref, out_ref, buf):
    core = pos_ref[1]
    me = pos_ref[2]
    for p in range(32):
        holder, slot = g_ref[p], s_ref[p]

        @pl.when(holder != me)
        def _():
            buf[p * 16 : (p + 1) * 16, :] = rec_ref[holder]

        @pl.when(holder == me)
        def _():
            buf[p * 16 : (p + 1) * 16, :] = own_ref[slot]

    r, c = iota((256, 256), 0), iota((256, 256), 1)
    spread = onehot((c < 224) & (((c < 112) & ((r == 224) | (r == 226))) | ((c >= 112) & ((r == 225) | (r == 227)))))
    lane = iota((256, 256), 1)
    for e in range(2):
        half = core if e == 0 else 1 - core
        at = pl.multiple_of(half * 256, 256)
        hot = onehot(iota((256, 512), 1) == place_ref[pl.ds(at, 256), :])
        prompt = dot(hot, buf[...])
        for t in range(2):
            part = prompt[:, t * 256 : (t + 1) * 256]
            den = den_ref[e, t * 256 : (t + 1) * 256, :] + dot(part.astype(BF), spread)
            num = num_ref[e, t * 256 : (t + 1) * 256, :] + part
            out = jnp.where(lane < 224, num / jnp.where(lane < 224, den, 1.0), 0.0)
            out = out.astype(BF)
            for part in range(2):
                out_ref[half * 2 + part, t * 128 : (t + 1) * 128, :] = out[part * 128 : (part + 1) * 128]


def out_kernel(pos_ref, own_ref, oth_ref, w0, w1, w2, w3, first_ref, second_ref):
    y, core, col = pos_ref[0], pos_ref[1], pos_ref[3]
    acc = [None, None]
    for shift, w_ref in enumerate((w0, w1, w2, w3)):
        j = lax.rem(y + 4 - shift, 4)
        for which, ref in enumerate((own_ref, oth_ref)):
            k = core if which == 0 else 1 - core
            heads = ref[j, :, 0:224]
            for e in range(2):
                part = dot(heads, w_ref[jnp.bitwise_xor(2 * e + k, col)])
                acc[e] = part if acc[e] is None else acc[e] + part
    even = lax.rem(y, 2) == 0
    first_ref[...] = jnp.where(even, acc[0], acc[1]).astype(BF)
    second_ref[...] = jnp.where(even, acc[1], acc[0]).astype(BF)


def body(tokens, w_query, w_key, w_value, w_out, cached_state, cached_norm, slot_prompt, prompt_of, tail_keys, tail_values, tail_length):
    y, core, col = lax.axis_index("y"), lax.axis_index("core"), lax.axis_index("col")
    me = lax.axis_index(("req", "col"))
    pos = jnp.stack([y, core, me, col]).astype(jnp.int32)
    def shifts(x, axis):
        return [x] + [lax.ppermute(x, axis, [(i, (i + s) % 4) for i in range(4)]) for s in range(1, 4)]

    tok = tokens.reshape(256, 896)
    blocks = shifts(tok, "y")
    value_w = jnp.moveaxis(w_value.reshape(2, 448, 112), 0, 1).reshape(448, 224)
    mine = shifts(jnp.concatenate([value_w, w_query, w_key], axis=1), "col")
    pieces = []
    for s in range(4):
        perm = [(k * 4 + c, (c >> 1) * 4 + (s ^ (2 * (c & 1) + k))) for k in range(2) for c in range(4)]
        pieces.append(lax.ppermute(w_out, ("core", "col"), perm))
    blocks, mine, pieces = lax.optimization_barrier((blocks, mine, pieces))
    pieces = jnp.stack(pieces)

    def later(x, step):
        x, held_back = lax.optimization_barrier((x, pieces))
        return x, lax.ppermute(held_back, "y", [(i, (i + step) % 4) for i in range(4)])

    owner = slot_prompt // 32
    slots = jnp.arange(32, dtype=jnp.int32)
    away = owner != me
    code = jnp.max(
        jnp.where((owner[None, :] == slots[:, None]) & away[None, :], (slots * 32 + slot_prompt % 32 + 1)[None, :], 0), axis=1
    )
    told = lax.all_to_all(code[:, None], ("req", "col"), split_axis=0, concat_axis=0, tiled=True)[:, 0]
    here = (slot_prompt[None, :] == (me * 32 + slots)[:, None])
    there = (told[None, :] > 0) & ((told[None, :] - 1) % 32 == slots[:, None])
    at_slot = jnp.max(jnp.where(here, slots[None, :], 0), axis=1)
    at_holder = jnp.where(jnp.any(here, axis=1), me, jnp.max(jnp.where(there, slots[None, :], 0), axis=1)).astype(jnp.int32)
    index = jnp.arange(512)
    rank = jnp.sum(((prompt_of[None, :] == prompt_of[:, None]) & (index[None, :] < index[:, None])).astype(jnp.int32), axis=1)
    place = (prompt_of - me * 32) * 16 + rank
    norms = jnp.concatenate([cached_norm, cached_norm, jnp.zeros((32, 273, 28), BF)], axis=2)
    states = jnp.transpose(cached_state[0].reshape(273, 224, 32), (2, 0, 1))
    states = jnp.concatenate([states, norms], axis=2)

    held = call(order_kernel, jax.ShapeDtypeStruct((4, 256, 896), BF), 1, pos, *blocks)
    held, out_w1 = later(held, 1)
    theirs = [lax.ppermute(w, "core", [(0, 1), (1, 0)]) for w in mine]
    held = lax.all_to_all(held, "col", split_axis=0, concat_axis=0, tiled=True)
    held, out_w1 = lax.optimization_barrier((held, out_w1))
    shape = jax.ShapeDtypeStruct((512, 288), BF)
    own, oth = call(project_kernel, (shape, shape), 1, pos, held, *mine, *theirs, scratch=[pltpu.VMEM((512, 288), BF)])
    oth, out_w2 = later(oth, 2)
    rec = lax.ppermute(oth, "core", [(0, 1), (1, 0)])

    shape = jax.ShapeDtypeStruct((32, 16, 128), BF)
    q_send, q_keep = call(
        group_kernel,
        (shape, shape),
        3,
        pos,
        at_holder,
        at_slot,
        own,
        rec,
        place.reshape(2, 1, 256),
        scratch=[pltpu.VMEM((512, 128), BF)],
    )
    q_rec = lax.all_to_all(q_send, ("req", "col"), split_axis=0, concat_axis=0, tiled=True)
    q_rec, out_w2 = lax.optimization_barrier((q_rec, out_w2))
    shape = jax.ShapeDtypeStruct((2, 512, 256), F32)
    num, den = call(tail_kernel, (shape, shape), 1, pos, own, rec, tail_keys, tail_values, tail_length[:, None])
    shape = jax.ShapeDtypeStruct((32, 16, 512), BF)
    whole = pl.BlockSpec((32, 16, 128), lambda i: (0, 0, 0))
    whole_out = pl.BlockSpec((32, 16, 512), lambda i: (0, 0, 0))
    r_send, r_keep = pl.pallas_call(
        slot_kernel,
        grid=(4,),
        out_shape=(shape, shape),
        in_specs=[SM, SM, whole, whole, pl.BlockSpec((8, 273, 256), lambda i: (i, 0, 0))],
        out_specs=(whole_out, whole_out),
        scratch_shapes=[pltpu.VMEM((128, 128), BF)],
        compiler_params=pltpu.CompilerParams(vmem_limit_bytes=VMEM_LIMIT),
    )(pos, owner, q_rec, q_keep, states)
    r_send, out_w3 = later(r_send, 3)
    r_rec = lax.all_to_all(r_send, ("req", "col"), split_axis=0, concat_axis=0, tiled=True)
    r_rec, out_w3 = lax.optimization_barrier((r_rec, out_w3))
    heads = call(
        combine_kernel,
        jax.ShapeDtypeStruct((4, 256, 256), BF),
        3,
        pos,
        at_holder,
        at_slot,
        num,
        den,
        r_rec,
        r_keep,
        place[:, None],
        scratch=[pltpu.VMEM((512, 512), BF)],
    )
    heads = lax.all_to_all(heads, "y", split_axis=0, concat_axis=0, tiled=True)
    heads_oth = lax.ppermute(heads, "core", [(0, 1), (1, 0)])
    shape = jax.ShapeDtypeStruct((256, 448), BF)
    mixed = call(out_kernel, (shape, shape), 1, pos, heads, heads_oth, pieces, out_w1, out_w2, out_w3)

    def at(y, core, col):
        return (y * 2 + core) * 4 + col

    got = []
    for s, part in enumerate(mixed):
        perm = [
            (at(j, k, b), at(b, j >> 1, 2 * k + (s ^ (j & 1)))) for b in range(4) for j in range(4) for k in range(2)
        ]
        got.append(lax.ppermute(part, ("y", "core", "col"), perm).reshape(2, 128, 448))
    odd = col % 2 == 1
    mixed = jnp.concatenate([jnp.where(odd, got[1], got[0]), jnp.where(odd, got[0], got[1])], axis=1)
    mixed = jnp.transpose(mixed, (1, 0, 2)).astype(F32)
    return (mixed + tokens.astype(F32)).astype(BF)


def solution(mesh):
    inner = Mesh(mesh.devices.reshape(8, 4, 2, 4), ("req", "y", "core", "col"))
    rows = ("y", "core")
    hold = ("req", "col")
    return jax.shard_map(
        body,
        mesh=inner,
        in_specs=(
            P(("req", "y", "core"), None, "col"),
            P("col", rows),
            P("col", rows),
            P(rows, "col"),
            P(rows, "col"),
            P(hold, None, rows),
            P(hold, None, rows),
            P(hold),
            P(hold),
            P(hold, rows),
            P(hold, rows),
            P(hold),
        ),
        out_specs=P(("req", "y", "core"), None, "col"),
        check_vma=False,
    )
```

```python
import functools

import jax
import jax.numpy as jnp
from jax import lax
from jax.experimental import pallas as pl
from jax.experimental.pallas import tpu as pltpu
from jax.sharding import Mesh, PartitionSpec as P

BF = jnp.bfloat16
F32 = jnp.float32
VMEM_LIMIT = 48 * 1024 * 1024
SM = pl.BlockSpec(memory_space=pltpu.SMEM)


def dot(a, b):
    return jnp.dot(a, b, preferred_element_type=F32)


def iota(shape, dim):
    return lax.broadcasted_iota(jnp.int32, shape, dim)


def onehot(cond):
    return jnp.where(cond, 1.0, 0.0).astype(BF)


def split(x):
    high = x.astype(BF)
    return high, (x - high.astype(F32)).astype(BF)


def in_hbm(x):
    return pltpu.with_memory_space_constraint(x, pltpu.HBM)


def call(kernel, out_shapes, n_smem, *args, scratch=()):
    def full(shape):
        zeros = (0,) * len(shape)
        return pl.BlockSpec(shape, lambda i: zeros)

    return pl.pallas_call(
        kernel,
        grid=(1,),
        out_shape=jax.tree.map(lambda x: pltpu.HBM(x.shape, x.dtype), out_shapes),
        in_specs=[SM] * n_smem + [full(x.shape) for x in args[n_smem:]],
        out_specs=jax.tree.map(lambda x: full(x.shape), out_shapes),
        scratch_shapes=scratch,
        compiler_params=pltpu.CompilerParams(vmem_limit_bytes=VMEM_LIMIT),
    )(*args[:n_smem], *[in_hbm(x) for x in args[n_smem:]])


def order_kernel(pos_ref, t0, t1, t2, t3, out_ref):
    for shift, block in enumerate((t0, t1, t2, t3)):
        out_ref[lax.rem(pos_ref[0] + 4 - shift, 4)] = block[...]


def project_kernel(pos_ref, t_ref, *refs):
    weights, own_ref, oth_ref, padded = refs[:8], refs[8], refs[9], refs[10]
    padded[0:64, :] = jnp.zeros((64, 288), BF)
    for which, out_ref in enumerate((own_ref, oth_ref)):
        first = second = None
        for shift in range(4):
            block = lax.rem(pos_ref[3] + 4 - shift, 4)
            w = weights[which * 4 + shift][...]
            padded[64:512, :] = w
            one = dot(t_ref[block, :, 0:448], w)
            two = dot(t_ref[block, :, 384:896], padded[...])
            first = one if first is None else first + one
            second = two if second is None else second + two
        out_ref[0:256, :] = first.astype(BF)
        out_ref[256:512, :] = second.astype(BF)


def group_kernel(pos_ref, g_ref, s_ref, own_ref, rec_ref, place_ref, send_ref, keep_ref, grouped):
    core = pos_ref[1]
    me = pos_ref[2]
    rows, cols = iota((256, 128), 0), iota((256, 128), 1)
    acc = None
    for e, ref in enumerate((own_ref, rec_ref)):
        half = core if e == 0 else 1 - core
        queries = None
        for t in range(2):
            pick = onehot((rows >= 224) & (cols == rows - 224 + 32 * t))
            part = dot(ref[t * 256 : (t + 1) * 256, 0:256], pick)
            queries = part if queries is None else queries + part
        hot = onehot(iota((512, 256), 0) == place_ref[half])
        part = dot(hot, queries.astype(BF))
        acc = part if acc is None else acc + part
    grouped[...] = acc.astype(BF)
    send_ref[...] = jnp.zeros_like(send_ref)
    keep_ref[...] = jnp.zeros_like(keep_ref)
    for p in range(32):
        holder, slot = g_ref[p], s_ref[p]

        @pl.when(holder != me)
        def _():
            send_ref[holder] = grouped[p * 16 : (p + 1) * 16, :]

        @pl.when(holder == me)
        def _():
            keep_ref[slot] = grouped[p * 16 : (p + 1) * 16, :]


def slot_kernel(pos_ref, owner_ref, rec_ref, keep_ref, state_ref, norm_ref, send_ref, own_ref, buf, both_ref):
    me = pos_ref[2]
    step = pl.program_id(0)

    @pl.when(step == 0)
    def _():
        send_ref[...] = jnp.zeros_like(send_ref)
        own_ref[...] = jnp.zeros_like(own_ref)

    for i in range(8):
        slot = step * 8 + i
        owner = owner_ref[slot]

        @pl.when(owner != me)
        def _():
            buf[i * 16 : (i + 1) * 16, :] = rec_ref[owner]

        @pl.when(owner == me)
        def _():
            buf[i * 16 : (i + 1) * 16, :] = keep_ref[slot]

    q = buf[...]
    row, f = iota((128, 384), 0), iota((128, 384), 1)
    lane = iota((1, 384), 1)
    square, line = lane >= 17, (lane >= 1) & (lane < 17)
    unit_a = jnp.where(lane == 0, 1.0, 0.0)
    unit_b = jnp.where(lane < 17, 1.0, 0.0)
    scale = jnp.where(square, 0.5**0.5 / 4.0, jnp.where(line, 0.5, 1.0))
    scale = jnp.where(lane < 273, scale, 0.0)
    a_at = jnp.where(f >= 17, lax.shift_right_logical(f - 17, 4), f - 1)
    b_at = (f - 17) & 15
    live_a = (f >= 1) & (f < 273)
    live_b = (f >= 17) & (f < 273)
    high, low = [], []
    for t in range(2):
        for h in range(2):
            base = t * 32 + h * 16
            left = dot(q, onehot(live_a & (row == a_at + base))) + unit_a
            right = dot(q, onehot(live_b & (row == b_at + base))) + unit_b
            one, two = split(left * right * scale)
            high.append(one)
            low.append(two)
    out_lane = iota((16, 256), 1)
    first_head = (out_lane < 112) | (out_lane == 224) | (out_lane == 226)
    for i in range(8):
        phi = jnp.concatenate([x[i * 16 : (i + 1) * 16, 0:273] for x in high + low], axis=0)
        both_ref[:, 0:224] = state_ref[i]
        both_ref[:, 224:256] = norm_ref[i]
        both = dot(phi, both_ref[...])
        terms = both[0:64] + both[64:128]
        results = []
        for t in range(2):
            r = jnp.where(first_head, terms[t * 32 : t * 32 + 16], terms[t * 32 + 16 : t * 32 + 32])
            rough = r.astype(BF).astype(F32)
            results.append(jnp.where(out_lane >= 226, r - rough, r).astype(BF))
        slot = step * 8 + i
        owner = owner_ref[slot]

        @pl.when(owner != me)
        def _():
            send_ref[owner, :, 0:256] = results[0]
            send_ref[owner, :, 256:512] = results[1]

        @pl.when(owner == me)
        def _():
            own_ref[slot, :, 0:256] = results[0]
            own_ref[slot, :, 256:512] = results[1]


def kappa(s):
    return 1.0 + s + 0.5 * s * s


def tail_kernel(pos_ref, own_ref, rec_ref, tk_ref, tv_ref, len_ref, num_ref, den_ref):
    core = pos_ref[1]
    r, c = iota((256, 256), 0), iota((256, 256), 1)
    expand_q = onehot((r >= 224) & (r - 224 == lax.shift_right_logical(c, 7) * 16 + (c & 15)))
    r, c = iota((256, 128), 0), iota((256, 128), 1)
    sum_a = onehot(lax.shift_right_logical(r, 4) == c)
    pick_q = onehot((r >= 224) & (r - 224 == c))
    r, c = iota((128, 128), 0), iota((128, 128), 1)
    pick_k = onehot(iota((32, 128), 0) == iota((32, 128), 1))
    sum_new = onehot((r < 32) & (lax.shift_right_logical(r, 4) == c))
    r, c = iota((128, 1792), 0), iota((128, 1792), 1)
    expand_w = onehot((r < 16) & (c >= r * 112) & (c < (r + 1) * 112))
    r, c = iota((1792, 256), 0), iota((1792, 256), 1)
    sum_v = onehot(
        functools.reduce(
            jnp.logical_or,
            [(r - c == 112 * (7 * (k // 8) + k % 8)) & (c >= 112 * (k // 8)) & (c < 112 * (k // 8 + 1)) for k in range(16)],
        )
    )
    r, c = iota((128, 256), 0), iota((128, 256), 1)
    spread = onehot((r < 16) & (c < 224) & ((c >= 112) == (r >= 8)))
    spread_new = onehot((r < 2) & (c < 224) & ((c >= 112) == (r >= 1)))
    head_lane = iota((256, 128), 1)
    for e, ref in enumerate((own_ref, rec_ref)):
        half = core if e == 0 else 1 - core
        at = pl.multiple_of(half * 256, 256)
        keys = tk_ref[pl.ds(at, 256), :].astype(F32)
        live = (head_lane & 7) < len_ref[pl.ds(at, 256), :]
        live = live & (head_lane < 16)
        values = tv_ref[pl.ds(at, 256), :]
        new_keys = [dot(ref[t * 256 : (t + 1) * 256, 256:288], pick_k) for t in range(2)]
        for t in range(2):
            vq = ref[t * 256 : (t + 1) * 256, 0:256]
            one, two = split(dot(vq, expand_q) * keys)
            weight = kappa((dot(one, sum_a) + dot(two, sum_a)) * 0.25)
            weight = jnp.where(live, weight, 0.0)
            one, two = split(weight)
            den = dot(one, spread) + dot(two, spread)
            terms = dot(one, expand_w).astype(BF) * values
            num = dot(terms, sum_v)
            query = dot(vq, pick_q)
            for i in range(t + 1):
                one, two = split(query * new_keys[i])
                weight = kappa((dot(one, sum_new) + dot(two, sum_new)) * 0.25)
                one, two = split(weight)
                high = dot(one, spread_new)
                den = den + high + dot(two, spread_new)
                num = num + high * ref[i * 256 : (i + 1) * 256, 0:256].astype(F32)
            num_ref[e, t * 256 : (t + 1) * 256, :] = num
            den_ref[e, t * 256 : (t + 1) * 256, :] = den


def combine_kernel(pos_ref, g_ref, s_ref, num_ref, den_ref, rec_ref, own_ref, place_ref, out_ref, buf):
    core = pos_ref[1]
    me = pos_ref[2]
    for p in range(32):
        holder, slot = g_ref[p], s_ref[p]

        @pl.when(holder != me)
        def _():
            buf[p * 16 : (p + 1) * 16, :] = rec_ref[holder]

        @pl.when(holder == me)
        def _():
            buf[p * 16 : (p + 1) * 16, :] = own_ref[slot]

    r, c = iota((256, 256), 0), iota((256, 256), 1)
    spread = onehot((c < 224) & (((c < 112) & ((r == 224) | (r == 226))) | ((c >= 112) & ((r == 225) | (r == 227)))))
    lane = iota((256, 256), 1)
    for e in range(2):
        half = core if e == 0 else 1 - core
        at = pl.multiple_of(half * 256, 256)
        hot = onehot(iota((256, 512), 1) == place_ref[pl.ds(at, 256), :])
        prompt = dot(hot, buf[...])
        for t in range(2):
            part = prompt[:, t * 256 : (t + 1) * 256]
            den = den_ref[e, t * 256 : (t + 1) * 256, :] + dot(part.astype(BF), spread)
            num = num_ref[e, t * 256 : (t + 1) * 256, :] + part
            out = jnp.where(lane < 224, num / jnp.where(lane < 224, den, 1.0), 0.0)
            out = out.astype(BF)
            for part in range(2):
                out_ref[half * 2 + part, t * 128 : (t + 1) * 128, :] = out[part * 128 : (part + 1) * 128]


def out_kernel(pos_ref, own_ref, oth_ref, w0, w1, w3, far_1, far_3, first_ref, second_ref, far):
    y, core, col = pos_ref[0], pos_ref[1], pos_ref[3]
    acc = [None, None]
    far[0:2] = far_1[...]
    far[2:4] = far_3[...]
    for shift, w_ref in enumerate((w0, w1, far, w3)):
        j = lax.rem(y + 4 - shift, 4)
        for which, ref in enumerate((own_ref, oth_ref)):
            k = core if which == 0 else 1 - core
            heads = ref[j, :, 0:224]
            for e in range(2):
                part = dot(heads, w_ref[jnp.bitwise_xor(2 * e + k, col)])
                acc[e] = part if acc[e] is None else acc[e] + part
    even = lax.rem(y, 2) == 0
    first_ref[...] = jnp.where(even, acc[0], acc[1]).astype(BF)
    second_ref[...] = jnp.where(even, acc[1], acc[0]).astype(BF)


def body(tokens, w_query, w_key, w_value, w_out, cached_state, cached_norm, slot_prompt, prompt_of, tail_keys, tail_values, tail_length):
    y, core, col = lax.axis_index("y"), lax.axis_index("core"), lax.axis_index("col")
    me = lax.axis_index(("req", "col"))
    pos = jnp.stack([y, core, me, col]).astype(jnp.int32)
    def shifts(x, axis):
        return [x] + [lax.ppermute(x, axis, [(i, (i + s) % 4) for i in range(4)]) for s in range(1, 4)]

    blocks = shifts(tokens.reshape(256, 896), "y")
    blocks, w_out = lax.optimization_barrier((blocks, w_out))
    value_w = jnp.moveaxis(w_value.reshape(2, 448, 112), 0, 1).reshape(448, 224)
    mine = shifts(jnp.concatenate([value_w, w_query, w_key], axis=1), "col")
    pieces = []
    for s in range(4):
        perm = [(k * 4 + c, (c >> 1) * 4 + (s ^ (2 * (c & 1) + k))) for k in range(2) for c in range(4)]
        pieces.append(lax.ppermute(w_out, ("core", "col"), perm))
    blocks, mine = lax.optimization_barrier((blocks, mine))
    pieces = jnp.stack(pieces)

    def over_y(x, step):
        return lax.ppermute(x, "y", [(i, (i + step) % 4) for i in range(4)])

    owner = slot_prompt // 32
    slots = jnp.arange(32, dtype=jnp.int32)
    away = owner != me
    code = jnp.max(
        jnp.where((owner[None, :] == slots[:, None]) & away[None, :], (slots * 32 + slot_prompt % 32 + 1)[None, :], 0), axis=1
    )
    told = lax.all_to_all(code[:, None], ("req", "col"), split_axis=0, concat_axis=0, tiled=True)[:, 0]
    here = (slot_prompt[None, :] == (me * 32 + slots)[:, None])
    there = (told[None, :] > 0) & ((told[None, :] - 1) % 32 == slots[:, None])
    at_slot = jnp.max(jnp.where(here, slots[None, :], 0), axis=1)
    at_holder = jnp.where(jnp.any(here, axis=1), me, jnp.max(jnp.where(there, slots[None, :], 0), axis=1)).astype(jnp.int32)
    index = jnp.arange(512)
    rank = jnp.sum(((prompt_of[None, :] == prompt_of[:, None]) & (index[None, :] < index[:, None])).astype(jnp.int32), axis=1)
    place = (prompt_of - me * 32) * 16 + rank
    norms = jnp.concatenate([cached_norm, cached_norm, jnp.zeros((32, 273, 28), BF)], axis=2)
    states = jnp.transpose(cached_state[0].reshape(273, 224, 32), (2, 0, 1))

    held = call(order_kernel, jax.ShapeDtypeStruct((4, 256, 896), BF), 1, pos, *blocks)
    theirs = [lax.ppermute(w, "core", [(0, 1), (1, 0)]) for w in mine]
    held = lax.all_to_all(held, "col", split_axis=0, concat_axis=0, tiled=True)
    held, states, norms = lax.optimization_barrier((held, states, norms))
    shape = jax.ShapeDtypeStruct((512, 288), BF)
    own, oth = call(project_kernel, (shape, shape), 1, pos, held, *mine, *theirs, scratch=[pltpu.VMEM((512, 288), BF)])
    oth, pieces = lax.optimization_barrier((oth, pieces))
    out_w1, out_w3 = over_y(pieces, 1), over_y(pieces, 3)
    rec = lax.ppermute(oth, "core", [(0, 1), (1, 0)])

    shape = jax.ShapeDtypeStruct((32, 16, 128), BF)
    q_send, q_keep = call(
        group_kernel,
        (shape, shape),
        3,
        pos,
        at_holder,
        at_slot,
        own,
        rec,
        place.reshape(2, 1, 256),
        scratch=[pltpu.VMEM((512, 128), BF)],
    )
    q_rec = lax.all_to_all(q_send, ("req", "col"), split_axis=0, concat_axis=0, tiled=True)
    q_rec, out_w1, out_w3 = lax.optimization_barrier((q_rec, out_w1, out_w3))
    shape = jax.ShapeDtypeStruct((2, 512, 256), F32)
    num, den = call(tail_kernel, (shape, shape), 1, pos, own, rec, tail_keys, tail_values, tail_length[:, None])
    shape = jax.ShapeDtypeStruct((32, 16, 512), BF)
    whole = pl.BlockSpec((32, 16, 128), lambda i: (0, 0, 0))
    whole_out = pl.BlockSpec((32, 16, 512), lambda i: (0, 0, 0))
    r_send, r_keep = pl.pallas_call(
        slot_kernel,
        grid=(4,),
        out_shape=(pltpu.HBM(shape.shape, BF), pltpu.HBM(shape.shape, BF)),
        in_specs=[
            SM,
            SM,
            whole,
            whole,
            pl.BlockSpec((8, 273, 224), lambda i: (i, 0, 0)),
            pl.BlockSpec((8, 273, 32), lambda i: (i, 0, 0)),
        ],
        out_specs=(whole_out, whole_out),
        scratch_shapes=[pltpu.VMEM((128, 128), BF), pltpu.VMEM((273, 256), BF)],
        compiler_params=pltpu.CompilerParams(vmem_limit_bytes=VMEM_LIMIT),
    )(pos, owner, in_hbm(q_rec), in_hbm(q_keep), in_hbm(states), in_hbm(norms))
    r_send, far_1, far_3 = lax.optimization_barrier((r_send, out_w1[:2], out_w3[2:]))
    far_1, far_3 = over_y(far_1, 1), over_y(far_3, 3)
    r_rec = lax.all_to_all(r_send, ("req", "col"), split_axis=0, concat_axis=0, tiled=True)
    r_rec, far_1, far_3 = lax.optimization_barrier((r_rec, far_1, far_3))
    heads = call(
        combine_kernel,
        jax.ShapeDtypeStruct((4, 256, 256), BF),
        3,
        pos,
        at_holder,
        at_slot,
        num,
        den,
        r_rec,
        r_keep,
        place[:, None],
        scratch=[pltpu.VMEM((512, 512), BF)],
    )
    heads = lax.all_to_all(heads, "y", split_axis=0, concat_axis=0, tiled=True)
    heads_oth = lax.ppermute(heads, "core", [(0, 1), (1, 0)])
    shape = jax.ShapeDtypeStruct((256, 448), BF)
    mixed = call(out_kernel, (shape, shape), 1, pos, heads, heads_oth, pieces, out_w1, out_w3, far_1, far_3, scratch=[pltpu.VMEM((4, 224, 448), BF)])

    def at(y, core, col):
        return (y * 2 + core) * 4 + col

    got = []
    for s, part in enumerate(mixed):
        perm = [
            (at(j, k, b), at(b, j >> 1, 2 * k + (s ^ (j & 1)))) for b in range(4) for j in range(4) for k in range(2)
        ]
        got.append(lax.ppermute(part, ("y", "core", "col"), perm).reshape(2, 128, 448))
    odd = col % 2 == 1
    mixed = jnp.concatenate([jnp.where(odd, got[1], got[0]), jnp.where(odd, got[0], got[1])], axis=1)
    mixed = jnp.transpose(mixed, (1, 0, 2)).astype(F32)
    return (mixed + tokens.astype(F32)).astype(BF)


def solution(mesh):
    inner = Mesh(mesh.devices.reshape(8, 4, 2, 4), ("req", "y", "core", "col"))
    rows = ("y", "core")
    hold = ("req", "col")
    return jax.shard_map(
        body,
        mesh=inner,
        in_specs=(
            P(("req", "y", "core"), None, "col"),
            P("col", rows),
            P("col", rows),
            P(rows, "col"),
            P(rows, "col"),
            P(hold, None, rows),
            P(hold, None, rows),
            P(hold),
            P(hold),
            P(hold, rows),
            P(hold, rows),
            P(hold),
        ),
        out_specs=P(("req", "y", "core"), None, "col"),
        check_vma=False,
    )
```

```python
import functools

import jax
import jax.numpy as jnp
from jax import lax
from jax.experimental import pallas as pl
from jax.experimental.pallas import tpu as pltpu
from jax.sharding import Mesh, PartitionSpec as P

BF = jnp.bfloat16
F32 = jnp.float32
VMEM_LIMIT = 48 * 1024 * 1024
SM = pl.BlockSpec(memory_space=pltpu.SMEM)


def dot(a, b):
    return jnp.dot(a, b, preferred_element_type=F32)


def iota(shape, dim):
    return lax.broadcasted_iota(jnp.int32, shape, dim)


def onehot(cond):
    return jnp.where(cond, 1.0, 0.0).astype(BF)


def split(x):
    high = x.astype(BF)
    return high, (x - high.astype(F32)).astype(BF)


def in_hbm(x):
    return pltpu.with_memory_space_constraint(x, pltpu.HBM)


def call(kernel, out_shapes, n_smem, *args, scratch=()):
    def full(shape):
        zeros = (0,) * len(shape)
        return pl.BlockSpec(shape, lambda i: zeros)

    return pl.pallas_call(
        kernel,
        grid=(1,),
        out_shape=jax.tree.map(lambda x: pltpu.HBM(x.shape, x.dtype), out_shapes),
        in_specs=[SM] * n_smem + [full(x.shape) for x in args[n_smem:]],
        out_specs=jax.tree.map(lambda x: full(x.shape), out_shapes),
        scratch_shapes=scratch,
        compiler_params=pltpu.CompilerParams(vmem_limit_bytes=VMEM_LIMIT),
    )(*args[:n_smem], *[in_hbm(x) for x in args[n_smem:]])


def order_kernel(pos_ref, *refs):
    out_ref = refs[8]
    for shift in range(4):
        slot = lax.rem(pos_ref[0] + 4 - shift, 4)
        out_ref[slot, 0:128, :] = refs[2 * shift][...]
        out_ref[slot, 128:256, :] = refs[2 * shift + 1][...]


def project_kernel(pos_ref, t_ref, *refs):
    weights, own_ref, oth_ref, padded = refs[:8], refs[8], refs[9], refs[10]
    padded[0:64, :] = jnp.zeros((64, 288), BF)
    for which, out_ref in enumerate((own_ref, oth_ref)):
        first = second = None
        for shift in range(4):
            block = lax.rem(pos_ref[3] + 4 - shift, 4)
            w = weights[which * 4 + shift][...]
            padded[64:512, :] = w
            one = dot(t_ref[block, :, 0:448], w)
            two = dot(t_ref[block, :, 384:896], padded[...])
            first = one if first is None else first + one
            second = two if second is None else second + two
        out_ref[0:256, :] = first.astype(BF)
        out_ref[256:512, :] = second.astype(BF)


def group_kernel(pos_ref, g_ref, s_ref, own_ref, rec_ref, place_ref, send_ref, keep_ref, grouped):
    core = pos_ref[1]
    me = pos_ref[2]
    rows, cols = iota((256, 128), 0), iota((256, 128), 1)
    acc = None
    for e, ref in enumerate((own_ref, rec_ref)):
        half = core if e == 0 else 1 - core
        queries = None
        for t in range(2):
            pick = onehot((rows >= 224) & (cols == rows - 224 + 32 * t))
            part = dot(ref[t * 256 : (t + 1) * 256, 0:256], pick)
            queries = part if queries is None else queries + part
        hot = onehot(iota((512, 256), 0) == place_ref[half])
        part = dot(hot, queries.astype(BF))
        acc = part if acc is None else acc + part
    grouped[...] = acc.astype(BF)
    send_ref[...] = jnp.zeros_like(send_ref)
    keep_ref[...] = jnp.zeros_like(keep_ref)
    for p in range(32):
        holder, slot = g_ref[p], s_ref[p]

        @pl.when(holder != me)
        def _():
            send_ref[holder] = grouped[p * 16 : (p + 1) * 16, :]

        @pl.when(holder == me)
        def _():
            keep_ref[slot] = grouped[p * 16 : (p + 1) * 16, :]


def slot_kernel(pos_ref, owner_ref, rec_ref, keep_ref, state_ref, norm_ref, send_ref, own_ref, buf):
    me = pos_ref[2]
    step = pl.program_id(0)

    @pl.when(step == 0)
    def _():
        send_ref[...] = jnp.zeros_like(send_ref)
        own_ref[...] = jnp.zeros_like(own_ref)

    for i in range(8):
        slot = step * 8 + i
        owner = owner_ref[slot]

        @pl.when(owner != me)
        def _():
            buf[i * 16 : (i + 1) * 16, :] = rec_ref[owner]

        @pl.when(owner == me)
        def _():
            buf[i * 16 : (i + 1) * 16, :] = keep_ref[slot]

    q = buf[...]
    row, f = iota((128, 384), 0), iota((128, 384), 1)
    lane = iota((1, 384), 1)
    square, line = lane >= 17, (lane >= 1) & (lane < 17)
    unit_a = jnp.where(lane == 0, 1.0, 0.0)
    unit_b = jnp.where(lane < 17, 1.0, 0.0)
    scale = jnp.where(square, 0.5**0.5 / 4.0, jnp.where(line, 0.5, 1.0))
    scale = jnp.where(lane < 273, scale, 0.0)
    a_at = jnp.where(f >= 17, lax.shift_right_logical(f - 17, 4), f - 1)
    b_at = (f - 17) & 15
    live_a = (f >= 1) & (f < 273)
    live_b = (f >= 17) & (f < 273)
    r, c = iota((128, 16), 0), iota((128, 16), 1)
    den_lane = iota((128, 32), 1)
    phis, dens = [], []
    for t in range(2):
        tile = jnp.zeros((128, 32), F32)
        for h in range(2):
            base = t * 32 + h * 16
            left = dot(q, onehot(live_a & (row == a_at + base))) + unit_a
            right = dot(q, onehot(live_b & (row == b_at + base))) + unit_b
            phi = left * right * scale
            norm = dot(onehot(2 * lax.shift_right_logical(r, 4) + h == c), norm_ref[...])
            den = jnp.sum(phi * norm, axis=1, keepdims=True)
            rough = den.astype(BF).astype(F32)
            tile = jnp.where(den_lane == h, rough, jnp.where(den_lane == h + 2, den - rough, tile))
            phis.append(phi.astype(BF))
        dens.append(tile.astype(BF))
    first_head = iota((16, 224), 1) < 112
    for i in range(8):
        at = slice(i * 16, (i + 1) * 16)
        phi = jnp.concatenate([x[at, 0:273] for x in phis], axis=0)
        terms = dot(phi, state_ref[i])
        results = [
            jnp.where(first_head, terms[t * 32 : t * 32 + 16], terms[t * 32 + 16 : t * 32 + 32]).astype(BF) for t in range(2)
        ]
        slot = step * 8 + i
        owner = owner_ref[slot]

        @pl.when(owner != me)
        def _():
            for t in range(2):
                send_ref[owner, :, t * 256 : t * 256 + 224] = results[t]
                send_ref[owner, :, t * 256 + 224 : t * 256 + 256] = dens[t][at]

        @pl.when(owner == me)
        def _():
            for t in range(2):
                own_ref[slot, :, t * 256 : t * 256 + 224] = results[t]
                own_ref[slot, :, t * 256 + 224 : t * 256 + 256] = dens[t][at]


def kappa(s):
    return 1.0 + s + 0.5 * s * s


def tail_kernel(pos_ref, own_ref, rec_ref, tk_ref, tv_ref, len_ref, num_ref):
    core = pos_ref[1]
    r, c = iota((256, 256), 0), iota((256, 256), 1)
    expand_q = onehot((r >= 224) & (r - 224 == lax.shift_right_logical(c, 7) * 16 + (c & 15)))
    r, c = iota((256, 128), 0), iota((256, 128), 1)
    sum_a = onehot(lax.shift_right_logical(r, 4) == c)
    pick_q = onehot((r >= 224) & (r - 224 == c))
    r, c = iota((128, 128), 0), iota((128, 128), 1)
    pick_k = onehot(iota((32, 128), 0) == iota((32, 128), 1))
    sum_new = onehot((r < 32) & (lax.shift_right_logical(r, 4) == c))
    r, c = iota((128, 1792), 0), iota((128, 1792), 1)
    expand_w = onehot((r < 16) & (c >= r * 112) & (c < (r + 1) * 112))
    r, c = iota((1792, 256), 0), iota((1792, 256), 1)
    sum_v = onehot(
        functools.reduce(
            jnp.logical_or,
            [(r - c == 112 * (7 * (k // 8) + k % 8)) & (c >= 112 * (k // 8)) & (c < 112 * (k // 8 + 1)) for k in range(16)],
        )
    )
    r, c = iota((128, 256), 0), iota((128, 256), 1)
    den_at = onehot((r < 16) & (c == 224 + lax.shift_right_logical(r, 3)))
    den_new = onehot((r < 2) & (c == 224 + r))
    spread_new = onehot((r < 2) & (c < 224) & ((c >= 112) == (r >= 1)))
    head_lane = iota((256, 128), 1)
    for e, ref in enumerate((own_ref, rec_ref)):
        half = core if e == 0 else 1 - core
        at = pl.multiple_of(half * 256, 256)
        keys = tk_ref[pl.ds(at, 256), :].astype(F32)
        live = (head_lane & 7) < len_ref[pl.ds(at, 256), :]
        live = live & (head_lane < 16)
        values = tv_ref[pl.ds(at, 256), :]
        new_keys = [dot(ref[t * 256 : (t + 1) * 256, 256:288], pick_k) for t in range(2)]
        for t in range(2):
            vq = ref[t * 256 : (t + 1) * 256, 0:256]
            one, two = split(dot(vq, expand_q) * keys)
            weight = kappa((dot(one, sum_a) + dot(two, sum_a)) * 0.25)
            weight = jnp.where(live, weight, 0.0)
            one, two = split(weight)
            terms = dot(one, expand_w).astype(BF) * values
            num = dot(terms, sum_v) + (dot(one, den_at) + dot(two, den_at))
            query = dot(vq, pick_q)
            for i in range(t + 1):
                one, two = split(query * new_keys[i])
                weight = kappa((dot(one, sum_new) + dot(two, sum_new)) * 0.25)
                one, two = split(weight)
                num = num + dot(one, spread_new) * ref[i * 256 : (i + 1) * 256, 0:256].astype(F32)
                num = num + (dot(one, den_new) + dot(two, den_new))
            num_ref[e, t * 256 : (t + 1) * 256, :] = num


def combine_kernel(pos_ref, g_ref, s_ref, num_ref, rec_ref, own_ref, place_ref, out_ref, buf):
    core = pos_ref[1]
    me = pos_ref[2]
    for p in range(32):
        holder, slot = g_ref[p], s_ref[p]

        @pl.when(holder != me)
        def _():
            buf[p * 16 : (p + 1) * 16, :] = rec_ref[holder]

        @pl.when(holder == me)
        def _():
            buf[p * 16 : (p + 1) * 16, :] = own_ref[slot]

    r, c = iota((256, 256), 0), iota((256, 256), 1)
    spread = onehot((c < 224) & (((c < 112) & ((r == 224) | (r == 226))) | ((c >= 112) & ((r == 225) | (r == 227)))))
    lane = iota((256, 256), 1)
    for e in range(2):
        half = core if e == 0 else 1 - core
        at = pl.multiple_of(half * 256, 256)
        hot = onehot(iota((256, 512), 1) == place_ref[pl.ds(at, 256), :])
        prompt = dot(hot, buf[...])
        for t in range(2):
            num = num_ref[e, t * 256 : (t + 1) * 256, :] + prompt[:, t * 256 : (t + 1) * 256]
            one, two = split(num)
            den = dot(one, spread) + dot(two, spread)
            out = jnp.where(lane < 224, num / jnp.where(lane < 224, den, 1.0), 0.0)
            out = out.astype(BF)
            for part in range(2):
                out_ref[half * 2 + part, t * 128 : (t + 1) * 128, :] = out[part * 128 : (part + 1) * 128]


def out_kernel(pos_ref, own_ref, oth_ref, *refs):
    parts, first_ref, second_ref, weights = refs[:8], refs[8], refs[9], refs[10]
    y, core, col = pos_ref[0], pos_ref[1], pos_ref[3]
    acc = [None, None]
    for shift in range(4):
        weights[shift, 0:2] = parts[2 * shift][...]
        weights[shift, 2:4] = parts[2 * shift + 1][...]
        j = lax.rem(y + 4 - shift, 4)
        for which, ref in enumerate((own_ref, oth_ref)):
            k = core if which == 0 else 1 - core
            heads = ref[j, :, 0:224]
            for e in range(2):
                part = dot(heads, weights[shift, jnp.bitwise_xor(2 * e + k, col)])
                acc[e] = part if acc[e] is None else acc[e] + part
    even = lax.rem(y, 2) == 0
    first_ref[...] = jnp.where(even, acc[0], acc[1]).astype(BF)
    second_ref[...] = jnp.where(even, acc[1], acc[0]).astype(BF)


def body(tokens, w_query, w_key, w_value, w_out, cached_state, cached_norm, slot_prompt, prompt_of, tail_keys, tail_values, tail_length):
    y, core, col = lax.axis_index("y"), lax.axis_index("core"), lax.axis_index("col")
    me = lax.axis_index(("req", "col"))
    pos = jnp.stack([y, core, me, col]).astype(jnp.int32)
    def shifts(x, axis):
        return [x] + [lax.ppermute(x, axis, [(i, (i + s) % 4) for i in range(4)]) for s in range(1, 4)]

    def over_y(x, step):
        return lax.ppermute(x, "y", [(i, (i + step) % 4) for i in range(4)])

    top, low = tokens[:128].reshape(128, 896), tokens[128:].reshape(128, 896)
    top_1, low_3 = over_y(top, 1), over_y(low, 3)
    low_1, top_3 = over_y(low, 1), over_y(top, 3)
    top_1, low_3, w_out = lax.optimization_barrier((top_1, low_3, w_out))
    blocks = [top, low, top_1, low_1, over_y(top_1, 1), over_y(low_3, 3), top_3, low_3]
    value_w = jnp.moveaxis(w_value.reshape(2, 448, 112), 0, 1).reshape(448, 224)
    mine = shifts(jnp.concatenate([value_w, w_query, w_key], axis=1), "col")
    pieces = []
    for s in range(4):
        perm = [(k * 4 + c, (c >> 1) * 4 + (s ^ (2 * (c & 1) + k))) for k in range(2) for c in range(4)]
        pieces.append(lax.ppermute(w_out, ("core", "col"), perm))
    blocks, mine = lax.optimization_barrier((blocks, mine))
    pieces = [jnp.stack(pieces[:2]), jnp.stack(pieces[2:])]

    owner = slot_prompt // 32
    slots = jnp.arange(32, dtype=jnp.int32)
    away = owner != me
    code = jnp.max(
        jnp.where((owner[None, :] == slots[:, None]) & away[None, :], (slots * 32 + slot_prompt % 32 + 1)[None, :], 0), axis=1
    )
    told = lax.all_to_all(code[:, None], ("req", "col"), split_axis=0, concat_axis=0, tiled=True)[:, 0]
    here = (slot_prompt[None, :] == (me * 32 + slots)[:, None])
    there = (told[None, :] > 0) & ((told[None, :] - 1) % 32 == slots[:, None])
    at_slot = jnp.max(jnp.where(here, slots[None, :], 0), axis=1)
    at_holder = jnp.where(jnp.any(here, axis=1), me, jnp.max(jnp.where(there, slots[None, :], 0), axis=1)).astype(jnp.int32)
    index = jnp.arange(512)
    rank = jnp.sum(((prompt_of[None, :] == prompt_of[:, None]) & (index[None, :] < index[:, None])).astype(jnp.int32), axis=1)
    place = (prompt_of - me * 32) * 16 + rank
    norms = jnp.pad(jnp.transpose(cached_norm, (0, 2, 1)).reshape(64, 273), ((0, 0), (0, 111)))
    states = cached_state[0].reshape(273, 224, 32)

    held = call(order_kernel, jax.ShapeDtypeStruct((4, 256, 896), BF), 1, pos, *blocks)
    theirs = [lax.ppermute(w, "core", [(0, 1), (1, 0)]) for w in mine]
    held = lax.all_to_all(held, "col", split_axis=0, concat_axis=0, tiled=True)
    held, states, norms = lax.optimization_barrier((held, states, norms))
    states = jnp.transpose(states, (2, 0, 1))
    shape = jax.ShapeDtypeStruct((512, 288), BF)
    own, oth = call(project_kernel, (shape, shape), 1, pos, held, *mine, *theirs, scratch=[pltpu.VMEM((512, 288), BF)])
    rec = lax.ppermute(oth, "core", [(0, 1), (1, 0)])
    rec, pieces = lax.optimization_barrier((rec, pieces))
    out_w = [over_y(x, step) for step in (1, 3) for x in pieces]

    shape = jax.ShapeDtypeStruct((32, 16, 128), BF)
    q_send, q_keep = call(
        group_kernel,
        (shape, shape),
        3,
        pos,
        at_holder,
        at_slot,
        own,
        rec,
        place.reshape(2, 1, 256),
        scratch=[pltpu.VMEM((512, 128), BF)],
    )
    q_rec = lax.all_to_all(q_send, ("req", "col"), split_axis=0, concat_axis=0, tiled=True)
    q_rec, out_w = lax.optimization_barrier((q_rec, out_w))
    shape = jax.ShapeDtypeStruct((2, 512, 256), F32)
    num = call(tail_kernel, shape, 1, pos, own, rec, tail_keys, tail_values, tail_length[:, None])
    shape = jax.ShapeDtypeStruct((32, 16, 512), BF)
    whole = pl.BlockSpec((32, 16, 128), lambda i: (0, 0, 0))
    whole_out = pl.BlockSpec((32, 16, 512), lambda i: (0, 0, 0))
    r_send, r_keep = pl.pallas_call(
        slot_kernel,
        grid=(4,),
        out_shape=(pltpu.HBM(shape.shape, BF), pltpu.HBM(shape.shape, BF)),
        in_specs=[
            SM,
            SM,
            whole,
            whole,
            pl.BlockSpec((8, 273, 224), lambda i: (i, 0, 0)),
            pl.BlockSpec((16, 384), lambda i: (i, 0)),
        ],
        out_specs=(whole_out, whole_out),
        scratch_shapes=[pltpu.VMEM((128, 128), BF)],
        compiler_params=pltpu.CompilerParams(vmem_limit_bytes=VMEM_LIMIT),
    )(pos, owner, in_hbm(q_rec), in_hbm(q_keep), in_hbm(states), in_hbm(norms))
    r_send, far_1, far_3 = lax.optimization_barrier((r_send, out_w[0], out_w[3]))
    far_1, far_3 = over_y(far_1, 1), over_y(far_3, 3)
    r_rec = lax.all_to_all(r_send, ("req", "col"), split_axis=0, concat_axis=0, tiled=True)
    r_rec, far_1, far_3 = lax.optimization_barrier((r_rec, far_1, far_3))
    heads = call(
        combine_kernel,
        jax.ShapeDtypeStruct((4, 256, 256), BF),
        3,
        pos,
        at_holder,
        at_slot,
        num,
        r_rec,
        r_keep,
        place[:, None],
        scratch=[pltpu.VMEM((512, 512), BF)],
    )
    heads = lax.all_to_all(heads, "y", split_axis=0, concat_axis=0, tiled=True)
    heads_oth = lax.ppermute(heads, "core", [(0, 1), (1, 0)])
    shape = jax.ShapeDtypeStruct((256, 448), BF)
    mixed = call(out_kernel, (shape, shape), 1, pos, heads, heads_oth, *pieces, out_w[0], out_w[1], far_1, far_3, out_w[2], out_w[3], scratch=[pltpu.VMEM((4, 4, 224, 448), BF)])

    def at(y, core, col):
        return (y * 2 + core) * 4 + col

    got = []
    for s, part in enumerate(mixed):
        perm = [
            (at(j, k, b), at(b, j >> 1, 2 * k + (s ^ (j & 1)))) for b in range(4) for j in range(4) for k in range(2)
        ]
        got.append(lax.ppermute(part, ("y", "core", "col"), perm).reshape(2, 128, 448))
    odd = col % 2 == 1
    mixed = jnp.concatenate([jnp.where(odd, got[1], got[0]), jnp.where(odd, got[0], got[1])], axis=1)
    mixed = jnp.transpose(mixed, (1, 0, 2)).astype(F32)
    return (mixed + tokens.astype(F32)).astype(BF)


def solution(mesh):
    inner = Mesh(mesh.devices.reshape(8, 4, 2, 4), ("req", "y", "core", "col"))
    rows = ("y", "core")
    hold = ("req", "col")
    return jax.shard_map(
        body,
        mesh=inner,
        in_specs=(
            P(("req", "y", "core"), None, "col"),
            P("col", rows),
            P("col", rows),
            P(rows, "col"),
            P(rows, "col"),
            P(hold, None, rows),
            P(hold, None, rows),
            P(hold),
            P(hold),
            P(hold, rows),
            P(hold, rows),
            P(hold),
        ),
        out_specs=P(("req", "y", "core"), None, "col"),
        check_vma=False,
    )
```

```python
import functools

import jax
import jax.numpy as jnp
from jax import lax
from jax.experimental import pallas as pl
from jax.experimental.pallas import tpu as pltpu
from jax.sharding import Mesh, PartitionSpec as P

BF = jnp.bfloat16
F32 = jnp.float32
VMEM_LIMIT = 48 * 1024 * 1024
SM = pl.BlockSpec(memory_space=pltpu.SMEM)


def dot(a, b):
    return jnp.dot(a, b, preferred_element_type=F32)


def iota(shape, dim):
    return lax.broadcasted_iota(jnp.int32, shape, dim)


def onehot(cond):
    return jnp.where(cond, 1.0, 0.0).astype(BF)


def split(x):
    high = x.astype(BF)
    return high, (x - high.astype(F32)).astype(BF)


def in_hbm(x):
    return pltpu.with_memory_space_constraint(x, pltpu.HBM)


def call(kernel, out_shapes, n_smem, *args, scratch=(), free=()):
    def full(shape):
        zeros = (0,) * len(shape)
        return pl.BlockSpec(shape, lambda i: zeros)

    return pl.pallas_call(
        kernel,
        grid=(1,),
        out_shape=jax.tree.map(lambda x: pltpu.HBM(x.shape, x.dtype), out_shapes),
        in_specs=[SM] * n_smem + [full(x.shape) for x in args[n_smem:]],
        out_specs=jax.tree.map(lambda x: full(x.shape), out_shapes),
        scratch_shapes=scratch,
        compiler_params=pltpu.CompilerParams(vmem_limit_bytes=VMEM_LIMIT),
    )(*args[:n_smem], *[x if i + n_smem in free else in_hbm(x) for i, x in enumerate(args[n_smem:])])


def project_kernel(pos_ref, *refs):
    blocks, mine_ref, theirs_ref, out_ref, first, second = refs[:8], refs[8], refs[9], refs[10], refs[11], refs[12]
    core = pos_ref[1]
    one = jnp.where(core == 0, mine_ref[...], theirs_ref[...])
    two = jnp.where(core == 0, theirs_ref[...], mine_ref[...])
    first[:, 0:256] = one[:, 0:256]
    first[:, 256:512] = two[:, 0:256]
    first[:, 512:640] = jnp.concatenate([one[:, 256:288], two[:, 256:288], jnp.zeros((448, 64), BF)], axis=1)
    second[0:64, :] = jnp.zeros((64, 640), BF)
    second[64:512, 0:128] = jnp.concatenate([jnp.zeros((448, 64), BF), one[:, 256:288], two[:, 256:288]], axis=1)
    second[64:512, 128:384] = one[:, 0:256]
    second[64:512, 384:640] = two[:, 0:256]
    for shift in range(4):
        slot = lax.rem(pos_ref[0] + 4 - shift, 4)
        for part in range(2):
            block = blocks[2 * shift + part]
            a = dot(block[:, 0:448], first[...])
            b = dot(block[:, 384:896], second[...])
            at = slice(part * 128, (part + 1) * 128)
            out_ref[slot, at, 0:512] = a[:, 0:512].astype(BF)
            out_ref[slot, at, 512:640] = (a[:, 512:640] + b[:, 0:128]).astype(BF)
            out_ref[slot, at, 640:1152] = b[:, 128:640].astype(BF)


def sum_kernel(pos_ref, p_ref, own_ref, oth_ref):
    core = pos_ref[1]

    def total(lo, hi):
        acc = p_ref[0, :, lo:hi].astype(F32)
        for i in range(1, 4):
            acc = acc + p_ref[i, :, lo:hi].astype(F32)
        return acc.astype(BF)

    keys = total(512, 640)
    for t in range(2):
        at = slice(t * 256, (t + 1) * 256)
        one, two = total(t * 640, t * 640 + 256), total(t * 640 + 256, t * 640 + 512)
        own_ref[at, 0:256] = jnp.where(core == 0, one, two)
        oth_ref[at, 0:256] = jnp.where(core == 0, two, one)
        one, two = keys[:, t * 64 : t * 64 + 32], keys[:, t * 64 + 32 : t * 64 + 64]
        own_ref[at, 256:288] = jnp.where(core == 0, one, two)
        oth_ref[at, 256:288] = jnp.where(core == 0, two, one)


def group_kernel(pos_ref, g_ref, s_ref, own_ref, rec_ref, place_ref, send_ref, keep_ref, grouped):
    core = pos_ref[1]
    me = pos_ref[2]
    rows, cols = iota((256, 128), 0), iota((256, 128), 1)
    acc = None
    for e, ref in enumerate((own_ref, rec_ref)):
        half = core if e == 0 else 1 - core
        queries = None
        for t in range(2):
            pick = onehot((rows >= 224) & (cols == rows - 224 + 32 * t))
            part = dot(ref[t * 256 : (t + 1) * 256, 0:256], pick)
            queries = part if queries is None else queries + part
        hot = onehot(iota((512, 256), 0) == place_ref[half])
        part = dot(hot, queries.astype(BF))
        acc = part if acc is None else acc + part
    grouped[...] = acc.astype(BF)
    send_ref[...] = jnp.zeros_like(send_ref)
    keep_ref[...] = jnp.zeros_like(keep_ref)
    for p in range(32):
        holder, slot = g_ref[p], s_ref[p]

        @pl.when(holder != me)
        def _():
            send_ref[holder] = grouped[p * 16 : (p + 1) * 16, :]

        @pl.when(holder == me)
        def _():
            keep_ref[slot] = grouped[p * 16 : (p + 1) * 16, :]


def slot_kernel(pos_ref, owner_ref, rec_ref, keep_ref, state_ref, norm_ref, send_ref, own_ref, buf):
    me = pos_ref[2]
    step = pl.program_id(0)

    @pl.when(step == 0)
    def _():
        send_ref[...] = jnp.zeros_like(send_ref)
        own_ref[...] = jnp.zeros_like(own_ref)

    for i in range(8):
        slot = step * 8 + i
        owner = owner_ref[slot]

        @pl.when(owner != me)
        def _():
            buf[i * 16 : (i + 1) * 16, :] = rec_ref[owner]

        @pl.when(owner == me)
        def _():
            buf[i * 16 : (i + 1) * 16, :] = keep_ref[slot]

    q = buf[...]
    row, f = iota((128, 384), 0), iota((128, 384), 1)
    lane = iota((1, 384), 1)
    square, line = lane >= 17, (lane >= 1) & (lane < 17)
    unit_a = jnp.where(lane == 0, 1.0, 0.0)
    unit_b = jnp.where(lane < 17, 1.0, 0.0)
    scale = jnp.where(square, 0.5**0.5 / 4.0, jnp.where(line, 0.5, 1.0))
    scale = jnp.where(lane < 273, scale, 0.0)
    a_at = jnp.where(f >= 17, lax.shift_right_logical(f - 17, 4), f - 1)
    b_at = (f - 17) & 15
    live_a = (f >= 1) & (f < 273)
    live_b = (f >= 17) & (f < 273)
    r, c = iota((128, 16), 0), iota((128, 16), 1)
    den_lane = iota((128, 32), 1)
    phis, dens = [], []
    for t in range(2):
        tile = jnp.zeros((128, 32), F32)
        for h in range(2):
            base = t * 32 + h * 16
            left = dot(q, onehot(live_a & (row == a_at + base))) + unit_a
            right = dot(q, onehot(live_b & (row == b_at + base))) + unit_b
            phi = left * right * scale
            norm = dot(onehot(2 * lax.shift_right_logical(r, 4) + h == c), norm_ref[...])
            den = jnp.sum(phi * norm, axis=1, keepdims=True)
            rough = den.astype(BF).astype(F32)
            tile = jnp.where(den_lane == h, rough, jnp.where(den_lane == h + 2, den - rough, tile))
            phis.append(phi.astype(BF))
        dens.append(tile.astype(BF))
    first_head = iota((16, 224), 1) < 112
    for i in range(8):
        at = slice(i * 16, (i + 1) * 16)
        phi = jnp.concatenate([x[at, 0:273] for x in phis], axis=0)
        terms = dot(phi, state_ref[i])
        results = [
            jnp.where(first_head, terms[t * 32 : t * 32 + 16], terms[t * 32 + 16 : t * 32 + 32]).astype(BF) for t in range(2)
        ]
        slot = step * 8 + i
        owner = owner_ref[slot]

        @pl.when(owner != me)
        def _():
            for t in range(2):
                send_ref[owner, :, t * 256 : t * 256 + 224] = results[t]
                send_ref[owner, :, t * 256 + 224 : t * 256 + 256] = dens[t][at]

        @pl.when(owner == me)
        def _():
            for t in range(2):
                own_ref[slot, :, t * 256 : t * 256 + 224] = results[t]
                own_ref[slot, :, t * 256 + 224 : t * 256 + 256] = dens[t][at]


def kappa(s):
    return 1.0 + s + 0.5 * s * s


def tail_kernel(pos_ref, own_ref, rec_ref, tk_ref, tv_ref, len_ref, num_ref):
    core = pos_ref[1]
    r, c = iota((256, 256), 0), iota((256, 256), 1)
    expand_q = onehot((r >= 224) & (r - 224 == lax.shift_right_logical(c, 7) * 16 + (c & 15)))
    r, c = iota((256, 128), 0), iota((256, 128), 1)
    sum_a = onehot(lax.shift_right_logical(r, 4) == c)
    pick_q = onehot((r >= 224) & (r - 224 == c))
    r, c = iota((128, 128), 0), iota((128, 128), 1)
    pick_k = onehot(iota((32, 128), 0) == iota((32, 128), 1))
    sum_new = onehot((r < 32) & (lax.shift_right_logical(r, 4) == c))
    r, c = iota((128, 1792), 0), iota((128, 1792), 1)
    expand_w = onehot((r < 16) & (c >= r * 112) & (c < (r + 1) * 112))
    r, c = iota((1792, 256), 0), iota((1792, 256), 1)
    sum_v = onehot(
        functools.reduce(
            jnp.logical_or,
            [(r - c == 112 * (7 * (k // 8) + k % 8)) & (c >= 112 * (k // 8)) & (c < 112 * (k // 8 + 1)) for k in range(16)],
        )
    )
    r, c = iota((128, 256), 0), iota((128, 256), 1)
    den_at = onehot((r < 16) & (c == 224 + lax.shift_right_logical(r, 3)))
    den_new = onehot((r < 2) & (c == 224 + r))
    spread_new = onehot((r < 2) & (c < 224) & ((c >= 112) == (r >= 1)))
    head_lane = iota((256, 128), 1)
    for e, ref in enumerate((own_ref, rec_ref)):
        half = core if e == 0 else 1 - core
        at = pl.multiple_of(half * 256, 256)
        keys = tk_ref[pl.ds(at, 256), :].astype(F32)
        live = (head_lane & 7) < len_ref[pl.ds(at, 256), :]
        live = live & (head_lane < 16)
        values = tv_ref[pl.ds(at, 256), :]
        new_keys = [dot(ref[t * 256 : (t + 1) * 256, 256:288], pick_k) for t in range(2)]
        for t in range(2):
            vq = ref[t * 256 : (t + 1) * 256, 0:256]
            one, two = split(dot(vq, expand_q) * keys)
            weight = kappa((dot(one, sum_a) + dot(two, sum_a)) * 0.25)
            weight = jnp.where(live, weight, 0.0)
            one, two = split(weight)
            terms = dot(one, expand_w).astype(BF) * values
            num = dot(terms, sum_v) + (dot(one, den_at) + dot(two, den_at))
            query = dot(vq, pick_q)
            for i in range(t + 1):
                one, two = split(query * new_keys[i])
                weight = kappa((dot(one, sum_new) + dot(two, sum_new)) * 0.25)
                one, two = split(weight)
                num = num + dot(one, spread_new) * ref[i * 256 : (i + 1) * 256, 0:256].astype(F32)
                num = num + (dot(one, den_new) + dot(two, den_new))
            num_ref[e, t * 256 : (t + 1) * 256, :] = num


def combine_kernel(pos_ref, g_ref, s_ref, num_ref, rec_ref, own_ref, place_ref, out_ref, buf):
    core = pos_ref[1]
    me = pos_ref[2]
    for p in range(32):
        holder, slot = g_ref[p], s_ref[p]

        @pl.when(holder != me)
        def _():
            buf[p * 16 : (p + 1) * 16, :] = rec_ref[holder]

        @pl.when(holder == me)
        def _():
            buf[p * 16 : (p + 1) * 16, :] = own_ref[slot]

    r, c = iota((256, 256), 0), iota((256, 256), 1)
    spread = onehot((c < 224) & (((c < 112) & ((r == 224) | (r == 226))) | ((c >= 112) & ((r == 225) | (r == 227)))))
    lane = iota((256, 256), 1)
    for e in range(2):
        half = core if e == 0 else 1 - core
        at = pl.multiple_of(half * 256, 256)
        hot = onehot(iota((256, 512), 1) == place_ref[pl.ds(at, 256), :])
        prompt = dot(hot, buf[...])
        for t in range(2):
            num = num_ref[e, t * 256 : (t + 1) * 256, :] + prompt[:, t * 256 : (t + 1) * 256]
            one, two = split(num)
            den = dot(one, spread) + dot(two, spread)
            out = jnp.where(lane < 224, num / jnp.where(lane < 224, den, 1.0), 0.0)
            out = out.astype(BF)
            for part in range(2):
                out_ref[half * 2 + part, t * 128 : (t + 1) * 128, :] = out[part * 128 : (part + 1) * 128]


def out_kernel(pos_ref, own_ref, oth_ref, *refs):
    parts, first_ref, second_ref = refs[:8], refs[8], refs[9]
    y, core, col = pos_ref[0], pos_ref[1], pos_ref[3]
    acc = [None, None]
    for shift in range(4):
        j = lax.rem(y + 4 - shift, 4)
        for which, ref in enumerate((own_ref, oth_ref)):
            k = core if which == 0 else 1 - core
            heads = ref[j, :, 0:224]
            for e in range(2):
                part = dot(heads, parts[2 * shift + e][jnp.bitwise_xor(k, lax.rem(col, 2))])
                acc[e] = part if acc[e] is None else acc[e] + part
    same = lax.rem(y, 2) == lax.div(col, 2)
    first_ref[...] = jnp.where(same, acc[0], acc[1]).astype(BF)
    second_ref[...] = jnp.where(same, acc[1], acc[0]).astype(BF)


def body(tokens, w_query, w_key, w_value, w_out, cached_state, cached_norm, slot_prompt, prompt_of, tail_keys, tail_values, tail_length):
    y, core, col = lax.axis_index("y"), lax.axis_index("core"), lax.axis_index("col")
    me = lax.axis_index(("req", "col"))
    pos = jnp.stack([y, core, me, col]).astype(jnp.int32)
    def over_y(x, step):
        return lax.ppermute(x, "y", [(i, (i + step) % 4) for i in range(4)])

    top, low = tokens[:128].reshape(128, 896), tokens[128:].reshape(128, 896)
    top_1, low_3 = over_y(top, 1), over_y(low, 3)
    low_1, top_3 = over_y(low, 1), over_y(top, 3)
    top_1, low_3, w_out = lax.optimization_barrier((top_1, low_3, w_out))
    blocks = [top, low, top_1, low_1, over_y(top_1, 1), over_y(low_3, 3), top_3, low_3]
    value_w = jnp.moveaxis(w_value.reshape(2, 448, 112), 0, 1).reshape(448, 224)
    mine = jnp.concatenate([value_w, w_query, w_key], axis=1)
    theirs = lax.ppermute(mine, "core", [(0, 1), (1, 0)])
    pieces = []
    for s in range(4):
        perm = [(k * 4 + c, (c >> 1) * 4 + (s ^ (2 * (c & 1) + k))) for k in range(2) for c in range(4)]
        pieces.append(lax.ppermute(w_out, ("core", "col"), perm))
    pieces = [jnp.stack(pieces[:2]), jnp.stack(pieces[2:])]

    owner = slot_prompt // 32
    slots = jnp.arange(32, dtype=jnp.int32)
    away = owner != me
    code = jnp.max(
        jnp.where((owner[None, :] == slots[:, None]) & away[None, :], (slots * 32 + slot_prompt % 32 + 1)[None, :], 0), axis=1
    )
    told = lax.all_to_all(code[:, None], ("req", "col"), split_axis=0, concat_axis=0, tiled=True)[:, 0]
    here = (slot_prompt[None, :] == (me * 32 + slots)[:, None])
    there = (told[None, :] > 0) & ((told[None, :] - 1) % 32 == slots[:, None])
    at_slot = jnp.max(jnp.where(here, slots[None, :], 0), axis=1)
    at_holder = jnp.where(jnp.any(here, axis=1), me, jnp.max(jnp.where(there, slots[None, :], 0), axis=1)).astype(jnp.int32)
    index = jnp.arange(512)
    rank = jnp.sum(((prompt_of[None, :] == prompt_of[:, None]) & (index[None, :] < index[:, None])).astype(jnp.int32), axis=1)
    place = (prompt_of - me * 32) * 16 + rank
    norms = jnp.pad(jnp.transpose(cached_norm, (0, 2, 1)).reshape(64, 273), ((0, 0), (0, 111)))
    states = cached_state[0].reshape(273, 224, 32)

    partial = call(
        project_kernel,
        jax.ShapeDtypeStruct((4, 256, 1152), BF),
        1,
        pos,
        *blocks,
        mine,
        theirs,
        scratch=[pltpu.VMEM((448, 640), BF), pltpu.VMEM((512, 640), BF)],
        free=range(1, 11),
    )
    partial = lax.all_to_all(partial, "col", split_axis=0, concat_axis=0, tiled=True)
    states = jnp.transpose(states, (2, 0, 1))
    partial, states, norms = lax.optimization_barrier((partial, states, norms))
    shape = jax.ShapeDtypeStruct((512, 288), BF)
    own, oth = call(sum_kernel, (shape, shape), 1, pos, partial, free=(1,))
    rec = lax.ppermute(oth, "core", [(0, 1), (1, 0)])

    shape = jax.ShapeDtypeStruct((32, 16, 128), BF)
    q_send, q_keep = call(
        group_kernel,
        (shape, shape),
        3,
        pos,
        at_holder,
        at_slot,
        own,
        rec,
        place.reshape(2, 1, 256),
        scratch=[pltpu.VMEM((512, 128), BF)],
        free=(3, 4),
    )
    q_send, pieces = lax.optimization_barrier((q_send, pieces))
    out_w = [over_y(x, step) for step in (1, 3) for x in pieces]
    q_rec = lax.all_to_all(q_send, ("req", "col"), split_axis=0, concat_axis=0, tiled=True)
    shape = jax.ShapeDtypeStruct((2, 512, 256), F32)
    num = call(tail_kernel, shape, 1, pos, own, rec, tail_keys, tail_values, tail_length[:, None])
    q_rec, num = lax.optimization_barrier((q_rec, num))
    shape = jax.ShapeDtypeStruct((32, 16, 512), BF)
    whole = pl.BlockSpec((32, 16, 128), lambda i: (0, 0, 0))
    whole_out = pl.BlockSpec((32, 16, 512), lambda i: (0, 0, 0))
    r_send, r_keep = pl.pallas_call(
        slot_kernel,
        grid=(4,),
        out_shape=(pltpu.HBM(shape.shape, BF), pltpu.HBM(shape.shape, BF)),
        in_specs=[
            SM,
            SM,
            whole,
            whole,
            pl.BlockSpec((8, 273, 224), lambda i: (i, 0, 0)),
            pl.BlockSpec((16, 384), lambda i: (i, 0)),
        ],
        out_specs=(whole_out, whole_out),
        scratch_shapes=[pltpu.VMEM((128, 128), BF)],
        compiler_params=pltpu.CompilerParams(vmem_limit_bytes=VMEM_LIMIT),
    )(pos, owner, in_hbm(q_rec), in_hbm(q_keep), in_hbm(states), in_hbm(norms))
    r_send, out_w = lax.optimization_barrier((r_send, out_w))
    far_1, far_3 = over_y(out_w[0], 1), over_y(out_w[3], 3)
    r_rec = lax.all_to_all(r_send, ("req", "col"), split_axis=0, concat_axis=0, tiled=True)
    r_rec, far_1, far_3 = lax.optimization_barrier((r_rec, far_1, far_3))
    heads = call(
        combine_kernel,
        jax.ShapeDtypeStruct((4, 256, 256), BF),
        3,
        pos,
        at_holder,
        at_slot,
        num,
        r_rec,
        r_keep,
        place[:, None],
        scratch=[pltpu.VMEM((512, 512), BF)],
        free=(4,),
    )
    heads = lax.all_to_all(heads, "y", split_axis=0, concat_axis=0, tiled=True)
    heads_oth = lax.ppermute(heads, "core", [(0, 1), (1, 0)])
    shape = jax.ShapeDtypeStruct((256, 448), BF)
    mixed = call(out_kernel, (shape, shape), 1, pos, heads, heads_oth, *pieces, out_w[0], out_w[1], far_1, far_3, out_w[2], out_w[3], free=(1, 2))

    def at(y, core, col):
        return (y * 2 + core) * 4 + col

    got = []
    for s, part in enumerate(mixed):
        perm = [
            (at(j, k, b), at(b, j >> 1, 2 * k + (s ^ (j & 1)))) for b in range(4) for j in range(4) for k in range(2)
        ]
        got.append(lax.ppermute(part, ("y", "core", "col"), perm).reshape(2, 128, 448))
    odd = col % 2 == 1
    mixed = jnp.concatenate([jnp.where(odd, got[1], got[0]), jnp.where(odd, got[0], got[1])], axis=1)
    mixed = jnp.transpose(mixed, (1, 0, 2)).astype(F32)
    return (mixed + tokens.astype(F32)).astype(BF)


def solution(mesh):
    inner = Mesh(mesh.devices.reshape(8, 4, 2, 4), ("req", "y", "core", "col"))
    rows = ("y", "core")
    hold = ("req", "col")
    return jax.shard_map(
        body,
        mesh=inner,
        in_specs=(
            P(("req", "y", "core"), None, "col"),
            P("col", rows),
            P("col", rows),
            P(rows, "col"),
            P(rows, "col"),
            P(hold, None, rows),
            P(hold, None, rows),
            P(hold),
            P(hold),
            P(hold, rows),
            P(hold, rows),
            P(hold),
        ),
        out_specs=P(("req", "y", "core"), None, "col"),
        check_vma=False,
    )
```

```python
import functools

import jax
import jax.numpy as jnp
from jax import lax
from jax.experimental import pallas as pl
from jax.experimental.pallas import tpu as pltpu
from jax.sharding import Mesh, PartitionSpec as P

BF = jnp.bfloat16
F32 = jnp.float32
VMEM_LIMIT = 48 * 1024 * 1024
SM = pl.BlockSpec(memory_space=pltpu.SMEM)


def dot(a, b):
    return jnp.dot(a, b, preferred_element_type=F32)


def iota(shape, dim):
    return lax.broadcasted_iota(jnp.int32, shape, dim)


def onehot(cond):
    return jnp.where(cond, 1.0, 0.0).astype(BF)


def split(x):
    high = x.astype(BF)
    return high, (x - high.astype(F32)).astype(BF)


def in_hbm(x):
    return pltpu.with_memory_space_constraint(x, pltpu.HBM)


def call(kernel, out_shapes, n_smem, *args, scratch=(), free=()):
    def full(shape):
        zeros = (0,) * len(shape)
        return pl.BlockSpec(shape, lambda i: zeros)

    return pl.pallas_call(
        kernel,
        grid=(1,),
        out_shape=jax.tree.map(lambda x: pltpu.HBM(x.shape, x.dtype), out_shapes),
        in_specs=[SM] * n_smem + [full(x.shape) for x in args[n_smem:]],
        out_specs=jax.tree.map(lambda x: full(x.shape), out_shapes),
        scratch_shapes=scratch,
        compiler_params=pltpu.CompilerParams(vmem_limit_bytes=VMEM_LIMIT),
    )(*args[:n_smem], *[x if i + n_smem in free else in_hbm(x) for i, x in enumerate(args[n_smem:])])


def project_kernel(pos_ref, *refs):
    blocks, mine_ref, theirs_ref, out_ref, first, second = refs[:8], refs[8], refs[9], refs[10], refs[11], refs[12]
    core = pos_ref[1]
    one = jnp.where(core == 0, mine_ref[...], theirs_ref[...])
    two = jnp.where(core == 0, theirs_ref[...], mine_ref[...])
    first[:, 0:256] = one[:, 0:256]
    first[:, 256:512] = two[:, 0:256]
    first[:, 512:640] = jnp.concatenate([one[:, 256:288], two[:, 256:288], jnp.zeros((448, 64), BF)], axis=1)
    second[0:64, :] = jnp.zeros((64, 640), BF)
    second[64:512, 0:128] = jnp.concatenate([jnp.zeros((448, 64), BF), one[:, 256:288], two[:, 256:288]], axis=1)
    second[64:512, 128:384] = one[:, 0:256]
    second[64:512, 384:640] = two[:, 0:256]
    for shift in range(4):
        slot = lax.rem(pos_ref[0] + 4 - shift, 4)
        for part in range(2):
            block = blocks[2 * shift + part]
            a = dot(block[:, 0:448], first[...])
            b = dot(block[:, 384:896], second[...])
            at = slice(part * 128, (part + 1) * 128)
            out_ref[slot, at, 0:512] = a[:, 0:512].astype(BF)
            out_ref[slot, at, 512:640] = (a[:, 512:640] + b[:, 0:128]).astype(BF)
            out_ref[slot, at, 640:1152] = b[:, 128:640].astype(BF)


def sum_kernel(pos_ref, p_ref, own_ref, oth_ref):
    core = pos_ref[1]

    def total(lo, hi):
        acc = p_ref[0, :, lo:hi].astype(F32)
        for i in range(1, 4):
            acc = acc + p_ref[i, :, lo:hi].astype(F32)
        return acc.astype(BF)

    keys = total(512, 640)
    for t in range(2):
        at = slice(t * 256, (t + 1) * 256)
        one, two = total(t * 640, t * 640 + 256), total(t * 640 + 256, t * 640 + 512)
        own_ref[at, 0:256] = jnp.where(core == 0, one, two)
        oth_ref[at, 0:256] = jnp.where(core == 0, two, one)
        one, two = keys[:, t * 64 : t * 64 + 32], keys[:, t * 64 + 32 : t * 64 + 64]
        own_ref[at, 256:288] = jnp.where(core == 0, one, two)
        oth_ref[at, 256:288] = jnp.where(core == 0, two, one)


def group_kernel(pos_ref, g_ref, s_ref, own_ref, rec_ref, place_ref, send_ref, keep_ref, grouped):
    core = pos_ref[1]
    me = pos_ref[2]
    rows, cols = iota((256, 128), 0), iota((256, 128), 1)
    acc = None
    for e, ref in enumerate((own_ref, rec_ref)):
        half = core if e == 0 else 1 - core
        queries = None
        for t in range(2):
            pick = onehot((rows >= 224) & (cols == rows - 224 + 32 * t))
            part = dot(ref[t * 256 : (t + 1) * 256, 0:256], pick)
            queries = part if queries is None else queries + part
        hot = onehot(iota((512, 256), 0) == place_ref[half])
        part = dot(hot, queries.astype(BF))
        acc = part if acc is None else acc + part
    grouped[...] = acc.astype(BF)
    send_ref[...] = jnp.zeros_like(send_ref)
    keep_ref[...] = jnp.zeros_like(keep_ref)
    for p in range(32):
        holder, slot = g_ref[p], s_ref[p]

        @pl.when(holder != me)
        def _():
            send_ref[holder] = grouped[p * 16 : (p + 1) * 16, :]

        @pl.when(holder == me)
        def _():
            keep_ref[slot] = grouped[p * 16 : (p + 1) * 16, :]


def slot_kernel(pos_ref, owner_ref, rec_ref, keep_ref, state_ref, norm_ref, send_ref, own_ref, buf, spread):
    me = pos_ref[2]
    step = pl.program_id(0)

    @pl.when(step == 0)
    def _():
        send_ref[...] = jnp.zeros_like(send_ref)
        own_ref[...] = jnp.zeros_like(own_ref)
        row, f = iota((128, 384), 0), iota((128, 384), 1)
        a_at = jnp.where(f >= 17, lax.shift_right_logical(f - 17, 4), f - 1)
        b_at = (f - 17) & 15
        live_a = (f >= 1) & (f < 273)
        live_b = (f >= 17) & (f < 273)
        for base in range(4):
            spread[base * 2] = onehot(live_a & (row == a_at + base * 16))
            spread[base * 2 + 1] = onehot(live_b & (row == b_at + base * 16))

    for i in range(8):
        slot = step * 8 + i
        owner = owner_ref[slot]

        @pl.when(owner != me)
        def _():
            buf[i * 16 : (i + 1) * 16, :] = rec_ref[owner]

        @pl.when(owner == me)
        def _():
            buf[i * 16 : (i + 1) * 16, :] = keep_ref[slot]

    q = buf[...]
    lane = iota((1, 384), 1)
    square, line = lane >= 17, (lane >= 1) & (lane < 17)
    unit_a = jnp.where(lane == 0, 1.0, 0.0)
    unit_b = jnp.where(lane < 17, 1.0, 0.0)
    scale = jnp.where(square, 0.5**0.5 / 4.0, jnp.where(line, 0.5, 1.0))
    scale = jnp.where(lane < 273, scale, 0.0)
    r, c = iota((128, 16), 0), iota((128, 16), 1)
    den_lane = iota((128, 32), 1)
    phis, dens = [], []
    for t in range(2):
        tile = jnp.zeros((128, 32), F32)
        for h in range(2):
            left = dot(q, spread[t * 4 + h * 2]) + unit_a
            right = dot(q, spread[t * 4 + h * 2 + 1]) + unit_b
            phi = left * right * scale
            norm = dot(onehot(2 * lax.shift_right_logical(r, 4) + h == c), norm_ref[...])
            den = jnp.sum(phi * norm, axis=1, keepdims=True)
            rough = den.astype(BF).astype(F32)
            tile = jnp.where(den_lane == h, rough, jnp.where(den_lane == h + 2, den - rough, tile))
            phis.append(phi.astype(BF))
        dens.append(tile.astype(BF))
    first_head = iota((16, 224), 1) < 112
    for i in range(8):
        at = slice(i * 16, (i + 1) * 16)
        phi = jnp.concatenate([x[at, 0:273] for x in phis], axis=0)
        terms = dot(phi, state_ref[i])
        results = [
            jnp.where(first_head, terms[t * 32 : t * 32 + 16], terms[t * 32 + 16 : t * 32 + 32]).astype(BF) for t in range(2)
        ]
        slot = step * 8 + i
        owner = owner_ref[slot]

        @pl.when(owner != me)
        def _():
            for t in range(2):
                send_ref[owner, :, t * 256 : t * 256 + 224] = results[t]
                send_ref[owner, :, t * 256 + 224 : t * 256 + 256] = dens[t][at]

        @pl.when(owner == me)
        def _():
            for t in range(2):
                own_ref[slot, :, t * 256 : t * 256 + 224] = results[t]
                own_ref[slot, :, t * 256 + 224 : t * 256 + 256] = dens[t][at]


def kappa(s):
    return 1.0 + s + 0.5 * s * s


def tail_kernel(pos_ref, own_ref, rec_ref, tk_ref, tv_ref, len_ref, num_ref):
    core = pos_ref[1]
    r, c = iota((256, 256), 0), iota((256, 256), 1)
    expand_q = onehot((r >= 224) & (r - 224 == lax.shift_right_logical(c, 7) * 16 + (c & 15)))
    r, c = iota((256, 128), 0), iota((256, 128), 1)
    sum_a = onehot(lax.shift_right_logical(r, 4) == c)
    pick_q = onehot((r >= 224) & (r - 224 == c))
    r, c = iota((128, 128), 0), iota((128, 128), 1)
    pick_k = onehot(iota((32, 128), 0) == iota((32, 128), 1))
    sum_new = onehot((r < 32) & (lax.shift_right_logical(r, 4) == c))
    r, c = iota((128, 1792), 0), iota((128, 1792), 1)
    expand_w = onehot((r < 16) & (c >= r * 112) & (c < (r + 1) * 112))
    r, c = iota((1792, 256), 0), iota((1792, 256), 1)
    sum_v = onehot(
        functools.reduce(
            jnp.logical_or,
            [(r - c == 112 * (7 * (k // 8) + k % 8)) & (c >= 112 * (k // 8)) & (c < 112 * (k // 8 + 1)) for k in range(16)],
        )
    )
    r, c = iota((128, 256), 0), iota((128, 256), 1)
    den_at = onehot((r < 16) & (c == 224 + lax.shift_right_logical(r, 3)))
    den_new = onehot((r < 2) & (c == 224 + r))
    spread_new = onehot((r < 2) & (c < 224) & ((c >= 112) == (r >= 1)))
    head_lane = iota((256, 128), 1)
    for e, ref in enumerate((own_ref, rec_ref)):
        half = core if e == 0 else 1 - core
        at = pl.multiple_of(half * 256, 256)
        keys = tk_ref[pl.ds(at, 256), :].astype(F32)
        live = (head_lane & 7) < len_ref[pl.ds(at, 256), :]
        live = live & (head_lane < 16)
        values = tv_ref[pl.ds(at, 256), :]
        new_keys = [dot(ref[t * 256 : (t + 1) * 256, 256:288], pick_k) for t in range(2)]
        for t in range(2):
            vq = ref[t * 256 : (t + 1) * 256, 0:256]
            one, two = split(dot(vq, expand_q) * keys)
            weight = kappa((dot(one, sum_a) + dot(two, sum_a)) * 0.25)
            weight = jnp.where(live, weight, 0.0)
            one, two = split(weight)
            terms = dot(one, expand_w).astype(BF) * values
            num = dot(terms, sum_v) + (dot(one, den_at) + dot(two, den_at))
            query = dot(vq, pick_q)
            for i in range(t + 1):
                one, two = split(query * new_keys[i])
                weight = kappa((dot(one, sum_new) + dot(two, sum_new)) * 0.25)
                one, two = split(weight)
                num = num + dot(one, spread_new) * ref[i * 256 : (i + 1) * 256, 0:256].astype(F32)
                num = num + (dot(one, den_new) + dot(two, den_new))
            num_ref[e, t * 256 : (t + 1) * 256, :] = num


def combine_kernel(pos_ref, g_ref, s_ref, num_ref, rec_ref, own_ref, place_ref, out_ref, buf):
    core = pos_ref[1]
    me = pos_ref[2]
    for p in range(32):
        holder, slot = g_ref[p], s_ref[p]

        @pl.when(holder != me)
        def _():
            buf[p * 16 : (p + 1) * 16, :] = rec_ref[holder]

        @pl.when(holder == me)
        def _():
            buf[p * 16 : (p + 1) * 16, :] = own_ref[slot]

    r, c = iota((256, 256), 0), iota((256, 256), 1)
    spread = onehot((c < 224) & (((c < 112) & ((r == 224) | (r == 226))) | ((c >= 112) & ((r == 225) | (r == 227)))))
    lane = iota((256, 256), 1)
    for e in range(2):
        half = core if e == 0 else 1 - core
        at = pl.multiple_of(half * 256, 256)
        hot = onehot(iota((256, 512), 1) == place_ref[pl.ds(at, 256), :])
        prompt = dot(hot, buf[...])
        for t in range(2):
            num = num_ref[e, t * 256 : (t + 1) * 256, :] + prompt[:, t * 256 : (t + 1) * 256]
            one, two = split(num)
            den = dot(one, spread) + dot(two, spread)
            out = jnp.where(lane < 224, num / jnp.where(lane < 224, den, 1.0), 0.0)
            out = out.astype(BF)
            for part in range(2):
                out_ref[half * 2 + part, t * 128 : (t + 1) * 128, :] = out[part * 128 : (part + 1) * 128]


def out_kernel(pos_ref, own_ref, oth_ref, *refs):
    parts, first_ref, second_ref = refs[:8], refs[8], refs[9]
    y, core, col = pos_ref[0], pos_ref[1], pos_ref[3]
    acc = [None, None]
    for shift in range(4):
        j = lax.rem(y + 4 - shift, 4)
        for which, ref in enumerate((own_ref, oth_ref)):
            k = core if which == 0 else 1 - core
            heads = ref[j, :, 0:224]
            for e in range(2):
                part = dot(heads, parts[2 * shift + e][jnp.bitwise_xor(k, lax.rem(col, 2))])
                acc[e] = part if acc[e] is None else acc[e] + part
    same = lax.rem(y, 2) == lax.div(col, 2)
    first_ref[...] = jnp.where(same, acc[0], acc[1]).astype(BF)
    second_ref[...] = jnp.where(same, acc[1], acc[0]).astype(BF)


def body(tokens, w_query, w_key, w_value, w_out, cached_state, cached_norm, slot_prompt, prompt_of, tail_keys, tail_values, tail_length):
    y, core, col = lax.axis_index("y"), lax.axis_index("core"), lax.axis_index("col")
    me = lax.axis_index(("req", "col"))
    pos = jnp.stack([y, core, me, col]).astype(jnp.int32)
    owner = slot_prompt // 32
    slots = jnp.arange(32, dtype=jnp.int32)
    away = owner != me
    code = jnp.max(
        jnp.where((owner[None, :] == slots[:, None]) & away[None, :], (slots * 32 + slot_prompt % 32 + 1)[None, :], 0), axis=1
    )
    told = lax.all_to_all(code[:, None], ("req", "col"), split_axis=0, concat_axis=0, tiled=True)[:, 0]
    def over_y(x, step):
        return lax.ppermute(x, "y", [(i, (i + step) % 4) for i in range(4)])

    top, low = tokens[:128].reshape(128, 896), tokens[128:].reshape(128, 896)
    top_1, low_3 = over_y(top, 1), over_y(low, 3)
    low_1, top_3 = over_y(low, 1), over_y(top, 3)
    top_1, low_3, w_value, w_query, w_key = lax.optimization_barrier((top_1, low_3, w_value, w_query, w_key))
    top_1, low_3, low_1, top_3, told = lax.optimization_barrier((top_1, low_3, low_1, top_3, told))
    blocks = [top, low, top_1, low_1, over_y(top_1, 1), over_y(low_3, 3), top_3, low_3]
    value_w = jnp.moveaxis(w_value.reshape(2, 448, 112), 0, 1).reshape(448, 224)
    mine = jnp.concatenate([value_w, w_query, w_key], axis=1)
    theirs = lax.ppermute(mine, "core", [(0, 1), (1, 0)])
    here = (slot_prompt[None, :] == (me * 32 + slots)[:, None])
    there = (told[None, :] > 0) & ((told[None, :] - 1) % 32 == slots[:, None])
    at_slot = jnp.max(jnp.where(here, slots[None, :], 0), axis=1)
    at_holder = jnp.where(jnp.any(here, axis=1), me, jnp.max(jnp.where(there, slots[None, :], 0), axis=1)).astype(jnp.int32)
    index = jnp.arange(512)
    rank = jnp.sum(((prompt_of[None, :] == prompt_of[:, None]) & (index[None, :] < index[:, None])).astype(jnp.int32), axis=1)
    place = (prompt_of - me * 32) * 16 + rank
    norms = jnp.pad(jnp.transpose(cached_norm, (0, 2, 1)).reshape(64, 273), ((0, 0), (0, 111)))
    states = cached_state[0].reshape(273, 224, 32)

    partial = call(
        project_kernel,
        jax.ShapeDtypeStruct((4, 256, 1152), BF),
        1,
        pos,
        *blocks,
        mine,
        theirs,
        scratch=[pltpu.VMEM((448, 640), BF), pltpu.VMEM((512, 640), BF)],
        free=range(1, 11),
    )
    partial = lax.all_to_all(partial, "col", split_axis=0, concat_axis=0, tiled=True)
    states = jnp.transpose(states, (2, 0, 1))
    partial, states, norms = lax.optimization_barrier((partial, states, norms))
    shape = jax.ShapeDtypeStruct((512, 288), BF)
    own, oth = call(sum_kernel, (shape, shape), 1, pos, partial, free=(1,))
    rec = lax.ppermute(oth, "core", [(0, 1), (1, 0)])

    shape = jax.ShapeDtypeStruct((32, 16, 128), BF)
    q_send, q_keep = call(
        group_kernel,
        (shape, shape),
        3,
        pos,
        at_holder,
        at_slot,
        own,
        rec,
        place.reshape(2, 1, 256),
        scratch=[pltpu.VMEM((512, 128), BF)],
        free=(3, 4),
    )
    q_send, w_out = lax.optimization_barrier((q_send, w_out))
    pieces = []
    for s in range(4):
        perm = [(k * 4 + c, (c >> 1) * 4 + (s ^ (2 * (c & 1) + k))) for k in range(2) for c in range(4)]
        pieces.append(lax.ppermute(w_out, ("core", "col"), perm))
    pieces = [jnp.stack(pieces[:2]), jnp.stack(pieces[2:])]
    q_rec = lax.all_to_all(q_send, ("req", "col"), split_axis=0, concat_axis=0, tiled=True)
    q_rec, pieces = lax.optimization_barrier((q_rec, pieces))
    near_1, near_3 = over_y(pieces[0], 1), over_y(pieces[1], 3)
    shape = jax.ShapeDtypeStruct((2, 512, 256), F32)
    num = call(tail_kernel, shape, 1, pos, own, rec, tail_keys, tail_values, tail_length[:, None])
    shape = jax.ShapeDtypeStruct((32, 16, 512), BF)
    whole = pl.BlockSpec((32, 16, 128), lambda i: (0, 0, 0))
    whole_out = pl.BlockSpec((32, 16, 512), lambda i: (0, 0, 0))
    r_send, r_keep = pl.pallas_call(
        slot_kernel,
        grid=(4,),
        out_shape=(pltpu.HBM(shape.shape, BF), pltpu.HBM(shape.shape, BF)),
        in_specs=[
            SM,
            SM,
            whole,
            whole,
            pl.BlockSpec((8, 273, 224), lambda i: (i, 0, 0)),
            pl.BlockSpec((16, 384), lambda i: (i, 0)),
        ],
        out_specs=(whole_out, whole_out),
        scratch_shapes=[pltpu.VMEM((128, 128), BF), pltpu.VMEM((8, 128, 384), BF)],
        compiler_params=pltpu.CompilerParams(vmem_limit_bytes=VMEM_LIMIT),
    )(pos, owner, in_hbm(q_rec), in_hbm(q_keep), in_hbm(states), in_hbm(norms))
    r_send, near_1, near_3 = lax.optimization_barrier((r_send, near_1, near_3))
    out_w = [near_1, over_y(pieces[1], 1), over_y(pieces[0], 3), near_3]
    far_1, far_3 = over_y(near_1, 1), over_y(near_3, 3)
    r_rec = lax.all_to_all(r_send, ("req", "col"), split_axis=0, concat_axis=0, tiled=True)
    r_rec, num, out_w, far_1, far_3 = lax.optimization_barrier((r_rec, num, out_w, far_1, far_3))
    heads = call(
        combine_kernel,
        jax.ShapeDtypeStruct((4, 256, 256), BF),
        3,
        pos,
        at_holder,
        at_slot,
        num,
        r_rec,
        r_keep,
        place[:, None],
        scratch=[pltpu.VMEM((512, 512), BF)],
        free=(4,),
    )
    heads = lax.all_to_all(heads, "y", split_axis=0, concat_axis=0, tiled=True)
    heads_oth = lax.ppermute(heads, "core", [(0, 1), (1, 0)])
    shape = jax.ShapeDtypeStruct((256, 448), BF)
    mixed = call(out_kernel, (shape, shape), 1, pos, heads, heads_oth, *pieces, out_w[0], out_w[1], far_1, far_3, out_w[2], out_w[3], free=(1, 2))

    def at(y, core, col):
        return (y * 2 + core) * 4 + col

    got = []
    for s, part in enumerate(mixed):
        perm = [
            (at(j, k, b), at(b, j >> 1, 2 * k + (s ^ (j & 1)))) for b in range(4) for j in range(4) for k in range(2)
        ]
        got.append(lax.ppermute(part, ("y", "core", "col"), perm).reshape(2, 128, 448))
    odd = col % 2 == 1
    mixed = jnp.concatenate([jnp.where(odd, got[1], got[0]), jnp.where(odd, got[0], got[1])], axis=1)
    mixed = jnp.transpose(mixed, (1, 0, 2)).astype(F32)
    return (mixed + tokens.astype(F32)).astype(BF)


def solution(mesh):
    inner = Mesh(mesh.devices.reshape(8, 4, 2, 4), ("req", "y", "core", "col"))
    rows = ("y", "core")
    hold = ("req", "col")
    return jax.shard_map(
        body,
        mesh=inner,
        in_specs=(
            P(("req", "y", "core"), None, "col"),
            P("col", rows),
            P("col", rows),
            P(rows, "col"),
            P(rows, "col"),
            P(hold, None, rows),
            P(hold, None, rows),
            P(hold),
            P(hold),
            P(hold, rows),
            P(hold, rows),
            P(hold),
        ),
        out_specs=P(("req", "y", "core"), None, "col"),
        check_vma=False,
    )
```

```python
import functools

import jax
import jax.numpy as jnp
from jax import lax
from jax.experimental import pallas as pl
from jax.experimental.pallas import tpu as pltpu
from jax.sharding import Mesh, PartitionSpec as P

BF = jnp.bfloat16
F32 = jnp.float32
VMEM_LIMIT = 48 * 1024 * 1024
SM = pl.BlockSpec(memory_space=pltpu.SMEM)


def dot(a, b):
    return jnp.dot(a, b, preferred_element_type=F32)


def iota(shape, dim):
    return lax.broadcasted_iota(jnp.int32, shape, dim)


def onehot(cond):
    return jnp.where(cond, 1.0, 0.0).astype(BF)


def split(x):
    high = x.astype(BF)
    return high, (x - high.astype(F32)).astype(BF)


def in_hbm(x):
    return pltpu.with_memory_space_constraint(x, pltpu.HBM)


def call(kernel, out_shapes, n_smem, *args, scratch=(), free=()):
    def full(shape):
        zeros = (0,) * len(shape)
        return pl.BlockSpec(shape, lambda i: zeros)

    return pl.pallas_call(
        kernel,
        grid=(1,),
        out_shape=jax.tree.map(lambda x: pltpu.HBM(x.shape, x.dtype), out_shapes),
        in_specs=[SM] * n_smem + [full(x.shape) for x in args[n_smem:]],
        out_specs=jax.tree.map(lambda x: full(x.shape), out_shapes),
        scratch_shapes=scratch,
        compiler_params=pltpu.CompilerParams(vmem_limit_bytes=VMEM_LIMIT),
    )(*args[:n_smem], *[x if i + n_smem in free else in_hbm(x) for i, x in enumerate(args[n_smem:])])


def project_kernel(pos_ref, *refs):
    blocks, mine_ref, theirs_ref, out_ref, first, second = refs[:8], refs[8], refs[9], refs[10], refs[11], refs[12]
    core = pos_ref[1]
    one = jnp.where(core == 0, mine_ref[...], theirs_ref[...])
    two = jnp.where(core == 0, theirs_ref[...], mine_ref[...])
    first[:, 0:256] = one[:, 0:256]
    first[:, 256:512] = two[:, 0:256]
    first[:, 512:640] = jnp.concatenate([one[:, 256:288], two[:, 256:288], jnp.zeros((448, 64), BF)], axis=1)
    second[0:64, :] = jnp.zeros((64, 640), BF)
    second[64:512, 0:128] = jnp.concatenate([jnp.zeros((448, 64), BF), one[:, 256:288], two[:, 256:288]], axis=1)
    second[64:512, 128:384] = one[:, 0:256]
    second[64:512, 384:640] = two[:, 0:256]
    for shift in range(4):
        slot = lax.rem(pos_ref[0] + 4 - shift, 4)
        for part in range(2):
            block = blocks[2 * shift + part]
            a = dot(block[:, 0:448], first[...])
            b = dot(block[:, 384:896], second[...])
            at = slice(part * 128, (part + 1) * 128)
            out_ref[slot, at, 0:512] = a[:, 0:512].astype(BF)
            out_ref[slot, at, 512:640] = (a[:, 512:640] + b[:, 0:128]).astype(BF)
            out_ref[slot, at, 640:1152] = b[:, 128:640].astype(BF)


def sum_kernel(pos_ref, p_ref, own_ref, oth_ref):
    core = pos_ref[1]

    def total(lo, hi):
        acc = p_ref[0, :, lo:hi].astype(F32)
        for i in range(1, 4):
            acc = acc + p_ref[i, :, lo:hi].astype(F32)
        return acc.astype(BF)

    keys = total(512, 640)
    for t in range(2):
        at = slice(t * 256, (t + 1) * 256)
        one, two = total(t * 640, t * 640 + 256), total(t * 640 + 256, t * 640 + 512)
        own_ref[at, 0:256] = jnp.where(core == 0, one, two)
        oth_ref[at, 0:256] = jnp.where(core == 0, two, one)
        one, two = keys[:, t * 64 : t * 64 + 32], keys[:, t * 64 + 32 : t * 64 + 64]
        own_ref[at, 256:288] = jnp.where(core == 0, one, two)
        oth_ref[at, 256:288] = jnp.where(core == 0, two, one)


def group_kernel(pos_ref, g_ref, s_ref, own_ref, rec_ref, place_ref, send_ref, keep_ref, grouped):
    core = pos_ref[1]
    me = pos_ref[2]
    rows, cols = iota((256, 128), 0), iota((256, 128), 1)
    acc = None
    for e, ref in enumerate((own_ref, rec_ref)):
        half = core if e == 0 else 1 - core
        queries = None
        for t in range(2):
            pick = onehot((rows >= 224) & (cols == rows - 224 + 32 * t))
            part = dot(ref[t * 256 : (t + 1) * 256, 0:256], pick)
            queries = part if queries is None else queries + part
        hot = onehot(iota((512, 256), 0) == place_ref[half])
        part = dot(hot, queries.astype(BF))
        acc = part if acc is None else acc + part
    grouped[...] = acc.astype(BF)
    send_ref[...] = jnp.zeros_like(send_ref)
    keep_ref[...] = jnp.zeros_like(keep_ref)
    for p in range(32):
        holder, slot = g_ref[p], s_ref[p]

        @pl.when(holder != me)
        def _():
            send_ref[holder] = grouped[p * 16 : (p + 1) * 16, :]

        @pl.when(holder == me)
        def _():
            keep_ref[slot] = grouped[p * 16 : (p + 1) * 16, :]


def slot_kernel(pos_ref, owner_ref, rec_ref, keep_ref, state_ref, norm_ref, send_ref, own_ref, buf):
    me = pos_ref[2]
    step = pl.program_id(0)

    @pl.when(step == 0)
    def _():
        send_ref[...] = jnp.zeros_like(send_ref)
        own_ref[...] = jnp.zeros_like(own_ref)

    for i in range(8):
        slot = step * 8 + i
        owner = owner_ref[slot]

        @pl.when(owner != me)
        def _():
            buf[i * 16 : (i + 1) * 16, :] = rec_ref[owner]

        @pl.when(owner == me)
        def _():
            buf[i * 16 : (i + 1) * 16, :] = keep_ref[slot]

    q = buf[...]
    row, f = iota((128, 384), 0), iota((128, 384), 1)
    lane = iota((1, 384), 1)
    square, line = lane >= 17, (lane >= 1) & (lane < 17)
    unit_a = jnp.where(lane == 0, 1.0, 0.0)
    unit_b = jnp.where(lane < 17, 1.0, 0.0)
    scale = jnp.where(square, 0.5**0.5 / 4.0, jnp.where(line, 0.5, 1.0))
    scale = jnp.where(lane < 273, scale, 0.0)
    a_at = jnp.where(f >= 17, lax.shift_right_logical(f - 17, 4), f - 1)
    b_at = (f - 17) & 15
    live_a = (f >= 1) & (f < 273)
    live_b = (f >= 17) & (f < 273)
    r, c = iota((128, 16), 0), iota((128, 16), 1)
    den_lane = iota((128, 32), 1)
    phis, dens = [], []
    for t in range(2):
        tile = jnp.zeros((128, 32), F32)
        for h in range(2):
            base = t * 32 + h * 16
            left = dot(q, onehot(live_a & (row == a_at + base))) + unit_a
            right = dot(q, onehot(live_b & (row == b_at + base))) + unit_b
            phi = left * right * scale
            norm = dot(onehot(2 * lax.shift_right_logical(r, 4) + h == c), norm_ref[...])
            den = jnp.sum(phi * norm, axis=1, keepdims=True)
            rough = den.astype(BF).astype(F32)
            tile = jnp.where(den_lane == h, rough, jnp.where(den_lane == h + 2, den - rough, tile))
            phis.append(phi.astype(BF))
        dens.append(tile.astype(BF))
    first_head = iota((16, 224), 1) < 112
    for i in range(8):
        at = slice(i * 16, (i + 1) * 16)
        phi = jnp.concatenate([x[at, 0:273] for x in phis], axis=0)
        terms = dot(phi, state_ref[i])
        results = [
            jnp.where(first_head, terms[t * 32 : t * 32 + 16], terms[t * 32 + 16 : t * 32 + 32]).astype(BF) for t in range(2)
        ]
        slot = step * 8 + i
        owner = owner_ref[slot]

        @pl.when(owner != me)
        def _():
            for t in range(2):
                send_ref[owner, :, t * 256 : t * 256 + 224] = results[t]
                send_ref[owner, :, t * 256 + 224 : t * 256 + 256] = dens[t][at]

        @pl.when(owner == me)
        def _():
            for t in range(2):
                own_ref[slot, :, t * 256 : t * 256 + 224] = results[t]
                own_ref[slot, :, t * 256 + 224 : t * 256 + 256] = dens[t][at]


def kappa(s):
    return 1.0 + s + 0.5 * s * s


def tail_kernel(pos_ref, own_ref, rec_ref, tk_ref, tv_ref, len_ref, num_ref):
    core = pos_ref[1]
    r, c = iota((256, 256), 0), iota((256, 256), 1)
    expand_q = onehot((r >= 224) & (r - 224 == lax.shift_right_logical(c, 7) * 16 + (c & 15)))
    r, c = iota((256, 128), 0), iota((256, 128), 1)
    sum_a = onehot(lax.shift_right_logical(r, 4) == c)
    pick_q = onehot((r >= 224) & (r - 224 == c))
    r, c = iota((128, 128), 0), iota((128, 128), 1)
    pick_k = onehot(iota((32, 128), 0) == iota((32, 128), 1))
    sum_new = onehot((r < 32) & (lax.shift_right_logical(r, 4) == c))
    r, c = iota((128, 1792), 0), iota((128, 1792), 1)
    expand_w = onehot((r < 16) & (c >= r * 112) & (c < (r + 1) * 112))
    r, c = iota((1792, 256), 0), iota((1792, 256), 1)
    sum_v = onehot(
        functools.reduce(
            jnp.logical_or,
            [(r - c == 112 * (7 * (k // 8) + k % 8)) & (c >= 112 * (k // 8)) & (c < 112 * (k // 8 + 1)) for k in range(16)],
        )
    )
    r, c = iota((128, 256), 0), iota((128, 256), 1)
    den_at = onehot((r < 16) & (c == 224 + lax.shift_right_logical(r, 3)))
    den_new = onehot((r < 2) & (c == 224 + r))
    spread_new = onehot((r < 2) & (c < 224) & ((c >= 112) == (r >= 1)))
    head_lane = iota((256, 128), 1)
    for e, ref in enumerate((own_ref, rec_ref)):
        half = core if e == 0 else 1 - core
        at = pl.multiple_of(half * 256, 256)
        keys = tk_ref[pl.ds(at, 256), :].astype(F32)
        live = (head_lane & 7) < len_ref[pl.ds(at, 256), :]
        live = live & (head_lane < 16)
        values = tv_ref[pl.ds(at, 256), :]
        new_keys = [dot(ref[t * 256 : (t + 1) * 256, 256:288], pick_k) for t in range(2)]
        for t in range(2):
            vq = ref[t * 256 : (t + 1) * 256, 0:256]
            one, two = split(dot(vq, expand_q) * keys)
            weight = kappa((dot(one, sum_a) + dot(two, sum_a)) * 0.25)
            weight = jnp.where(live, weight, 0.0)
            one, two = split(weight)
            terms = dot(one, expand_w).astype(BF) * values
            num = dot(terms, sum_v) + (dot(one, den_at) + dot(two, den_at))
            query = dot(vq, pick_q)
            for i in range(t + 1):
                one, two = split(query * new_keys[i])
                weight = kappa((dot(one, sum_new) + dot(two, sum_new)) * 0.25)
                one, two = split(weight)
                num = num + dot(one, spread_new) * ref[i * 256 : (i + 1) * 256, 0:256].astype(F32)
                num = num + (dot(one, den_new) + dot(two, den_new))
            num_ref[e, t * 256 : (t + 1) * 256, :] = num


def combine_kernel(pos_ref, g_ref, s_ref, num_ref, rec_ref, own_ref, place_ref, out_ref, buf):
    core = pos_ref[1]
    me = pos_ref[2]
    for p in range(32):
        holder, slot = g_ref[p], s_ref[p]

        @pl.when(holder != me)
        def _():
            buf[p * 16 : (p + 1) * 16, :] = rec_ref[holder]

        @pl.when(holder == me)
        def _():
            buf[p * 16 : (p + 1) * 16, :] = own_ref[slot]

    r, c = iota((256, 256), 0), iota((256, 256), 1)
    spread = onehot((c < 224) & (((c < 112) & ((r == 224) | (r == 226))) | ((c >= 112) & ((r == 225) | (r == 227)))))
    lane = iota((256, 256), 1)
    for e in range(2):
        half = core if e == 0 else 1 - core
        at = pl.multiple_of(half * 256, 256)
        hot = onehot(iota((256, 512), 1) == place_ref[pl.ds(at, 256), :])
        prompt = dot(hot, buf[...])
        for t in range(2):
            num = num_ref[e, t * 256 : (t + 1) * 256, :] + prompt[:, t * 256 : (t + 1) * 256]
            one, two = split(num)
            den = dot(one, spread) + dot(two, spread)
            out = jnp.where(lane < 224, num / jnp.where(lane < 224, den, 1.0), 0.0)
            out = out.astype(BF)
            for part in range(2):
                out_ref[half * 2 + part, t * 128 : (t + 1) * 128, :] = out[part * 128 : (part + 1) * 128]


def out_kernel(pos_ref, own_ref, oth_ref, w_ref, first_ref, second_ref):
    y, core = pos_ref[0], pos_ref[1]
    acc = [None, None]
    for j in range(4):
        for which, ref in enumerate((own_ref, oth_ref)):
            row = j * 2 + (core if which == 0 else 1 - core)
            heads = ref[j, :, 0:224]
            for e in range(2):
                part = dot(heads, w_ref[row, e])
                acc[e] = part if acc[e] is None else acc[e] + part
    even = lax.rem(y, 2) == 0
    first_ref[...] = jnp.where(even, acc[0], acc[1]).astype(BF)
    second_ref[...] = jnp.where(even, acc[1], acc[0]).astype(BF)


def body(tokens, w_query, w_key, w_value, w_out, cached_state, cached_norm, slot_prompt, prompt_of, tail_keys, tail_values, tail_length):
    y, core, col = lax.axis_index("y"), lax.axis_index("core"), lax.axis_index("col")
    me = lax.axis_index(("req", "col"))
    pos = jnp.stack([y, core, me, col]).astype(jnp.int32)
    def over_y(x, step):
        return lax.ppermute(x, "y", [(i, (i + step) % 4) for i in range(4)])

    top, low = tokens[:128].reshape(128, 896), tokens[128:].reshape(128, 896)
    top_1, low_3 = over_y(top, 1), over_y(low, 3)
    low_1, top_3 = over_y(low, 1), over_y(top, 3)
    blocks = [top, low, top_1, low_1, over_y(top_1, 1), over_y(low_3, 3), top_3, low_3]
    value_w = jnp.moveaxis(w_value.reshape(2, 448, 112), 0, 1).reshape(448, 224)
    mine = jnp.concatenate([value_w, w_query, w_key], axis=1)
    theirs = lax.ppermute(mine, "core", [(0, 1), (1, 0)])
    owner = slot_prompt // 32
    slots = jnp.arange(32, dtype=jnp.int32)
    away = owner != me
    code = jnp.max(
        jnp.where((owner[None, :] == slots[:, None]) & away[None, :], (slots * 32 + slot_prompt % 32 + 1)[None, :], 0), axis=1
    )
    told = lax.all_to_all(code[:, None], ("req", "col"), split_axis=0, concat_axis=0, tiled=True)[:, 0]
    theirs, told = lax.optimization_barrier((theirs, told))
    here = (slot_prompt[None, :] == (me * 32 + slots)[:, None])
    there = (told[None, :] > 0) & ((told[None, :] - 1) % 32 == slots[:, None])
    at_slot = jnp.max(jnp.where(here, slots[None, :], 0), axis=1)
    at_holder = jnp.where(jnp.any(here, axis=1), me, jnp.max(jnp.where(there, slots[None, :], 0), axis=1)).astype(jnp.int32)
    index = jnp.arange(512)
    rank = jnp.sum(((prompt_of[None, :] == prompt_of[:, None]) & (index[None, :] < index[:, None])).astype(jnp.int32), axis=1)
    place = (prompt_of - me * 32) * 16 + rank
    norms = jnp.pad(jnp.transpose(cached_norm, (0, 2, 1)).reshape(64, 273), ((0, 0), (0, 111)))
    states = cached_state[0].reshape(273, 224, 32)

    partial = call(
        project_kernel,
        jax.ShapeDtypeStruct((4, 256, 1152), BF),
        1,
        pos,
        *blocks,
        mine,
        theirs,
        scratch=[pltpu.VMEM((448, 640), BF), pltpu.VMEM((512, 640), BF)],
        free=range(1, 11),
    )
    partial, w_out = lax.optimization_barrier((partial, w_out))
    out_w = lax.all_gather(w_out, ("y", "core", "col"), axis=0, tiled=False).reshape(8, 4, 224, 448)
    partial = lax.all_to_all(partial, "col", split_axis=0, concat_axis=0, tiled=True)
    states = jnp.transpose(states, (2, 0, 1))
    partial, states, norms = lax.optimization_barrier((partial, states, norms))
    shape = jax.ShapeDtypeStruct((512, 288), BF)
    own, oth = call(sum_kernel, (shape, shape), 1, pos, partial, free=(1,))
    rec = lax.ppermute(oth, "core", [(0, 1), (1, 0)])

    shape = jax.ShapeDtypeStruct((32, 16, 128), BF)
    q_send, q_keep = call(
        group_kernel,
        (shape, shape),
        3,
        pos,
        at_holder,
        at_slot,
        own,
        rec,
        place.reshape(2, 1, 256),
        scratch=[pltpu.VMEM((512, 128), BF)],
        free=(3, 4),
    )
    q_rec = lax.all_to_all(q_send, ("req", "col"), split_axis=0, concat_axis=0, tiled=True)
    shape = jax.ShapeDtypeStruct((2, 512, 256), F32)
    num = call(tail_kernel, shape, 1, pos, own, rec, tail_keys, tail_values, tail_length[:, None])
    q_rec, num = lax.optimization_barrier((q_rec, num))
    shape = jax.ShapeDtypeStruct((32, 16, 512), BF)
    whole = pl.BlockSpec((32, 16, 128), lambda i: (0, 0, 0))
    whole_out = pl.BlockSpec((32, 16, 512), lambda i: (0, 0, 0))
    r_send, r_keep = pl.pallas_call(
        slot_kernel,
        grid=(4,),
        out_shape=(pltpu.HBM(shape.shape, BF), pltpu.HBM(shape.shape, BF)),
        in_specs=[
            SM,
            SM,
            whole,
            whole,
            pl.BlockSpec((8, 273, 224), lambda i: (i, 0, 0)),
            pl.BlockSpec((16, 384), lambda i: (i, 0)),
        ],
        out_specs=(whole_out, whole_out),
        scratch_shapes=[pltpu.VMEM((128, 128), BF)],
        compiler_params=pltpu.CompilerParams(vmem_limit_bytes=VMEM_LIMIT),
    )(pos, owner, in_hbm(q_rec), in_hbm(q_keep), in_hbm(states), in_hbm(norms))
    r_rec = lax.all_to_all(r_send, ("req", "col"), split_axis=0, concat_axis=0, tiled=True)
    heads = call(
        combine_kernel,
        jax.ShapeDtypeStruct((4, 256, 256), BF),
        3,
        pos,
        at_holder,
        at_slot,
        num,
        r_rec,
        r_keep,
        place[:, None],
        scratch=[pltpu.VMEM((512, 512), BF)],
        free=(4,),
    )
    heads = lax.all_to_all(heads, "y", split_axis=0, concat_axis=0, tiled=True)
    heads_oth = lax.ppermute(heads, "core", [(0, 1), (1, 0)])
    heads_spec = pl.BlockSpec((4, 256, 256), lambda i, pos_ref: (0, 0, 0))
    half_spec = pl.BlockSpec((256, 448), lambda i, pos_ref: (0, 0))
    mixed = pl.pallas_call(
        out_kernel,
        out_shape=(pltpu.HBM((256, 448), BF), pltpu.HBM((256, 448), BF)),
        grid_spec=pltpu.PrefetchScalarGridSpec(
            num_scalar_prefetch=1,
            grid=(1,),
            in_specs=[
                heads_spec,
                heads_spec,
                pl.BlockSpec((8, 2, 224, 448), lambda i, pos_ref: (0, pos_ref[1], 0, 0)),
            ],
            out_specs=(half_spec, half_spec),
        ),
        compiler_params=pltpu.CompilerParams(vmem_limit_bytes=VMEM_LIMIT),
    )(pos, heads, heads_oth, in_hbm(out_w))

    def at(y, core, col):
        return (y * 2 + core) * 4 + col

    got = []
    for s, part in enumerate(mixed):
        perm = [
            (at(j, k, b), at(b, j >> 1, 2 * k + (s ^ (j & 1)))) for b in range(4) for j in range(4) for k in range(2)
        ]
        got.append(lax.ppermute(part, ("y", "core", "col"), perm).reshape(2, 128, 448))
    odd = col % 2 == 1
    mixed = jnp.concatenate([jnp.where(odd, got[1], got[0]), jnp.where(odd, got[0], got[1])], axis=1)
    mixed = jnp.transpose(mixed, (1, 0, 2)).astype(F32)
    return (mixed + tokens.astype(F32)).astype(BF)


def solution(mesh):
    inner = Mesh(mesh.devices.reshape(8, 4, 2, 4), ("req", "y", "core", "col"))
    rows = ("y", "core")
    hold = ("req", "col")
    return jax.shard_map(
        body,
        mesh=inner,
        in_specs=(
            P(("req", "y", "core"), None, "col"),
            P("col", rows),
            P("col", rows),
            P(rows, "col"),
            P(rows, "col"),
            P(hold, None, rows),
            P(hold, None, rows),
            P(hold),
            P(hold),
            P(hold, rows),
            P(hold, rows),
            P(hold),
        ),
        out_specs=P(("req", "y", "core"), None, "col"),
        check_vma=False,
    )
```

```python
import functools

import jax
import jax.numpy as jnp
from jax import lax
from jax.experimental import pallas as pl
from jax.experimental.pallas import tpu as pltpu
from jax.sharding import Mesh, PartitionSpec as P

BF = jnp.bfloat16
F32 = jnp.float32
VMEM_LIMIT = 48 * 1024 * 1024
SM = pl.BlockSpec(memory_space=pltpu.SMEM)


def dot(a, b):
    return jnp.dot(a, b, preferred_element_type=F32)


def iota(shape, dim):
    return lax.broadcasted_iota(jnp.int32, shape, dim)


def onehot(cond):
    return jnp.where(cond, 1.0, 0.0).astype(BF)


def split(x):
    high = x.astype(BF)
    return high, (x - high.astype(F32)).astype(BF)


def in_hbm(x):
    return pltpu.with_memory_space_constraint(x, pltpu.HBM)


def call(kernel, out_shapes, n_smem, *args, scratch=(), free=()):
    def full(shape):
        zeros = (0,) * len(shape)
        return pl.BlockSpec(shape, lambda i: zeros)

    return pl.pallas_call(
        kernel,
        grid=(1,),
        out_shape=jax.tree.map(lambda x: pltpu.HBM(x.shape, x.dtype), out_shapes),
        in_specs=[SM] * n_smem + [full(x.shape) for x in args[n_smem:]],
        out_specs=jax.tree.map(lambda x: full(x.shape), out_shapes),
        scratch_shapes=scratch,
        compiler_params=pltpu.CompilerParams(vmem_limit_bytes=VMEM_LIMIT),
    )(*args[:n_smem], *[x if i + n_smem in free else in_hbm(x) for i, x in enumerate(args[n_smem:])])


def project_kernel(pos_ref, *refs):
    blocks, mine_ref, theirs_ref, out_ref, first, second = refs[:8], refs[8], refs[9], refs[10], refs[11], refs[12]
    core = pos_ref[1]
    one = jnp.where(core == 0, mine_ref[...], theirs_ref[...])
    two = jnp.where(core == 0, theirs_ref[...], mine_ref[...])
    first[:, 0:256] = one[:, 0:256]
    first[:, 256:512] = two[:, 0:256]
    first[:, 512:640] = jnp.concatenate([one[:, 256:288], two[:, 256:288], jnp.zeros((448, 64), BF)], axis=1)
    second[0:64, :] = jnp.zeros((64, 640), BF)
    second[64:512, 0:128] = jnp.concatenate([jnp.zeros((448, 64), BF), one[:, 256:288], two[:, 256:288]], axis=1)
    second[64:512, 128:384] = one[:, 0:256]
    second[64:512, 384:640] = two[:, 0:256]
    for shift in range(4):
        slot = lax.rem(pos_ref[0] + 4 - shift, 4)
        for part in range(2):
            block = blocks[2 * shift + part]
            a = dot(block[:, 0:448], first[...])
            b = dot(block[:, 384:896], second[...])
            at = slice(part * 128, (part + 1) * 128)
            out_ref[slot, at, 0:512] = a[:, 0:512].astype(BF)
            out_ref[slot, at, 512:640] = (a[:, 512:640] + b[:, 0:128]).astype(BF)
            out_ref[slot, at, 640:1152] = b[:, 128:640].astype(BF)


def sum_kernel(pos_ref, p_ref, own_ref, oth_ref):
    core = pos_ref[1]

    def total(lo, hi):
        acc = p_ref[0, :, lo:hi].astype(F32)
        for i in range(1, 4):
            acc = acc + p_ref[i, :, lo:hi].astype(F32)
        return acc.astype(BF)

    keys = total(512, 640)
    for t in range(2):
        at = slice(t * 256, (t + 1) * 256)
        one, two = total(t * 640, t * 640 + 256), total(t * 640 + 256, t * 640 + 512)
        own_ref[at, 0:256] = jnp.where(core == 0, one, two)
        oth_ref[at, 0:256] = jnp.where(core == 0, two, one)
        one, two = keys[:, t * 64 : t * 64 + 32], keys[:, t * 64 + 32 : t * 64 + 64]
        own_ref[at, 256:288] = jnp.where(core == 0, one, two)
        oth_ref[at, 256:288] = jnp.where(core == 0, two, one)


def group_kernel(pos_ref, g_ref, s_ref, own_ref, rec_ref, place_ref, send_ref, keep_ref, grouped):
    core = pos_ref[1]
    me = pos_ref[2]
    rows, cols = iota((256, 128), 0), iota((256, 128), 1)
    acc = None
    for e, ref in enumerate((own_ref, rec_ref)):
        half = core if e == 0 else 1 - core
        queries = None
        for t in range(2):
            pick = onehot((rows >= 224) & (cols == rows - 224 + 32 * t))
            part = dot(ref[t * 256 : (t + 1) * 256, 0:256], pick)
            queries = part if queries is None else queries + part
        hot = onehot(iota((512, 256), 0) == place_ref[half])
        part = dot(hot, queries.astype(BF))
        acc = part if acc is None else acc + part
    grouped[...] = acc.astype(BF)
    send_ref[...] = jnp.zeros_like(send_ref)
    keep_ref[...] = jnp.zeros_like(keep_ref)
    for p in range(32):
        holder, slot = g_ref[p], s_ref[p]

        @pl.when(holder != me)
        def _():
            send_ref[holder] = grouped[p * 16 : (p + 1) * 16, :]

        @pl.when(holder == me)
        def _():
            keep_ref[slot] = grouped[p * 16 : (p + 1) * 16, :]


def slot_kernel(pos_ref, owner_ref, rec_ref, keep_ref, state_ref, norm_ref, send_ref, own_ref, buf):
    me = pos_ref[2]
    step = pl.program_id(0)

    @pl.when(step == 0)
    def _():
        send_ref[...] = jnp.zeros_like(send_ref)
        own_ref[...] = jnp.zeros_like(own_ref)

    for i in range(8):
        slot = step * 8 + i
        owner = owner_ref[slot]

        @pl.when(owner != me)
        def _():
            buf[i * 16 : (i + 1) * 16, :] = rec_ref[owner]

        @pl.when(owner == me)
        def _():
            buf[i * 16 : (i + 1) * 16, :] = keep_ref[slot]

    q = buf[...]
    row, f = iota((128, 384), 0), iota((128, 384), 1)
    lane = iota((1, 384), 1)
    square, line = lane >= 17, (lane >= 1) & (lane < 17)
    unit_a = jnp.where(lane == 0, 1.0, 0.0)
    unit_b = jnp.where(lane < 17, 1.0, 0.0)
    scale = jnp.where(square, 0.5**0.5 / 4.0, jnp.where(line, 0.5, 1.0))
    scale = jnp.where(lane < 273, scale, 0.0)
    a_at = jnp.where(f >= 17, lax.shift_right_logical(f - 17, 4), f - 1)
    b_at = (f - 17) & 15
    live_a = (f >= 1) & (f < 273)
    live_b = (f >= 17) & (f < 273)
    r, c = iota((128, 16), 0), iota((128, 16), 1)
    den_lane = iota((128, 32), 1)
    phis, dens = [], []
    for t in range(2):
        tile = jnp.zeros((128, 32), F32)
        for h in range(2):
            base = t * 32 + h * 16
            left = dot(q, onehot(live_a & (row == a_at + base))) + unit_a
            right = dot(q, onehot(live_b & (row == b_at + base))) + unit_b
            phi = left * right * scale
            norm = dot(onehot(2 * lax.shift_right_logical(r, 4) + h == c), norm_ref[...])
            den = jnp.sum(phi * norm, axis=1, keepdims=True)
            rough = den.astype(BF).astype(F32)
            tile = jnp.where(den_lane == h, rough, jnp.where(den_lane == h + 2, den - rough, tile))
            phis.append(phi.astype(BF))
        dens.append(tile.astype(BF))
    first_head = iota((16, 224), 1) < 112
    for i in range(8):
        at = slice(i * 16, (i + 1) * 16)
        phi = jnp.concatenate([x[at, 0:273] for x in phis], axis=0)
        terms = dot(phi, state_ref[i])
        results = [
            jnp.where(first_head, terms[t * 32 : t * 32 + 16], terms[t * 32 + 16 : t * 32 + 32]).astype(BF) for t in range(2)
        ]
        slot = step * 8 + i
        owner = owner_ref[slot]

        @pl.when(owner != me)
        def _():
            for t in range(2):
                send_ref[owner, :, t * 256 : t * 256 + 224] = results[t]
                send_ref[owner, :, t * 256 + 224 : t * 256 + 256] = dens[t][at]

        @pl.when(owner == me)
        def _():
            for t in range(2):
                own_ref[slot, :, t * 256 : t * 256 + 224] = results[t]
                own_ref[slot, :, t * 256 + 224 : t * 256 + 256] = dens[t][at]


def kappa(s):
    return 1.0 + s + 0.5 * s * s


def tail_kernel(pos_ref, own_ref, rec_ref, tk_ref, tv_ref, len_ref, num_ref):
    core = pos_ref[1]
    r, c = iota((256, 256), 0), iota((256, 256), 1)
    expand_q = onehot((r >= 224) & (r - 224 == lax.shift_right_logical(c, 7) * 16 + (c & 15)))
    r, c = iota((256, 128), 0), iota((256, 128), 1)
    sum_a = onehot(lax.shift_right_logical(r, 4) == c)
    pick_q = onehot((r >= 224) & (r - 224 == c))
    r, c = iota((128, 128), 0), iota((128, 128), 1)
    pick_k = onehot(iota((32, 128), 0) == iota((32, 128), 1))
    sum_new = onehot((r < 32) & (lax.shift_right_logical(r, 4) == c))
    r, c = iota((128, 1792), 0), iota((128, 1792), 1)
    expand_w = onehot((r < 16) & (c >= r * 112) & (c < (r + 1) * 112))
    r, c = iota((1792, 256), 0), iota((1792, 256), 1)
    sum_v = onehot(
        functools.reduce(
            jnp.logical_or,
            [(r - c == 112 * (7 * (k // 8) + k % 8)) & (c >= 112 * (k // 8)) & (c < 112 * (k // 8 + 1)) for k in range(16)],
        )
    )
    r, c = iota((128, 256), 0), iota((128, 256), 1)
    den_at = onehot((r < 16) & (c == 224 + lax.shift_right_logical(r, 3)))
    den_new = onehot((r < 2) & (c == 224 + r))
    spread_new = onehot((r < 2) & (c < 224) & ((c >= 112) == (r >= 1)))
    head_lane = iota((256, 128), 1)
    for e, ref in enumerate((own_ref, rec_ref)):
        half = core if e == 0 else 1 - core
        at = pl.multiple_of(half * 256, 256)
        keys = tk_ref[pl.ds(at, 256), :].astype(F32)
        live = (head_lane & 7) < len_ref[pl.ds(at, 256), :]
        live = live & (head_lane < 16)
        values = tv_ref[pl.ds(at, 256), :]
        new_keys = [dot(ref[t * 256 : (t + 1) * 256, 256:288], pick_k) for t in range(2)]
        for t in range(2):
            vq = ref[t * 256 : (t + 1) * 256, 0:256]
            one, two = split(dot(vq, expand_q) * keys)
            weight = kappa((dot(one, sum_a) + dot(two, sum_a)) * 0.25)
            weight = jnp.where(live, weight, 0.0)
            one, two = split(weight)
            terms = dot(one, expand_w).astype(BF) * values
            num = dot(terms, sum_v) + (dot(one, den_at) + dot(two, den_at))
            query = dot(vq, pick_q)
            for i in range(t + 1):
                one, two = split(query * new_keys[i])
                weight = kappa((dot(one, sum_new) + dot(two, sum_new)) * 0.25)
                one, two = split(weight)
                num = num + dot(one, spread_new) * ref[i * 256 : (i + 1) * 256, 0:256].astype(F32)
                num = num + (dot(one, den_new) + dot(two, den_new))
            num_ref[e, t * 256 : (t + 1) * 256, :] = num


def combine_kernel(pos_ref, g_ref, s_ref, num_ref, rec_ref, own_ref, place_ref, out_ref, buf):
    core = pos_ref[1]
    me = pos_ref[2]
    for p in range(32):
        holder, slot = g_ref[p], s_ref[p]

        @pl.when(holder != me)
        def _():
            buf[p * 16 : (p + 1) * 16, :] = rec_ref[holder]

        @pl.when(holder == me)
        def _():
            buf[p * 16 : (p + 1) * 16, :] = own_ref[slot]

    r, c = iota((256, 256), 0), iota((256, 256), 1)
    spread = onehot((c < 224) & (((c < 112) & ((r == 224) | (r == 226))) | ((c >= 112) & ((r == 225) | (r == 227)))))
    lane = iota((256, 256), 1)
    for e in range(2):
        half = core if e == 0 else 1 - core
        at = pl.multiple_of(half * 256, 256)
        hot = onehot(iota((256, 512), 1) == place_ref[pl.ds(at, 256), :])
        prompt = dot(hot, buf[...])
        for t in range(2):
            num = num_ref[e, t * 256 : (t + 1) * 256, :] + prompt[:, t * 256 : (t + 1) * 256]
            one, two = split(num)
            den = dot(one, spread) + dot(two, spread)
            out = jnp.where(lane < 224, num / jnp.where(lane < 224, den, 1.0), 0.0)
            out = out.astype(BF)
            for part in range(2):
                out_ref[half * 2 + part, t * 128 : (t + 1) * 128, :] = out[part * 128 : (part + 1) * 128]


def out_kernel(pos_ref, own_ref, oth_ref, *refs):
    w0, w1, far_1, far_3, w3, first_ref, second_ref = refs
    y, core, col = pos_ref[0], pos_ref[1], pos_ref[3]
    acc = [None, None]
    for shift in range(4):
        j = lax.rem(y + 4 - shift, 4)
        for which, ref in enumerate((own_ref, oth_ref)):
            k = core if which == 0 else 1 - core
            heads = ref[j, :, 0:224]
            for e in range(2):
                at = jnp.bitwise_xor(k, lax.rem(col, 2))
                w = (far_1, far_3)[e][at] if shift == 2 else (w0, w1, None, w3)[shift][2 * e + at]
                part = dot(heads, w)
                acc[e] = part if acc[e] is None else acc[e] + part
    same = lax.rem(y, 2) == lax.div(col, 2)
    first_ref[...] = jnp.where(same, acc[0], acc[1]).astype(BF)
    second_ref[...] = jnp.where(same, acc[1], acc[0]).astype(BF)


def body(tokens, w_query, w_key, w_value, w_out, cached_state, cached_norm, slot_prompt, prompt_of, tail_keys, tail_values, tail_length):
    y, core, col = lax.axis_index("y"), lax.axis_index("core"), lax.axis_index("col")
    me = lax.axis_index(("req", "col"))
    pos = jnp.stack([y, core, me, col]).astype(jnp.int32)
    def over_y(x, step):
        return lax.ppermute(x, "y", [(i, (i + step) % 4) for i in range(4)])

    top, low = tokens[:128].reshape(128, 896), tokens[128:].reshape(128, 896)
    top_1, low_3 = over_y(top, 1), over_y(low, 3)
    low_1, top_3 = over_y(low, 1), over_y(top, 3)
    blocks = [top, low, top_1, low_1, over_y(top_1, 1), over_y(low_3, 3), top_3, low_3]
    value_w = jnp.moveaxis(w_value.reshape(2, 448, 112), 0, 1).reshape(448, 224)
    mine = jnp.concatenate([value_w, w_query, w_key], axis=1)
    theirs = lax.ppermute(mine, "core", [(0, 1), (1, 0)])
    owner = slot_prompt // 32
    slots = jnp.arange(32, dtype=jnp.int32)
    away = owner != me
    code = jnp.max(
        jnp.where((owner[None, :] == slots[:, None]) & away[None, :], (slots * 32 + slot_prompt % 32 + 1)[None, :], 0), axis=1
    )
    told = lax.all_to_all(code[:, None], ("req", "col"), split_axis=0, concat_axis=0, tiled=True)[:, 0]
    here = (slot_prompt[None, :] == (me * 32 + slots)[:, None])
    there = (told[None, :] > 0) & ((told[None, :] - 1) % 32 == slots[:, None])
    at_slot = jnp.max(jnp.where(here, slots[None, :], 0), axis=1)
    at_holder = jnp.where(jnp.any(here, axis=1), me, jnp.max(jnp.where(there, slots[None, :], 0), axis=1)).astype(jnp.int32)
    index = jnp.arange(512)
    rank = jnp.sum(((prompt_of[None, :] == prompt_of[:, None]) & (index[None, :] < index[:, None])).astype(jnp.int32), axis=1)
    place = (prompt_of - me * 32) * 16 + rank
    norms = jnp.pad(jnp.transpose(cached_norm, (0, 2, 1)).reshape(64, 273), ((0, 0), (0, 111)))
    states = cached_state[0].reshape(273, 224, 32)

    partial = call(
        project_kernel,
        jax.ShapeDtypeStruct((4, 256, 1152), BF),
        1,
        pos,
        *blocks,
        mine,
        theirs,
        scratch=[pltpu.VMEM((448, 640), BF), pltpu.VMEM((512, 640), BF)],
        free=range(1, 11),
    )
    partial, w_out = lax.optimization_barrier((partial, w_out))
    pieces = []
    for s in range(4):
        perm = [(k * 4 + c, (c >> 1) * 4 + (s ^ (2 * (c & 1) + k))) for k in range(2) for c in range(4)]
        pieces.append(lax.ppermute(w_out, ("core", "col"), perm))
    pieces = jnp.stack(pieces)
    out_1, out_3 = over_y(pieces, 1), over_y(pieces, 3)
    partial = lax.all_to_all(partial, "col", split_axis=0, concat_axis=0, tiled=True)
    partial, states, norms = lax.optimization_barrier((partial, states, norms))
    states = jnp.transpose(states, (2, 0, 1))
    shape = jax.ShapeDtypeStruct((512, 288), BF)
    own, oth = call(sum_kernel, (shape, shape), 1, pos, partial, free=(1,))
    rec = lax.ppermute(oth, "core", [(0, 1), (1, 0)])

    shape = jax.ShapeDtypeStruct((32, 16, 128), BF)
    q_send, q_keep = call(
        group_kernel,
        (shape, shape),
        3,
        pos,
        at_holder,
        at_slot,
        own,
        rec,
        place.reshape(2, 1, 256),
        scratch=[pltpu.VMEM((512, 128), BF)],
        free=(3, 4),
    )
    q_rec = lax.all_to_all(q_send, ("req", "col"), split_axis=0, concat_axis=0, tiled=True)
    shape = jax.ShapeDtypeStruct((2, 512, 256), F32)
    num = call(tail_kernel, shape, 1, pos, own, rec, tail_keys, tail_values, tail_length[:, None], free=(1, 2))
    q_rec, out_1, out_3 = lax.optimization_barrier((q_rec, out_1, out_3))
    shape = jax.ShapeDtypeStruct((32, 16, 512), BF)
    whole = pl.BlockSpec((32, 16, 128), lambda i: (0, 0, 0))
    whole_out = pl.BlockSpec((32, 16, 512), lambda i: (0, 0, 0))
    r_send, r_keep = pl.pallas_call(
        slot_kernel,
        grid=(4,),
        out_shape=(pltpu.HBM(shape.shape, BF), pltpu.HBM(shape.shape, BF)),
        in_specs=[
            SM,
            SM,
            whole,
            whole,
            pl.BlockSpec((8, 273, 224), lambda i: (i, 0, 0)),
            pl.BlockSpec((16, 384), lambda i: (i, 0)),
        ],
        out_specs=(whole_out, whole_out),
        scratch_shapes=[pltpu.VMEM((128, 128), BF)],
        compiler_params=pltpu.CompilerParams(vmem_limit_bytes=VMEM_LIMIT),
    )(pos, owner, in_hbm(q_rec), in_hbm(q_keep), in_hbm(states), in_hbm(norms))
    r_send, near_1, near_3 = lax.optimization_barrier((r_send, out_1, out_3))
    far_1, far_3 = over_y(near_1[:2], 1), over_y(near_3[2:], 3)
    r_rec = lax.all_to_all(r_send, ("req", "col"), split_axis=0, concat_axis=0, tiled=True)
    r_rec, num, far_1, far_3 = lax.optimization_barrier((r_rec, num, far_1, far_3))
    heads = call(
        combine_kernel,
        jax.ShapeDtypeStruct((4, 256, 256), BF),
        3,
        pos,
        at_holder,
        at_slot,
        num,
        r_rec,
        r_keep,
        place[:, None],
        scratch=[pltpu.VMEM((512, 512), BF)],
        free=(4,),
    )
    heads = lax.all_to_all(heads, "y", split_axis=0, concat_axis=0, tiled=True)
    heads_oth = lax.ppermute(heads, "core", [(0, 1), (1, 0)])
    shape = jax.ShapeDtypeStruct((256, 448), BF)
    mixed = call(out_kernel, (shape, shape), 1, pos, heads, heads_oth, pieces, out_1, far_1, far_3, out_3, free=(1, 2))

    def at(y, core, col):
        return (y * 2 + core) * 4 + col

    got = []
    for s, part in enumerate(mixed):
        perm = [
            (at(j, k, b), at(b, j >> 1, 2 * k + (s ^ (j & 1)))) for b in range(4) for j in range(4) for k in range(2)
        ]
        got.append(lax.ppermute(part, ("y", "core", "col"), perm).reshape(2, 128, 448))
    odd = col % 2 == 1
    mixed = jnp.concatenate([jnp.where(odd, got[1], got[0]), jnp.where(odd, got[0], got[1])], axis=1)
    mixed = jnp.transpose(mixed, (1, 0, 2)).astype(F32)
    return (mixed + tokens.astype(F32)).astype(BF)


def solution(mesh):
    inner = Mesh(mesh.devices.reshape(8, 4, 2, 4), ("req", "y", "core", "col"))
    rows = ("y", "core")
    hold = ("req", "col")
    return jax.shard_map(
        body,
        mesh=inner,
        in_specs=(
            P(("req", "y", "core"), None, "col"),
            P("col", rows),
            P("col", rows),
            P(rows, "col"),
            P(rows, "col"),
            P(hold, None, rows),
            P(hold, None, rows),
            P(hold),
            P(hold),
            P(hold, rows),
            P(hold, rows),
            P(hold),
        ),
        out_specs=P(("req", "y", "core"), None, "col"),
        check_vma=False,
    )
```

```python
import functools

import jax
import jax.numpy as jnp
from jax import lax
from jax.experimental import pallas as pl
from jax.experimental.pallas import tpu as pltpu
from jax.sharding import Mesh, PartitionSpec as P

BF = jnp.bfloat16
F32 = jnp.float32
VMEM_LIMIT = 48 * 1024 * 1024
SM = pl.BlockSpec(memory_space=pltpu.SMEM)


def dot(a, b):
    return jnp.dot(a, b, preferred_element_type=F32)


def iota(shape, dim):
    return lax.broadcasted_iota(jnp.int32, shape, dim)


def onehot(cond):
    return jnp.where(cond, 1.0, 0.0).astype(BF)


def split(x):
    high = x.astype(BF)
    return high, (x - high.astype(F32)).astype(BF)


def in_hbm(x):
    return pltpu.with_memory_space_constraint(x, pltpu.HBM)


def call(kernel, out_shapes, n_smem, *args, scratch=(), free=(), pin=True):
    def full(shape):
        zeros = (0,) * len(shape)
        return pl.BlockSpec(shape, lambda i: zeros)

    return pl.pallas_call(
        kernel,
        grid=(1,),
        out_shape=jax.tree.map(lambda x: pltpu.HBM(x.shape, x.dtype), out_shapes) if pin else out_shapes,
        in_specs=[SM] * n_smem + [full(x.shape) for x in args[n_smem:]],
        out_specs=jax.tree.map(lambda x: full(x.shape), out_shapes),
        scratch_shapes=scratch,
        compiler_params=pltpu.CompilerParams(vmem_limit_bytes=VMEM_LIMIT),
    )(*args[:n_smem], *[x if i + n_smem in free else in_hbm(x) for i, x in enumerate(args[n_smem:])])


def project_kernel(pos_ref, *refs):
    blocks, mine_ref, theirs_ref, outs, (first, second, out_ref) = refs[:8], refs[8], refs[9], refs[10:15], refs[15:]
    core = pos_ref[1]
    one = jnp.where(core == 0, mine_ref[...], theirs_ref[...])
    two = jnp.where(core == 0, theirs_ref[...], mine_ref[...])
    first[:, 0:256] = one[:, 0:256]
    first[:, 256:512] = two[:, 0:256]
    first[:, 512:640] = jnp.concatenate([one[:, 256:288], two[:, 256:288], jnp.zeros((448, 64), BF)], axis=1)
    second[0:64, :] = jnp.zeros((64, 640), BF)
    second[64:512, 0:128] = jnp.concatenate([jnp.zeros((448, 64), BF), one[:, 256:288], two[:, 256:288]], axis=1)
    second[64:512, 128:384] = one[:, 0:256]
    second[64:512, 384:640] = two[:, 0:256]
    for shift in range(4):
        slot = lax.rem(pos_ref[0] + 8 - shift - pos_ref[3], 4)
        for part in range(2):
            block = blocks[2 * shift + part]
            a = dot(block[:, 0:448], first[...])
            b = dot(block[:, 384:896], second[...])
            at = slice(part * 128, (part + 1) * 128)
            out_ref[slot, at, 0:512] = a[:, 0:512].astype(BF)
            out_ref[slot, at, 512:640] = (a[:, 512:640] + b[:, 0:128]).astype(BF)
            out_ref[slot, at, 640:1152] = b[:, 128:640].astype(BF)
    outs[0][...] = out_ref[0]
    outs[1][...] = out_ref[1]
    outs[2][...] = out_ref[2, 0:128]
    outs[3][...] = out_ref[2, 128:256]
    outs[4][...] = out_ref[3]


def sum_kernel(pos_ref, p0, p1, p3, top, low, own_ref, oth_ref):
    core = pos_ref[1]

    def total(lo, hi):
        acc = jnp.concatenate([top[:, lo:hi], low[:, lo:hi]], axis=0).astype(F32)
        for ref in (p0, p1, p3):
            acc = acc + ref[:, lo:hi].astype(F32)
        return acc.astype(BF)

    keys = total(512, 640)
    for t in range(2):
        at = slice(t * 256, (t + 1) * 256)
        one, two = total(t * 640, t * 640 + 256), total(t * 640 + 256, t * 640 + 512)
        own_ref[at, 0:256] = jnp.where(core == 0, one, two)
        oth_ref[at, 0:256] = jnp.where(core == 0, two, one)
        one, two = keys[:, t * 64 : t * 64 + 32], keys[:, t * 64 + 32 : t * 64 + 64]
        own_ref[at, 256:288] = jnp.where(core == 0, one, two)
        oth_ref[at, 256:288] = jnp.where(core == 0, two, one)


def group_kernel(pos_ref, g_ref, s_ref, own_ref, rec_ref, place_ref, send_ref, keep_ref, grouped):
    core = pos_ref[1]
    me = pos_ref[2]
    rows, cols = iota((256, 128), 0), iota((256, 128), 1)
    acc = None
    for e, ref in enumerate((own_ref, rec_ref)):
        half = core if e == 0 else 1 - core
        queries = None
        for t in range(2):
            pick = onehot((rows >= 224) & (cols == rows - 224 + 32 * t))
            part = dot(ref[t * 256 : (t + 1) * 256, 0:256], pick)
            queries = part if queries is None else queries + part
        hot = onehot(iota((512, 256), 0) == place_ref[half])
        part = dot(hot, queries.astype(BF))
        acc = part if acc is None else acc + part
    grouped[...] = acc.astype(BF)
    send_ref[...] = jnp.zeros_like(send_ref)
    keep_ref[...] = jnp.zeros_like(keep_ref)
    for p in range(32):
        holder, slot = g_ref[p], s_ref[p]

        @pl.when(holder != me)
        def _():
            send_ref[holder] = grouped[p * 16 : (p + 1) * 16, :]

        @pl.when(holder == me)
        def _():
            keep_ref[slot] = grouped[p * 16 : (p + 1) * 16, :]


def slot_kernel(pos_ref, owner_ref, rec_ref, keep_ref, state_ref, norm_ref, send_ref, own_ref, buf):
    me = pos_ref[2]
    step = pl.program_id(0)

    @pl.when(step == 0)
    def _():
        send_ref[...] = jnp.zeros_like(send_ref)
        own_ref[...] = jnp.zeros_like(own_ref)

    for i in range(8):
        slot = step * 8 + i
        owner = owner_ref[slot]

        @pl.when(owner != me)
        def _():
            buf[i * 16 : (i + 1) * 16, :] = rec_ref[owner]

        @pl.when(owner == me)
        def _():
            buf[i * 16 : (i + 1) * 16, :] = keep_ref[slot]

    q = buf[...]
    row, f = iota((128, 384), 0), iota((128, 384), 1)
    lane = iota((1, 384), 1)
    square, line = lane >= 17, (lane >= 1) & (lane < 17)
    unit_a = jnp.where(lane == 0, 1.0, 0.0)
    unit_b = jnp.where(lane < 17, 1.0, 0.0)
    scale = jnp.where(square, 0.5**0.5 / 4.0, jnp.where(line, 0.5, 1.0))
    scale = jnp.where(lane < 273, scale, 0.0)
    a_at = jnp.where(f >= 17, lax.shift_right_logical(f - 17, 4), f - 1)
    b_at = (f - 17) & 15
    live_a = (f >= 1) & (f < 273)
    live_b = (f >= 17) & (f < 273)
    r, c = iota((128, 16), 0), iota((128, 16), 1)
    den_lane = iota((128, 32), 1)
    phis, dens = [], []
    for t in range(2):
        tile = jnp.zeros((128, 32), F32)
        for h in range(2):
            base = t * 32 + h * 16
            left = dot(q, onehot(live_a & (row == a_at + base))) + unit_a
            right = dot(q, onehot(live_b & (row == b_at + base))) + unit_b
            phi = left * right * scale
            norm = dot(onehot(2 * lax.shift_right_logical(r, 4) + h == c), norm_ref[...])
            den = jnp.sum(phi * norm, axis=1, keepdims=True)
            rough = den.astype(BF).astype(F32)
            tile = jnp.where(den_lane == h, rough, jnp.where(den_lane == h + 2, den - rough, tile))
            phis.append(phi.astype(BF))
        dens.append(tile.astype(BF))
    first_head = iota((16, 224), 1) < 112
    for i in range(8):
        at = slice(i * 16, (i + 1) * 16)
        phi = jnp.concatenate([x[at, 0:273] for x in phis], axis=0)
        terms = dot(phi, state_ref[i])
        results = [
            jnp.where(first_head, terms[t * 32 : t * 32 + 16], terms[t * 32 + 16 : t * 32 + 32]).astype(BF) for t in range(2)
        ]
        slot = step * 8 + i
        owner = owner_ref[slot]

        @pl.when(owner != me)
        def _():
            for t in range(2):
                send_ref[owner, :, t * 256 : t * 256 + 224] = results[t]
                send_ref[owner, :, t * 256 + 224 : t * 256 + 256] = dens[t][at]

        @pl.when(owner == me)
        def _():
            for t in range(2):
                own_ref[slot, :, t * 256 : t * 256 + 224] = results[t]
                own_ref[slot, :, t * 256 + 224 : t * 256 + 256] = dens[t][at]


def kappa(s):
    return 1.0 + s + 0.5 * s * s


def tail_kernel(pos_ref, own_ref, rec_ref, tk_ref, tv_ref, len_ref, num_ref):
    core = pos_ref[1]
    r, c = iota((256, 256), 0), iota((256, 256), 1)
    expand_q = onehot((r >= 224) & (r - 224 == lax.shift_right_logical(c, 7) * 16 + (c & 15)))
    r, c = iota((256, 128), 0), iota((256, 128), 1)
    sum_a = onehot(lax.shift_right_logical(r, 4) == c)
    pick_q = onehot((r >= 224) & (r - 224 == c))
    r, c = iota((128, 128), 0), iota((128, 128), 1)
    pick_k = onehot(iota((32, 128), 0) == iota((32, 128), 1))
    sum_new = onehot((r < 32) & (lax.shift_right_logical(r, 4) == c))
    r, c = iota((128, 1792), 0), iota((128, 1792), 1)
    expand_w = onehot((r < 16) & (c >= r * 112) & (c < (r + 1) * 112))
    r, c = iota((1792, 256), 0), iota((1792, 256), 1)
    sum_v = onehot(
        functools.reduce(
            jnp.logical_or,
            [(r - c == 112 * (7 * (k // 8) + k % 8)) & (c >= 112 * (k // 8)) & (c < 112 * (k // 8 + 1)) for k in range(16)],
        )
    )
    r, c = iota((128, 256), 0), iota((128, 256), 1)
    den_at = onehot((r < 16) & (c == 224 + lax.shift_right_logical(r, 3)))
    den_new = onehot((r < 2) & (c == 224 + r))
    spread_new = onehot((r < 2) & (c < 224) & ((c >= 112) == (r >= 1)))
    head_lane = iota((256, 128), 1)
    for e, ref in enumerate((own_ref, rec_ref)):
        half = core if e == 0 else 1 - core
        at = pl.multiple_of(half * 256, 256)
        keys = tk_ref[pl.ds(at, 256), :].astype(F32)
        live = (head_lane & 7) < len_ref[pl.ds(at, 256), :]
        live = live & (head_lane < 16)
        values = tv_ref[pl.ds(at, 256), :]
        new_keys = [dot(ref[t * 256 : (t + 1) * 256, 256:288], pick_k) for t in range(2)]
        for t in range(2):
            vq = ref[t * 256 : (t + 1) * 256, 0:256]
            one, two = split(dot(vq, expand_q) * keys)
            weight = kappa((dot(one, sum_a) + dot(two, sum_a)) * 0.25)
            weight = jnp.where(live, weight, 0.0)
            one, two = split(weight)
            terms = dot(one, expand_w).astype(BF) * values
            num = dot(terms, sum_v) + (dot(one, den_at) + dot(two, den_at))
            query = dot(vq, pick_q)
            for i in range(t + 1):
                one, two = split(query * new_keys[i])
                weight = kappa((dot(one, sum_new) + dot(two, sum_new)) * 0.25)
                one, two = split(weight)
                num = num + dot(one, spread_new) * ref[i * 256 : (i + 1) * 256, 0:256].astype(F32)
                num = num + (dot(one, den_new) + dot(two, den_new))
            num_ref[e, t * 256 : (t + 1) * 256, :] = num


def combine_kernel(pos_ref, g_ref, s_ref, num_ref, rec_ref, own_ref, place_ref, out_ref, buf):
    core = pos_ref[1]
    me = pos_ref[2]
    for p in range(32):
        holder, slot = g_ref[p], s_ref[p]

        @pl.when(holder != me)
        def _():
            buf[p * 16 : (p + 1) * 16, :] = rec_ref[holder]

        @pl.when(holder == me)
        def _():
            buf[p * 16 : (p + 1) * 16, :] = own_ref[slot]

    r, c = iota((256, 256), 0), iota((256, 256), 1)
    spread = onehot((c < 224) & (((c < 112) & ((r == 224) | (r == 226))) | ((c >= 112) & ((r == 225) | (r == 227)))))
    lane = iota((256, 256), 1)
    for e in range(2):
        half = core if e == 0 else 1 - core
        at = pl.multiple_of(half * 256, 256)
        hot = onehot(iota((256, 512), 1) == place_ref[pl.ds(at, 256), :])
        prompt = dot(hot, buf[...])
        for t in range(2):
            num = num_ref[e, t * 256 : (t + 1) * 256, :] + prompt[:, t * 256 : (t + 1) * 256]
            one, two = split(num)
            den = dot(one, spread) + dot(two, spread)
            out = jnp.where(lane < 224, num / jnp.where(lane < 224, den, 1.0), 0.0)
            out = out.astype(BF)
            for part in range(2):
                out_ref[half * 2 + part, t * 128 : (t + 1) * 128, :] = out[part * 128 : (part + 1) * 128]


def out_kernel(pos_ref, own_ref, oth_ref, *refs):
    parts, first_ref, second_ref = refs[:8], refs[8], refs[9]
    y, core, col = pos_ref[0], pos_ref[1], pos_ref[3]
    acc = [None, None]
    for shift in range(4):
        j = lax.rem(y + 4 - shift, 4)
        for which, ref in enumerate((own_ref, oth_ref)):
            k = core if which == 0 else 1 - core
            heads = ref[j, :, 0:224]
            for e in range(2):
                at = jnp.bitwise_xor(k, lax.rem(col, 2))
                part = dot(heads, parts[2 * shift + e][at])
                acc[e] = part if acc[e] is None else acc[e] + part
    same = lax.rem(y, 2) == lax.div(col, 2)
    first_ref[...] = jnp.where(same, acc[0], acc[1]).astype(BF)
    second_ref[...] = jnp.where(same, acc[1], acc[0]).astype(BF)


def body(tokens, w_query, w_key, w_value, w_out, cached_state, cached_norm, slot_prompt, prompt_of, tail_keys, tail_values, tail_length):
    y, core, col = lax.axis_index("y"), lax.axis_index("core"), lax.axis_index("col")
    me = lax.axis_index(("req", "col"))
    pos = jnp.stack([y, core, me, col]).astype(jnp.int32)
    def over_y(x, step):
        return lax.ppermute(x, "y", [(i, (i + step) % 4) for i in range(4)])

    top, low = tokens[:128].reshape(128, 896), tokens[128:].reshape(128, 896)
    top_1, low_3 = over_y(top, 1), over_y(low, 3)
    low_1, top_3 = over_y(low, 1), over_y(top, 3)
    blocks = [top, low, top_1, low_1, over_y(top_1, 1), over_y(low_3, 3), top_3, low_3]
    value_w = jnp.moveaxis(w_value.reshape(2, 448, 112), 0, 1).reshape(448, 224)
    mine = jnp.concatenate([value_w, w_query, w_key], axis=1)
    theirs = lax.ppermute(mine, "core", [(0, 1), (1, 0)])
    owner = slot_prompt // 32
    slots = jnp.arange(32, dtype=jnp.int32)
    away = owner != me
    code = jnp.max(
        jnp.where((owner[None, :] == slots[:, None]) & away[None, :], (slots * 32 + slot_prompt % 32 + 1)[None, :], 0), axis=1
    )
    told = lax.all_to_all(code[:, None], ("req", "col"), split_axis=0, concat_axis=0, tiled=True)[:, 0]
    here = (slot_prompt[None, :] == (me * 32 + slots)[:, None])
    there = (told[None, :] > 0) & ((told[None, :] - 1) % 32 == slots[:, None])
    at_slot = jnp.max(jnp.where(here, slots[None, :], 0), axis=1)
    at_holder = jnp.where(jnp.any(here, axis=1), me, jnp.max(jnp.where(there, slots[None, :], 0), axis=1)).astype(jnp.int32)
    index = jnp.arange(512)
    rank = jnp.sum(((prompt_of[None, :] == prompt_of[:, None]) & (index[None, :] < index[:, None])).astype(jnp.int32), axis=1)
    place = (prompt_of - me * 32) * 16 + rank
    norms = jnp.pad(jnp.transpose(cached_norm, (0, 2, 1)).reshape(64, 273), ((0, 0), (0, 111)))
    states = cached_state[0].reshape(273, 224, 32)

    partial = call(
        project_kernel,
        [jax.ShapeDtypeStruct((n, 1152), BF) for n in (256, 256, 128, 128, 256)],
        1,
        pos,
        *blocks,
        mine,
        theirs,
        scratch=[pltpu.VMEM((448, 640), BF), pltpu.VMEM((512, 640), BF), pltpu.VMEM((4, 256, 1152), BF)],
        free=range(1, 11),
    )
    here_0, to_1, to_2, to_2_low, to_3 = partial

    def over_x(x, step):
        return lax.ppermute(x, "col", [(i, (i + step) % 4) for i in range(4)])

    from_1, from_3 = over_x(to_1, 1), over_x(to_3, 3)
    half_1, half_3 = over_x(to_2, 1), over_x(to_2_low, 3)
    half_1, half_3, w_out = lax.optimization_barrier((half_1, half_3, w_out))
    half_1, half_3 = over_x(half_1, 1), over_x(half_3, 3)
    pieces = []
    for s in range(4):
        perm = [(k * 4 + c, (c >> 1) * 4 + (s ^ (2 * (c & 1) + k))) for k in range(2) for c in range(4)]
        pieces.append(lax.ppermute(w_out, ("core", "col"), perm))
    pieces = [jnp.stack(pieces[:2]), jnp.stack(pieces[2:])]
    out_w = [over_y(x, step) for step in (1, 3) for x in pieces]
    partial = [here_0, from_1, from_3, half_1, half_3]
    partial, states, norms = lax.optimization_barrier((partial, states, norms))
    states = jnp.transpose(states, (2, 0, 1))
    shape = jax.ShapeDtypeStruct((512, 288), BF)
    own, oth = call(sum_kernel, (shape, shape), 1, pos, *partial, free=range(1, 6))
    rec = lax.ppermute(oth, "core", [(0, 1), (1, 0)])

    shape = jax.ShapeDtypeStruct((32, 16, 128), BF)
    q_send, q_keep = call(
        group_kernel,
        (shape, shape),
        3,
        pos,
        at_holder,
        at_slot,
        own,
        rec,
        place.reshape(2, 1, 256),
        scratch=[pltpu.VMEM((512, 128), BF)],
        free=(3, 4),
    )
    q_rec = lax.all_to_all(q_send, ("req", "col"), split_axis=0, concat_axis=0, tiled=True)
    shape = jax.ShapeDtypeStruct((2, 512, 256), F32)
    num = call(tail_kernel, shape, 1, pos, own, rec, tail_keys, tail_values, tail_length[:, None], free=(1, 2), pin=False)
    q_rec, out_w = lax.optimization_barrier((q_rec, out_w))
    shape = jax.ShapeDtypeStruct((32, 16, 512), BF)
    whole = pl.BlockSpec((32, 16, 128), lambda i: (0, 0, 0))
    whole_out = pl.BlockSpec((32, 16, 512), lambda i: (0, 0, 0))
    r_send, r_keep = pl.pallas_call(
        slot_kernel,
        grid=(4,),
        out_shape=(pltpu.HBM(shape.shape, BF), pltpu.HBM(shape.shape, BF)),
        in_specs=[
            SM,
            SM,
            whole,
            whole,
            pl.BlockSpec((8, 273, 224), lambda i: (i, 0, 0)),
            pl.BlockSpec((16, 384), lambda i: (i, 0)),
        ],
        out_specs=(whole_out, whole_out),
        scratch_shapes=[pltpu.VMEM((128, 128), BF)],
        compiler_params=pltpu.CompilerParams(vmem_limit_bytes=VMEM_LIMIT),
    )(pos, owner, in_hbm(q_rec), in_hbm(q_keep), in_hbm(states), in_hbm(norms))
    r_send, near_1, near_3 = lax.optimization_barrier((r_send, out_w[0], out_w[3]))
    far_1, far_3 = over_y(near_1, 1), over_y(near_3, 3)
    r_rec = lax.all_to_all(r_send, ("req", "col"), split_axis=0, concat_axis=0, tiled=True)
    r_rec, num, far_1, far_3 = lax.optimization_barrier((r_rec, num, far_1, far_3))
    heads = call(
        combine_kernel,
        jax.ShapeDtypeStruct((4, 256, 256), BF),
        3,
        pos,
        at_holder,
        at_slot,
        num,
        r_rec,
        r_keep,
        place[:, None],
        scratch=[pltpu.VMEM((512, 512), BF)],
        free=range(3, 7),
    )
    heads = lax.all_to_all(heads, "y", split_axis=0, concat_axis=0, tiled=True)
    heads_oth = lax.ppermute(heads, "core", [(0, 1), (1, 0)])
    shape = jax.ShapeDtypeStruct((256, 448), BF)
    mixed = call(out_kernel, (shape, shape), 1, pos, heads, heads_oth, *pieces, out_w[0], out_w[1], far_1, far_3, out_w[2], out_w[3], free=range(1, 11))

    def at(y, core, col):
        return (y * 2 + core) * 4 + col

    got = []
    for s, part in enumerate(mixed):
        perm = [
            (at(j, k, b), at(b, j >> 1, 2 * k + (s ^ (j & 1)))) for b in range(4) for j in range(4) for k in range(2)
        ]
        got.append(lax.ppermute(part, ("y", "core", "col"), perm).reshape(2, 128, 448))
    odd = col % 2 == 1
    mixed = jnp.concatenate([jnp.where(odd, got[1], got[0]), jnp.where(odd, got[0], got[1])], axis=1)
    mixed = jnp.transpose(mixed, (1, 0, 2)).astype(F32)
    return (mixed + tokens.astype(F32)).astype(BF)


def solution(mesh):
    inner = Mesh(mesh.devices.reshape(8, 4, 2, 4), ("req", "y", "core", "col"))
    rows = ("y", "core")
    hold = ("req", "col")
    return jax.shard_map(
        body,
        mesh=inner,
        in_specs=(
            P(("req", "y", "core"), None, "col"),
            P("col", rows),
            P("col", rows),
            P(rows, "col"),
            P(rows, "col"),
            P(hold, None, rows),
            P(hold, None, rows),
            P(hold),
            P(hold),
            P(hold, rows),
            P(hold, rows),
            P(hold),
        ),
        out_specs=P(("req", "y", "core"), None, "col"),
        check_vma=False,
    )
```

```python
import functools

import jax
import jax.numpy as jnp
from jax import lax
from jax.experimental import pallas as pl
from jax.experimental.pallas import tpu as pltpu
from jax.sharding import Mesh, PartitionSpec as P

BF = jnp.bfloat16
F32 = jnp.float32
VMEM_LIMIT = 48 * 1024 * 1024
SM = pl.BlockSpec(memory_space=pltpu.SMEM)


def dot(a, b):
    return jnp.dot(a, b, preferred_element_type=F32)


def iota(shape, dim):
    return lax.broadcasted_iota(jnp.int32, shape, dim)


def onehot(cond):
    return jnp.where(cond, 1.0, 0.0).astype(BF)


def split(x):
    high = x.astype(BF)
    return high, (x - high.astype(F32)).astype(BF)


def in_hbm(x):
    return pltpu.with_memory_space_constraint(x, pltpu.HBM)


def call(kernel, out_shapes, n_smem, *args, scratch=(), free=(), pin=True):
    def full(shape):
        zeros = (0,) * len(shape)
        return pl.BlockSpec(shape, lambda i: zeros)

    return pl.pallas_call(
        kernel,
        grid=(1,),
        out_shape=jax.tree.map(lambda x: pltpu.HBM(x.shape, x.dtype), out_shapes) if pin else out_shapes,
        in_specs=[SM] * n_smem + [full(x.shape) for x in args[n_smem:]],
        out_specs=jax.tree.map(lambda x: full(x.shape), out_shapes),
        scratch_shapes=scratch,
        compiler_params=pltpu.CompilerParams(vmem_limit_bytes=VMEM_LIMIT),
    )(*args[:n_smem], *[x if i + n_smem in free else in_hbm(x) for i, x in enumerate(args[n_smem:])])


def project_kernel(pos_ref, *refs):
    blocks, mine_ref, theirs_ref, out_ref, first, second = refs[:8], refs[8], refs[9], refs[10], refs[11], refs[12]
    core = pos_ref[1]
    one = jnp.where(core == 0, mine_ref[...], theirs_ref[...])
    two = jnp.where(core == 0, theirs_ref[...], mine_ref[...])
    first[:, 0:256] = one[:, 0:256]
    first[:, 256:512] = two[:, 0:256]
    first[:, 512:640] = jnp.concatenate([one[:, 256:288], two[:, 256:288], jnp.zeros((448, 64), BF)], axis=1)
    second[0:64, :] = jnp.zeros((64, 640), BF)
    second[64:512, 0:128] = jnp.concatenate([jnp.zeros((448, 64), BF), one[:, 256:288], two[:, 256:288]], axis=1)
    second[64:512, 128:384] = one[:, 0:256]
    second[64:512, 384:640] = two[:, 0:256]
    for shift in range(4):
        slot = lax.rem(pos_ref[0] + 4 - shift, 4)
        for part in range(2):
            block = blocks[2 * shift + part]
            a = dot(block[:, 0:448], first[...])
            b = dot(block[:, 384:896], second[...])
            at = slice(part * 128, (part + 1) * 128)
            out_ref[slot, at, 0:512] = a[:, 0:512].astype(BF)
            out_ref[slot, at, 512:640] = (a[:, 512:640] + b[:, 0:128]).astype(BF)
            out_ref[slot, at, 640:1152] = b[:, 128:640].astype(BF)


def sum_kernel(pos_ref, p_ref, own_ref, oth_ref):
    core = pos_ref[1]

    def total(lo, hi):
        acc = p_ref[0, :, lo:hi].astype(F32)
        for i in range(1, 4):
            acc = acc + p_ref[i, :, lo:hi].astype(F32)
        return acc.astype(BF)

    keys = total(512, 640)
    for t in range(2):
        at = slice(t * 256, (t + 1) * 256)
        one, two = total(t * 640, t * 640 + 256), total(t * 640 + 256, t * 640 + 512)
        own_ref[at, 0:256] = jnp.where(core == 0, one, two)
        oth_ref[at, 0:256] = jnp.where(core == 0, two, one)
        one, two = keys[:, t * 64 : t * 64 + 32], keys[:, t * 64 + 32 : t * 64 + 64]
        own_ref[at, 256:288] = jnp.where(core == 0, one, two)
        oth_ref[at, 256:288] = jnp.where(core == 0, two, one)


def group_kernel(pos_ref, g_ref, s_ref, own_ref, rec_ref, place_ref, send_ref, keep_ref, grouped):
    core = pos_ref[1]
    me = pos_ref[2]
    rows, cols = iota((256, 128), 0), iota((256, 128), 1)
    acc = None
    for e, ref in enumerate((own_ref, rec_ref)):
        half = core if e == 0 else 1 - core
        queries = None
        for t in range(2):
            pick = onehot((rows >= 224) & (cols == rows - 224 + 32 * t))
            part = dot(ref[t * 256 : (t + 1) * 256, 0:256], pick)
            queries = part if queries is None else queries + part
        hot = onehot(iota((512, 256), 0) == place_ref[half])
        part = dot(hot, queries.astype(BF))
        acc = part if acc is None else acc + part
    grouped[...] = acc.astype(BF)
    send_ref[...] = jnp.zeros_like(send_ref)
    keep_ref[...] = jnp.zeros_like(keep_ref)
    for p in range(32):
        holder, slot = g_ref[p], s_ref[p]

        @pl.when(holder != me)
        def _():
            send_ref[holder] = grouped[p * 16 : (p + 1) * 16, :]

        @pl.when(holder == me)
        def _():
            keep_ref[slot] = grouped[p * 16 : (p + 1) * 16, :]


def slot_kernel(pos_ref, owner_ref, rec_ref, keep_ref, state_ref, norm_ref, send_ref, own_ref, buf):
    me = pos_ref[2]
    step = pl.program_id(0)

    @pl.when(step == 0)
    def _():
        send_ref[...] = jnp.zeros_like(send_ref)
        own_ref[...] = jnp.zeros_like(own_ref)

    for i in range(8):
        slot = step * 8 + i
        owner = owner_ref[slot]

        @pl.when(owner != me)
        def _():
            buf[i * 16 : (i + 1) * 16, :] = rec_ref[owner]

        @pl.when(owner == me)
        def _():
            buf[i * 16 : (i + 1) * 16, :] = keep_ref[slot]

    q = buf[...]
    row, f = iota((128, 384), 0), iota((128, 384), 1)
    lane = iota((1, 384), 1)
    square, line = lane >= 17, (lane >= 1) & (lane < 17)
    unit_a = jnp.where(lane == 0, 1.0, 0.0)
    unit_b = jnp.where(lane < 17, 1.0, 0.0)
    scale = jnp.where(square, 0.5**0.5 / 4.0, jnp.where(line, 0.5, 1.0))
    scale = jnp.where(lane < 273, scale, 0.0)
    a_at = jnp.where(f >= 17, lax.shift_right_logical(f - 17, 4), f - 1)
    b_at = (f - 17) & 15
    live_a = (f >= 1) & (f < 273)
    live_b = (f >= 17) & (f < 273)
    r, c = iota((128, 16), 0), iota((128, 16), 1)
    den_lane = iota((128, 32), 1)
    phis, dens = [], []
    for t in range(2):
        tile = jnp.zeros((128, 32), F32)
        for h in range(2):
            base = t * 32 + h * 16
            left = dot(q, onehot(live_a & (row == a_at + base))) + unit_a
            right = dot(q, onehot(live_b & (row == b_at + base))) + unit_b
            phi = left * right * scale
            norm = dot(onehot(2 * lax.shift_right_logical(r, 4) + h == c), norm_ref[...])
            den = jnp.sum(phi * norm, axis=1, keepdims=True)
            rough = den.astype(BF).astype(F32)
            tile = jnp.where(den_lane == h, rough, jnp.where(den_lane == h + 2, den - rough, tile))
            phis.append(phi.astype(BF))
        dens.append(tile.astype(BF))
    first_head = iota((16, 224), 1) < 112
    for i in range(8):
        at = slice(i * 16, (i + 1) * 16)
        phi = jnp.concatenate([x[at, 0:273] for x in phis], axis=0)
        terms = dot(phi, state_ref[i])
        results = [
            jnp.where(first_head, terms[t * 32 : t * 32 + 16], terms[t * 32 + 16 : t * 32 + 32]).astype(BF) for t in range(2)
        ]
        slot = step * 8 + i
        owner = owner_ref[slot]

        @pl.when(owner != me)
        def _():
            for t in range(2):
                send_ref[owner, :, t * 256 : t * 256 + 224] = results[t]
                send_ref[owner, :, t * 256 + 224 : t * 256 + 256] = dens[t][at]

        @pl.when(owner == me)
        def _():
            for t in range(2):
                own_ref[slot, :, t * 256 : t * 256 + 224] = results[t]
                own_ref[slot, :, t * 256 + 224 : t * 256 + 256] = dens[t][at]


def kappa(s):
    return 1.0 + s + 0.5 * s * s


def tail_kernel(pos_ref, own_ref, rec_ref, tk_ref, tv_ref, len_ref, num_ref):
    core = pos_ref[1]
    r, c = iota((256, 256), 0), iota((256, 256), 1)
    expand_q = onehot((r >= 224) & (r - 224 == lax.shift_right_logical(c, 7) * 16 + (c & 15)))
    r, c = iota((256, 128), 0), iota((256, 128), 1)
    sum_a = onehot(lax.shift_right_logical(r, 4) == c)
    pick_q = onehot((r >= 224) & (r - 224 == c))
    r, c = iota((128, 128), 0), iota((128, 128), 1)
    pick_k = onehot(iota((32, 128), 0) == iota((32, 128), 1))
    sum_new = onehot((r < 32) & (lax.shift_right_logical(r, 4) == c))
    r, c = iota((128, 1792), 0), iota((128, 1792), 1)
    expand_w = onehot((r < 16) & (c >= r * 112) & (c < (r + 1) * 112))
    r, c = iota((1792, 256), 0), iota((1792, 256), 1)
    sum_v = onehot(
        functools.reduce(
            jnp.logical_or,
            [(r - c == 112 * (7 * (k // 8) + k % 8)) & (c >= 112 * (k // 8)) & (c < 112 * (k // 8 + 1)) for k in range(16)],
        )
    )
    r, c = iota((128, 256), 0), iota((128, 256), 1)
    den_at = onehot((r < 16) & (c == 224 + lax.shift_right_logical(r, 3)))
    den_new = onehot((r < 2) & (c == 224 + r))
    spread_new = onehot((r < 2) & (c < 224) & ((c >= 112) == (r >= 1)))
    head_lane = iota((256, 128), 1)
    for e, ref in enumerate((own_ref, rec_ref)):
        half = core if e == 0 else 1 - core
        at = pl.multiple_of(half * 256, 256)
        keys = tk_ref[pl.ds(at, 256), :].astype(F32)
        live = (head_lane & 7) < len_ref[pl.ds(at, 256), :]
        live = live & (head_lane < 16)
        values = tv_ref[pl.ds(at, 256), :]
        new_keys = [dot(ref[t * 256 : (t + 1) * 256, 256:288], pick_k) for t in range(2)]
        for t in range(2):
            vq = ref[t * 256 : (t + 1) * 256, 0:256]
            one, two = split(dot(vq, expand_q) * keys)
            weight = kappa((dot(one, sum_a) + dot(two, sum_a)) * 0.25)
            weight = jnp.where(live, weight, 0.0)
            one, two = split(weight)
            terms = dot(one, expand_w).astype(BF) * values
            num = dot(terms, sum_v) + (dot(one, den_at) + dot(two, den_at))
            query = dot(vq, pick_q)
            for i in range(t + 1):
                one, two = split(query * new_keys[i])
                weight = kappa((dot(one, sum_new) + dot(two, sum_new)) * 0.25)
                one, two = split(weight)
                num = num + dot(one, spread_new) * ref[i * 256 : (i + 1) * 256, 0:256].astype(F32)
                num = num + (dot(one, den_new) + dot(two, den_new))
            num_ref[e, t * 256 : (t + 1) * 256, :] = num


def combine_kernel(pos_ref, g_ref, s_ref, num_ref, rec_ref, own_ref, place_ref, out_ref, buf):
    core = pos_ref[1]
    me = pos_ref[2]
    for p in range(32):
        holder, slot = g_ref[p], s_ref[p]

        @pl.when(holder != me)
        def _():
            buf[p * 16 : (p + 1) * 16, :] = rec_ref[holder]

        @pl.when(holder == me)
        def _():
            buf[p * 16 : (p + 1) * 16, :] = own_ref[slot]

    r, c = iota((256, 256), 0), iota((256, 256), 1)
    spread = onehot((c < 224) & (((c < 112) & ((r == 224) | (r == 226))) | ((c >= 112) & ((r == 225) | (r == 227)))))
    lane = iota((256, 256), 1)
    for e in range(2):
        half = core if e == 0 else 1 - core
        at = pl.multiple_of(half * 256, 256)
        hot = onehot(iota((256, 512), 1) == place_ref[pl.ds(at, 256), :])
        prompt = dot(hot, buf[...])
        for t in range(2):
            num = num_ref[e, t * 256 : (t + 1) * 256, :] + prompt[:, t * 256 : (t + 1) * 256]
            one, two = split(num)
            den = dot(one, spread) + dot(two, spread)
            out = jnp.where(lane < 224, num / jnp.where(lane < 224, den, 1.0), 0.0)
            out = out.astype(BF)
            for part in range(2):
                out_ref[half * 2 + part, t * 128 : (t + 1) * 128, :] = out[part * 128 : (part + 1) * 128]


def out_kernel(pos_ref, own_ref, oth_ref, *refs):
    w0, w1, far_1, far_3, w3, first_ref, second_ref = refs
    y, core, col = pos_ref[0], pos_ref[1], pos_ref[3]
    acc = [None, None]
    for shift in range(4):
        j = lax.rem(y + 4 - shift, 4)
        for which, ref in enumerate((own_ref, oth_ref)):
            k = core if which == 0 else 1 - core
            heads = ref[j, :, 0:224]
            for e in range(2):
                at = jnp.bitwise_xor(k, lax.rem(col, 2))
                w = (far_1, far_3)[e][at] if shift == 2 else (w0, w1, None, w3)[shift][2 * e + at]
                part = dot(heads, w)
                acc[e] = part if acc[e] is None else acc[e] + part
    same = lax.rem(y, 2) == lax.div(col, 2)
    first_ref[...] = jnp.where(same, acc[0], acc[1]).astype(BF)
    second_ref[...] = jnp.where(same, acc[1], acc[0]).astype(BF)


def body(tokens, w_query, w_key, w_value, w_out, cached_state, cached_norm, slot_prompt, prompt_of, tail_keys, tail_values, tail_length):
    y, core, col = lax.axis_index("y"), lax.axis_index("core"), lax.axis_index("col")
    me = lax.axis_index(("req", "col"))
    pos = jnp.stack([y, core, me, col]).astype(jnp.int32)
    def over_y(x, step):
        return lax.ppermute(x, "y", [(i, (i + step) % 4) for i in range(4)])

    top, low = tokens[:128].reshape(128, 896), tokens[128:].reshape(128, 896)
    top_1, low_3 = over_y(top, 1), over_y(low, 3)
    low_1, top_3 = over_y(low, 1), over_y(top, 3)
    top_1, low_3, w_out = lax.optimization_barrier((top_1, low_3, w_out))
    blocks = [top, low, top_1, low_1, over_y(top_1, 1), over_y(low_3, 3), top_3, low_3]
    value_w = jnp.moveaxis(w_value.reshape(2, 448, 112), 0, 1).reshape(448, 224)
    mine = jnp.concatenate([value_w, w_query, w_key], axis=1)
    theirs = lax.ppermute(mine, "core", [(0, 1), (1, 0)])
    pieces = []
    for s in range(4):
        perm = [(k * 4 + c, (c >> 1) * 4 + (s ^ (2 * (c & 1) + k))) for k in range(2) for c in range(4)]
        pieces.append(lax.ppermute(w_out, ("core", "col"), perm))
    mine, pieces = lax.optimization_barrier((mine, pieces))
    owner = slot_prompt // 32
    slots = jnp.arange(32, dtype=jnp.int32)
    away = owner != me
    code = jnp.max(
        jnp.where((owner[None, :] == slots[:, None]) & away[None, :], (slots * 32 + slot_prompt % 32 + 1)[None, :], 0), axis=1
    )
    told = lax.all_to_all(code[:, None], ("req", "col"), split_axis=0, concat_axis=0, tiled=True)[:, 0]
    here = (slot_prompt[None, :] == (me * 32 + slots)[:, None])
    there = (told[None, :] > 0) & ((told[None, :] - 1) % 32 == slots[:, None])
    at_slot = jnp.max(jnp.where(here, slots[None, :], 0), axis=1)
    at_holder = jnp.where(jnp.any(here, axis=1), me, jnp.max(jnp.where(there, slots[None, :], 0), axis=1)).astype(jnp.int32)
    index = jnp.arange(512)
    rank = jnp.sum(((prompt_of[None, :] == prompt_of[:, None]) & (index[None, :] < index[:, None])).astype(jnp.int32), axis=1)
    place = (prompt_of - me * 32) * 16 + rank
    norms = jnp.pad(jnp.transpose(cached_norm, (0, 2, 1)).reshape(64, 273), ((0, 0), (0, 111)))
    states = cached_state[0].reshape(273, 224, 32)

    partial = call(
        project_kernel,
        jax.ShapeDtypeStruct((4, 256, 1152), BF),
        1,
        pos,
        *blocks,
        mine,
        theirs,
        scratch=[pltpu.VMEM((448, 640), BF), pltpu.VMEM((512, 640), BF)],
        free=range(1, 11),
    )
    partial, pieces = lax.optimization_barrier((partial, pieces))
    pieces = jnp.stack(pieces)
    out_1, out_3 = over_y(pieces, 1), over_y(pieces, 3)
    partial = lax.all_to_all(partial, "col", split_axis=0, concat_axis=0, tiled=True)
    partial, states, norms = lax.optimization_barrier((partial, states, norms))
    states = jnp.transpose(states, (2, 0, 1))
    shape = jax.ShapeDtypeStruct((512, 288), BF)
    own, oth = call(sum_kernel, (shape, shape), 1, pos, partial, free=(1,))
    rec = lax.ppermute(oth, "core", [(0, 1), (1, 0)])

    shape = jax.ShapeDtypeStruct((32, 16, 128), BF)
    q_send, q_keep = call(
        group_kernel,
        (shape, shape),
        3,
        pos,
        at_holder,
        at_slot,
        own,
        rec,
        place.reshape(2, 1, 256),
        scratch=[pltpu.VMEM((512, 128), BF)],
        free=(3, 4),
    )
    q_rec = lax.all_to_all(q_send, ("req", "col"), split_axis=0, concat_axis=0, tiled=True)
    shape = jax.ShapeDtypeStruct((2, 512, 256), F32)
    num = call(tail_kernel, shape, 1, pos, own, rec, tail_keys, tail_values, tail_length[:, None], free=(1, 2), pin=False)
    q_rec, out_1, out_3 = lax.optimization_barrier((q_rec, out_1, out_3))
    shape = jax.ShapeDtypeStruct((32, 16, 512), BF)
    whole = pl.BlockSpec((32, 16, 128), lambda i: (0, 0, 0))
    whole_out = pl.BlockSpec((32, 16, 512), lambda i: (0, 0, 0))
    r_send, r_keep = pl.pallas_call(
        slot_kernel,
        grid=(4,),
        out_shape=(pltpu.HBM(shape.shape, BF), pltpu.HBM(shape.shape, BF)),
        in_specs=[
            SM,
            SM,
            whole,
            whole,
            pl.BlockSpec((8, 273, 224), lambda i: (i, 0, 0)),
            pl.BlockSpec((16, 384), lambda i: (i, 0)),
        ],
        out_specs=(whole_out, whole_out),
        scratch_shapes=[pltpu.VMEM((128, 128), BF)],
        compiler_params=pltpu.CompilerParams(vmem_limit_bytes=VMEM_LIMIT),
    )(pos, owner, in_hbm(q_rec), in_hbm(q_keep), in_hbm(states), in_hbm(norms))
    r_send, near_1, near_3 = lax.optimization_barrier((r_send, out_1, out_3))
    far_1, far_3 = over_y(near_1[:2], 1), over_y(near_3[2:], 3)
    r_rec = lax.all_to_all(r_send, ("req", "col"), split_axis=0, concat_axis=0, tiled=True)
    r_rec, num, far_1, far_3 = lax.optimization_barrier((r_rec, num, far_1, far_3))
    heads = call(
        combine_kernel,
        jax.ShapeDtypeStruct((4, 256, 256), BF),
        3,
        pos,
        at_holder,
        at_slot,
        num,
        r_rec,
        r_keep,
        place[:, None],
        scratch=[pltpu.VMEM((512, 512), BF)],
        free=range(3, 7),
    )
    heads = lax.all_to_all(heads, "y", split_axis=0, concat_axis=0, tiled=True)
    heads_oth = lax.ppermute(heads, "core", [(0, 1), (1, 0)])
    shape = jax.ShapeDtypeStruct((256, 448), BF)
    mixed = call(out_kernel, (shape, shape), 1, pos, heads, heads_oth, pieces, out_1, far_1, far_3, out_3, free=range(1, 8))

    def at(y, core, col):
        return (y * 2 + core) * 4 + col

    got = []
    for s, part in enumerate(mixed):
        perm = [
            (at(j, k, b), at(b, j >> 1, 2 * k + (s ^ (j & 1)))) for b in range(4) for j in range(4) for k in range(2)
        ]
        got.append(lax.ppermute(part, ("y", "core", "col"), perm).reshape(2, 128, 448))
    odd = col % 2 == 1
    mixed = jnp.concatenate([jnp.where(odd, got[1], got[0]), jnp.where(odd, got[0], got[1])], axis=1)
    mixed = jnp.transpose(mixed, (1, 0, 2)).astype(F32)
    return (mixed + tokens.astype(F32)).astype(BF)


def solution(mesh):
    inner = Mesh(mesh.devices.reshape(8, 4, 2, 4), ("req", "y", "core", "col"))
    rows = ("y", "core")
    hold = ("req", "col")
    return jax.shard_map(
        body,
        mesh=inner,
        in_specs=(
            P(("req", "y", "core"), None, "col"),
            P("col", rows),
            P("col", rows),
            P(rows, "col"),
            P(rows, "col"),
            P(hold, None, rows),
            P(hold, None, rows),
            P(hold),
            P(hold),
            P(hold, rows),
            P(hold, rows),
            P(hold),
        ),
        out_specs=P(("req", "y", "core"), None, "col"),
        check_vma=False,
    )
```

```python
import functools

import jax
import jax.numpy as jnp
from jax import lax
from jax.experimental import pallas as pl
from jax.experimental.pallas import tpu as pltpu
from jax.sharding import Mesh, PartitionSpec as P

BF = jnp.bfloat16
F32 = jnp.float32
VMEM_LIMIT = 48 * 1024 * 1024
SM = pl.BlockSpec(memory_space=pltpu.SMEM)


def dot(a, b):
    return jnp.dot(a, b, preferred_element_type=F32)


def iota(shape, dim):
    return lax.broadcasted_iota(jnp.int32, shape, dim)


def onehot(cond):
    return jnp.where(cond, 1.0, 0.0).astype(BF)


def split(x):
    high = x.astype(BF)
    return high, (x - high.astype(F32)).astype(BF)


def in_hbm(x):
    return pltpu.with_memory_space_constraint(x, pltpu.HBM)


def call(kernel, out_shapes, n_smem, *args, scratch=(), free=(), pin=True):
    def full(shape):
        zeros = (0,) * len(shape)
        return pl.BlockSpec(shape, lambda i: zeros)

    return pl.pallas_call(
        kernel,
        grid=(1,),
        out_shape=jax.tree.map(lambda x: pltpu.HBM(x.shape, x.dtype), out_shapes) if pin else out_shapes,
        in_specs=[SM] * n_smem + [full(x.shape) for x in args[n_smem:]],
        out_specs=jax.tree.map(lambda x: full(x.shape), out_shapes),
        scratch_shapes=scratch,
        compiler_params=pltpu.CompilerParams(vmem_limit_bytes=VMEM_LIMIT),
    )(*args[:n_smem], *[x if i + n_smem in free else in_hbm(x) for i, x in enumerate(args[n_smem:])])


def project_kernel(pos_ref, *refs):
    blocks, mine_ref, theirs_ref, out_ref, first, second = refs[:8], refs[8], refs[9], refs[10], refs[11], refs[12]
    core = pos_ref[1]
    one = jnp.where(core == 0, mine_ref[...], theirs_ref[...])
    two = jnp.where(core == 0, theirs_ref[...], mine_ref[...])
    first[:, 0:256] = one[:, 0:256]
    first[:, 256:512] = two[:, 0:256]
    first[:, 512:640] = jnp.concatenate([one[:, 256:288], two[:, 256:288], jnp.zeros((448, 64), BF)], axis=1)
    second[0:64, :] = jnp.zeros((64, 640), BF)
    second[64:512, 0:128] = jnp.concatenate([jnp.zeros((448, 64), BF), one[:, 256:288], two[:, 256:288]], axis=1)
    second[64:512, 128:384] = one[:, 0:256]
    second[64:512, 384:640] = two[:, 0:256]
    for shift in range(4):
        slot = lax.rem(pos_ref[0] + 4 - shift, 4)
        for part in range(2):
            block = blocks[2 * shift + part]
            a = dot(block[:, 0:448], first[...])
            b = dot(block[:, 384:896], second[...])
            at = slice(part * 128, (part + 1) * 128)
            out_ref[slot, at, 0:512] = a[:, 0:512].astype(BF)
            out_ref[slot, at, 512:640] = (a[:, 512:640] + b[:, 0:128]).astype(BF)
            out_ref[slot, at, 640:1152] = b[:, 128:640].astype(BF)


def sum_kernel(pos_ref, p_ref, own_ref, oth_ref):
    core = pos_ref[1]

    def total(lo, hi):
        acc = p_ref[0, :, lo:hi].astype(F32)
        for i in range(1, 4):
            acc = acc + p_ref[i, :, lo:hi].astype(F32)
        return acc.astype(BF)

    keys = total(512, 640)
    for t in range(2):
        at = slice(t * 256, (t + 1) * 256)
        one, two = total(t * 640, t * 640 + 256), total(t * 640 + 256, t * 640 + 512)
        own_ref[at, 0:256] = jnp.where(core == 0, one, two)
        oth_ref[at, 0:256] = jnp.where(core == 0, two, one)
        one, two = keys[:, t * 64 : t * 64 + 32], keys[:, t * 64 + 32 : t * 64 + 64]
        own_ref[at, 256:288] = jnp.where(core == 0, one, two)
        oth_ref[at, 256:288] = jnp.where(core == 0, two, one)


def group_kernel(pos_ref, g_ref, s_ref, own_ref, rec_ref, place_ref, send_ref, keep_ref, grouped):
    core = pos_ref[1]
    me = pos_ref[2]
    rows, cols = iota((256, 128), 0), iota((256, 128), 1)
    acc = None
    for e, ref in enumerate((own_ref, rec_ref)):
        half = core if e == 0 else 1 - core
        queries = None
        for t in range(2):
            pick = onehot((rows >= 224) & (cols == rows - 224 + 32 * t))
            part = dot(ref[t * 256 : (t + 1) * 256, 0:256], pick)
            queries = part if queries is None else queries + part
        hot = onehot(iota((512, 256), 0) == place_ref[half])
        part = dot(hot, queries.astype(BF))
        acc = part if acc is None else acc + part
    grouped[...] = acc.astype(BF)
    send_ref[...] = jnp.zeros_like(send_ref)
    keep_ref[...] = jnp.zeros_like(keep_ref)
    for p in range(32):
        holder, slot = g_ref[p], s_ref[p]

        @pl.when(holder != me)
        def _():
            send_ref[holder] = grouped[p * 16 : (p + 1) * 16, :]

        @pl.when(holder == me)
        def _():
            keep_ref[slot] = grouped[p * 16 : (p + 1) * 16, :]


def slot_kernel(pos_ref, owner_ref, rec_ref, keep_ref, state_ref, norm_ref, send_ref, own_ref, buf):
    me = pos_ref[2]
    step = pl.program_id(0)

    @pl.when(step == 0)
    def _():
        send_ref[...] = jnp.zeros_like(send_ref)
        own_ref[...] = jnp.zeros_like(own_ref)

    for i in range(8):
        slot = step * 8 + i
        owner = owner_ref[slot]

        @pl.when(owner != me)
        def _():
            buf[i * 16 : (i + 1) * 16, :] = rec_ref[owner]

        @pl.when(owner == me)
        def _():
            buf[i * 16 : (i + 1) * 16, :] = keep_ref[slot]

    q = buf[...]
    row, f = iota((128, 384), 0), iota((128, 384), 1)
    lane = iota((1, 384), 1)
    square, line = lane >= 17, (lane >= 1) & (lane < 17)
    unit_a = jnp.where(lane == 0, 1.0, 0.0)
    unit_b = jnp.where(lane < 17, 1.0, 0.0)
    scale = jnp.where(square, 0.5**0.5 / 4.0, jnp.where(line, 0.5, 1.0))
    scale = jnp.where(lane < 273, scale, 0.0)
    a_at = jnp.where(f >= 17, lax.shift_right_logical(f - 17, 4), f - 1)
    b_at = (f - 17) & 15
    live_a = (f >= 1) & (f < 273)
    live_b = (f >= 17) & (f < 273)
    r, c = iota((128, 16), 0), iota((128, 16), 1)
    den_lane = iota((128, 32), 1)
    phis, dens = [], []
    for t in range(2):
        tile = jnp.zeros((128, 32), F32)
        for h in range(2):
            base = t * 32 + h * 16
            left = dot(q, onehot(live_a & (row == a_at + base))) + unit_a
            right = dot(q, onehot(live_b & (row == b_at + base))) + unit_b
            phi = left * right * scale
            norm = dot(onehot(2 * lax.shift_right_logical(r, 4) + h == c), norm_ref[...])
            den = jnp.sum(phi * norm, axis=1, keepdims=True)
            rough = den.astype(BF).astype(F32)
            tile = jnp.where(den_lane == h, rough, jnp.where(den_lane == h + 2, den - rough, tile))
            phis.append(phi.astype(BF))
        dens.append(tile.astype(BF))
    first_head = iota((16, 224), 1) < 112
    for i in range(8):
        at = slice(i * 16, (i + 1) * 16)
        phi = jnp.concatenate([x[at, 0:273] for x in phis], axis=0)
        terms = dot(phi, state_ref[i])
        results = [
            jnp.where(first_head, terms[t * 32 : t * 32 + 16], terms[t * 32 + 16 : t * 32 + 32]).astype(BF) for t in range(2)
        ]
        slot = step * 8 + i
        owner = owner_ref[slot]

        @pl.when(owner != me)
        def _():
            for t in range(2):
                send_ref[owner, :, t * 256 : t * 256 + 224] = results[t]
                send_ref[owner, :, t * 256 + 224 : t * 256 + 256] = dens[t][at]

        @pl.when(owner == me)
        def _():
            for t in range(2):
                own_ref[slot, :, t * 256 : t * 256 + 224] = results[t]
                own_ref[slot, :, t * 256 + 224 : t * 256 + 256] = dens[t][at]


def kappa(s):
    return 1.0 + s + 0.5 * s * s


def tail_kernel(pos_ref, own_ref, rec_ref, tk_ref, tv_ref, len_ref, num_ref):
    core = pos_ref[1]
    r, c = iota((256, 256), 0), iota((256, 256), 1)
    expand_q = onehot((r >= 224) & (r - 224 == lax.shift_right_logical(c, 7) * 16 + (c & 15)))
    r, c = iota((256, 128), 0), iota((256, 128), 1)
    sum_a = onehot(lax.shift_right_logical(r, 4) == c)
    pick_q = onehot((r >= 224) & (r - 224 == c))
    r, c = iota((128, 128), 0), iota((128, 128), 1)
    pick_k = onehot(iota((32, 128), 0) == iota((32, 128), 1))
    sum_new = onehot((r < 32) & (lax.shift_right_logical(r, 4) == c))
    r, c = iota((128, 1792), 0), iota((128, 1792), 1)
    expand_w = onehot((r < 16) & (c >= r * 112) & (c < (r + 1) * 112))
    r, c = iota((1792, 256), 0), iota((1792, 256), 1)
    sum_v = onehot(
        functools.reduce(
            jnp.logical_or,
            [(r - c == 112 * (7 * (k // 8) + k % 8)) & (c >= 112 * (k // 8)) & (c < 112 * (k // 8 + 1)) for k in range(16)],
        )
    )
    r, c = iota((128, 256), 0), iota((128, 256), 1)
    den_at = onehot((r < 16) & (c == 224 + lax.shift_right_logical(r, 3)))
    den_new = onehot((r < 2) & (c == 224 + r))
    spread_new = onehot((r < 2) & (c < 224) & ((c >= 112) == (r >= 1)))
    head_lane = iota((256, 128), 1)
    for e, ref in enumerate((own_ref, rec_ref)):
        half = core if e == 0 else 1 - core
        at = pl.multiple_of(half * 256, 256)
        keys = tk_ref[pl.ds(at, 256), :].astype(F32)
        live = (head_lane & 7) < len_ref[pl.ds(at, 256), :]
        live = live & (head_lane < 16)
        values = tv_ref[pl.ds(at, 256), :]
        new_keys = [dot(ref[t * 256 : (t + 1) * 256, 256:288], pick_k) for t in range(2)]
        for t in range(2):
            vq = ref[t * 256 : (t + 1) * 256, 0:256]
            one, two = split(dot(vq, expand_q) * keys)
            weight = kappa((dot(one, sum_a) + dot(two, sum_a)) * 0.25)
            weight = jnp.where(live, weight, 0.0)
            one, two = split(weight)
            terms = dot(one, expand_w).astype(BF) * values
            num = dot(terms, sum_v) + (dot(one, den_at) + dot(two, den_at))
            query = dot(vq, pick_q)
            for i in range(t + 1):
                one, two = split(query * new_keys[i])
                weight = kappa((dot(one, sum_new) + dot(two, sum_new)) * 0.25)
                one, two = split(weight)
                num = num + dot(one, spread_new) * ref[i * 256 : (i + 1) * 256, 0:256].astype(F32)
                num = num + (dot(one, den_new) + dot(two, den_new))
            num_ref[e, t * 256 : (t + 1) * 256, :] = num


def combine_kernel(pos_ref, g_ref, s_ref, num_ref, rec_ref, own_ref, place_ref, out_ref, buf):
    core = pos_ref[1]
    me = pos_ref[2]
    for p in range(32):
        holder, slot = g_ref[p], s_ref[p]

        @pl.when(holder != me)
        def _():
            buf[p * 16 : (p + 1) * 16, :] = rec_ref[holder]

        @pl.when(holder == me)
        def _():
            buf[p * 16 : (p + 1) * 16, :] = own_ref[slot]

    r, c = iota((256, 256), 0), iota((256, 256), 1)
    spread = onehot((c < 224) & (((c < 112) & ((r == 224) | (r == 226))) | ((c >= 112) & ((r == 225) | (r == 227)))))
    lane = iota((256, 256), 1)
    for e in range(2):
        half = core if e == 0 else 1 - core
        at = pl.multiple_of(half * 256, 256)
        hot = onehot(iota((256, 512), 1) == place_ref[pl.ds(at, 256), :])
        prompt = dot(hot, buf[...])
        for t in range(2):
            num = num_ref[e, t * 256 : (t + 1) * 256, :] + prompt[:, t * 256 : (t + 1) * 256]
            one, two = split(num)
            den = dot(one, spread) + dot(two, spread)
            out = jnp.where(lane < 224, num / jnp.where(lane < 224, den, 1.0), 0.0)
            out = out.astype(BF)
            for part in range(2):
                out_ref[half * 2 + part, t * 128 : (t + 1) * 128, :] = out[part * 128 : (part + 1) * 128]


def out_kernel(pos_ref, own_ref, oth_ref, *refs):
    parts, first_ref, second_ref = refs[:8], refs[8], refs[9]
    y, core, col = pos_ref[0], pos_ref[1], pos_ref[3]
    acc = [None, None]
    for shift in range(4):
        j = lax.rem(y + 4 - shift, 4)
        for which, ref in enumerate((own_ref, oth_ref)):
            k = core if which == 0 else 1 - core
            heads = ref[j, :, 0:224]
            for e in range(2):
                at = jnp.bitwise_xor(k, lax.rem(col, 2))
                part = dot(heads, parts[2 * shift + e][at])
                acc[e] = part if acc[e] is None else acc[e] + part
    same = lax.rem(y, 2) == lax.div(col, 2)
    first_ref[...] = jnp.where(same, acc[0], acc[1]).astype(BF)
    second_ref[...] = jnp.where(same, acc[1], acc[0]).astype(BF)


def body(tokens, w_query, w_key, w_value, w_out, cached_state, cached_norm, slot_prompt, prompt_of, tail_keys, tail_values, tail_length):
    y, core, col = lax.axis_index("y"), lax.axis_index("core"), lax.axis_index("col")
    me = lax.axis_index(("req", "col"))
    pos = jnp.stack([y, core, me, col]).astype(jnp.int32)
    def over_y(x, step):
        return lax.ppermute(x, "y", [(i, (i + step) % 4) for i in range(4)])

    top, low = tokens[:128].reshape(128, 896), tokens[128:].reshape(128, 896)
    top_1, low_3 = over_y(top, 1), over_y(low, 3)
    low_1, top_3 = over_y(low, 1), over_y(top, 3)
    blocks = [top, low, top_1, low_1, over_y(top_1, 1), over_y(low_3, 3), top_3, low_3]
    value_w = jnp.moveaxis(w_value.reshape(2, 448, 112), 0, 1).reshape(448, 224)
    mine = jnp.concatenate([value_w, w_query, w_key], axis=1)
    theirs = lax.ppermute(mine, "core", [(0, 1), (1, 0)])
    owner = slot_prompt // 32
    slots = jnp.arange(32, dtype=jnp.int32)
    away = owner != me
    code = jnp.max(
        jnp.where((owner[None, :] == slots[:, None]) & away[None, :], (slots * 32 + slot_prompt % 32 + 1)[None, :], 0), axis=1
    )
    told = lax.all_to_all(code[:, None], ("req", "col"), split_axis=0, concat_axis=0, tiled=True)[:, 0]
    here = (slot_prompt[None, :] == (me * 32 + slots)[:, None])
    there = (told[None, :] > 0) & ((told[None, :] - 1) % 32 == slots[:, None])
    at_slot = jnp.max(jnp.where(here, slots[None, :], 0), axis=1)
    at_holder = jnp.where(jnp.any(here, axis=1), me, jnp.max(jnp.where(there, slots[None, :], 0), axis=1)).astype(jnp.int32)
    index = jnp.arange(512)
    rank = jnp.sum(((prompt_of[None, :] == prompt_of[:, None]) & (index[None, :] < index[:, None])).astype(jnp.int32), axis=1)
    place = (prompt_of - me * 32) * 16 + rank
    norms = jnp.pad(jnp.transpose(cached_norm, (0, 2, 1)).reshape(64, 273), ((0, 0), (0, 111)))
    states = cached_state[0].reshape(273, 224, 32)

    partial = call(
        project_kernel,
        jax.ShapeDtypeStruct((4, 256, 1152), BF),
        1,
        pos,
        *blocks,
        mine,
        theirs,
        scratch=[pltpu.VMEM((448, 640), BF), pltpu.VMEM((512, 640), BF)],
        free=range(1, 11),
    )
    partial, w_out = lax.optimization_barrier((partial, w_out))
    pieces = []
    for s in range(4):
        perm = [(k * 4 + c, (c >> 1) * 4 + (s ^ (2 * (c & 1) + k))) for k in range(2) for c in range(4)]
        pieces.append(lax.ppermute(w_out, ("core", "col"), perm))
    pieces = [jnp.stack(pieces[:2]), jnp.stack(pieces[2:])]
    out_w = [over_y(x, step) for step in (1, 3) for x in pieces]
    partial = lax.all_to_all(partial, "col", split_axis=0, concat_axis=0, tiled=True)
    partial, states, norms = lax.optimization_barrier((partial, states, norms))
    states = jnp.transpose(states, (2, 0, 1))
    shape = jax.ShapeDtypeStruct((512, 288), BF)
    own, oth = call(sum_kernel, (shape, shape), 1, pos, partial, free=(1,))
    rec = lax.ppermute(oth, "core", [(0, 1), (1, 0)])

    shape = jax.ShapeDtypeStruct((32, 16, 128), BF)
    q_send, q_keep = call(
        group_kernel,
        (shape, shape),
        3,
        pos,
        at_holder,
        at_slot,
        own,
        rec,
        place.reshape(2, 1, 256),
        scratch=[pltpu.VMEM((512, 128), BF)],
        free=(3, 4),
    )
    q_rec = lax.all_to_all(q_send, ("req", "col"), split_axis=0, concat_axis=0, tiled=True)
    shape = jax.ShapeDtypeStruct((2, 512, 256), F32)
    num = call(tail_kernel, shape, 1, pos, own, rec, tail_keys, tail_values, tail_length[:, None], free=(1, 2), pin=False)
    q_rec, out_w = lax.optimization_barrier((q_rec, out_w))
    shape = jax.ShapeDtypeStruct((32, 16, 512), BF)
    whole = pl.BlockSpec((32, 16, 128), lambda i: (0, 0, 0))
    whole_out = pl.BlockSpec((32, 16, 512), lambda i: (0, 0, 0))
    r_send, r_keep = pl.pallas_call(
        slot_kernel,
        grid=(4,),
        out_shape=(pltpu.HBM(shape.shape, BF), pltpu.HBM(shape.shape, BF)),
        in_specs=[
            SM,
            SM,
            whole,
            whole,
            pl.BlockSpec((8, 273, 224), lambda i: (i, 0, 0)),
            pl.BlockSpec((16, 384), lambda i: (i, 0)),
        ],
        out_specs=(whole_out, whole_out),
        scratch_shapes=[pltpu.VMEM((128, 128), BF)],
        compiler_params=pltpu.CompilerParams(vmem_limit_bytes=VMEM_LIMIT),
    )(pos, owner, in_hbm(q_rec), in_hbm(q_keep), in_hbm(states), in_hbm(norms))
    r_send, near_1, near_3 = lax.optimization_barrier((r_send, out_w[0], out_w[3]))
    far_1, far_3 = over_y(near_1, 1), over_y(near_3, 3)
    r_rec = lax.all_to_all(r_send, ("req", "col"), split_axis=0, concat_axis=0, tiled=True)
    r_rec, num, far_1, far_3 = lax.optimization_barrier((r_rec, num, far_1, far_3))
    heads = call(
        combine_kernel,
        jax.ShapeDtypeStruct((4, 256, 256), BF),
        3,
        pos,
        at_holder,
        at_slot,
        num,
        r_rec,
        r_keep,
        place[:, None],
        scratch=[pltpu.VMEM((512, 512), BF)],
        free=range(3, 7),
    )
    heads = lax.all_to_all(heads, "y", split_axis=0, concat_axis=0, tiled=True)
    heads_oth = lax.ppermute(heads, "core", [(0, 1), (1, 0)])
    shape = jax.ShapeDtypeStruct((256, 448), BF)
    mixed = call(out_kernel, (shape, shape), 1, pos, heads, heads_oth, *pieces, out_w[0], out_w[1], far_1, far_3, out_w[2], out_w[3], free=range(1, 11))

    def at(y, core, col):
        return (y * 2 + core) * 4 + col

    got = []
    for s, part in enumerate(mixed):
        perm = [
            (at(j, k, b), at(b, j >> 1, 2 * k + (s ^ (j & 1)))) for b in range(4) for j in range(4) for k in range(2)
        ]
        got.append(lax.ppermute(part, ("y", "core", "col"), perm).reshape(2, 128, 448))
    odd = col % 2 == 1
    mixed = jnp.concatenate([jnp.where(odd, got[1], got[0]), jnp.where(odd, got[0], got[1])], axis=1)
    mixed = jnp.transpose(mixed, (1, 0, 2)).astype(F32)
    return (mixed + tokens.astype(F32)).astype(BF)


def solution(mesh):
    inner = Mesh(mesh.devices.reshape(8, 4, 2, 4), ("req", "y", "core", "col"))
    rows = ("y", "core")
    hold = ("req", "col")
    return jax.shard_map(
        body,
        mesh=inner,
        in_specs=(
            P(("req", "y", "core"), None, "col"),
            P("col", rows),
            P("col", rows),
            P(rows, "col"),
            P(rows, "col"),
            P(hold, None, rows),
            P(hold, None, rows),
            P(hold),
            P(hold),
            P(hold, rows),
            P(hold, rows),
            P(hold),
        ),
        out_specs=P(("req", "y", "core"), None, "col"),
        check_vma=False,
    )
```
